32 devices in a mesh: dp: 8 (over z, y), tensor: 4 (over x, core).
Axes of the slice: x: 2, y: 2, z: 4, core: 2. Of those that a mesh axis runs over, the one named last changes fastest.
Arguments:
- tokens: bfloat16 [32, 1024, 768], P('dp', 'tensor'), may hold values from -6 to 6
- segments: int32 [32, 1024], P('dp'), may hold values from 0 to 17, as said below
- qkv_weight: bfloat16 [3, 768, 768], P(None, 'dp', 'tensor'), may hold values from -0.3125 to 0.3125
- out_weight: bfloat16 [768, 768], P('tensor', 'dp'), may hold values from -0.625 to 0.625
- in_weight: bfloat16 [768, 3072], P('dp', 'tensor'), may hold values from -0.21875 to 0.21875
- down_weight: bfloat16 [3072, 768], P('tensor', 'dp'), may hold values from -0.15625 to 0.15625
- vectors: float32 [12, 768], P(None, ('dp', 'tensor')), may hold values from -0.9 to 1.75
- cotangent: bfloat16 [32, 1024, 768], P('dp', 'tensor'), may hold values from -6 to 6
Outputs:
- output: bfloat16 [32, 1024, 768], P('dp', 'tensor')
- grad_tokens: bfloat16 [32, 1024, 768], P('dp', 'tensor')
- query_key_value_gradient: float32 [3, 768, 768], P(None, 'dp', 'tensor')
- out_weight_gradient: float32 [768, 768], P('tensor', 'dp')
- in_weight_gradient: float32 [768, 3072], P('dp', 'tensor')
- down_weight_gradient: float32 [3072, 768], P('tensor', 'dp')
- grad_vectors: float32 [12, 768], P(None, ('dp', 'tensor'))
The draws below stay inside these ranges and needn't reach their ends.
Inputs may be any that keep to these rules, and one draw needn't show every extreme that they name: `segments`: within each sequence the numbers start at 0 and rise by one where a document begins; documents have 60 to 800 tokens, except the last of a sequence, which the sequence's end may cut.
All inputs are finite; a program needn't handle non-finite values.
Results may differ from the reference program's by a relative error of at most 0.022.
Values may be sent and summed in bfloat16 or wider, within the bound.
A program may use at most 256 MiB of HBM per device.

```python
import jax
import jax.numpy as jnp
from jax import lax

D = 768
H = 12
HD = 64
FF = 3072
SEQ = 1024
SEQS_DEV = 4
QBLK = 512
DOC_MIN = 60
DOC_MAX = 800
HGROUPS = 4
NSEQ = 32
N_DP = 8


def draw_segments(key, part):
    doc_slots = SEQ // DOC_MIN + 1
    lengths = jax.random.randint(key, (NSEQ, doc_slots), DOC_MIN, DOC_MAX + 1)
    packed_row = jax.random.randint(jax.random.fold_in(key, 7), (), 0, NSEQ)
    row_ids = jnp.arange(NSEQ, dtype=jnp.int32)
    lengths = jnp.where((row_ids == packed_row)[:, None], DOC_MIN, lengths)
    doc_ends = jnp.cumsum(lengths, axis=1)
    places = jnp.arange(SEQ, dtype=jnp.int32)
    passed = (places[None, :, None] >= doc_ends[:, None, :]).astype(jnp.int32)
    return jnp.sum(passed, axis=2).astype(jnp.int32)


def draw_vectors(key, part):
    row_count = 8 + FF // D
    normal_draw = jnp.clip(jax.random.normal(key, (row_count, D), jnp.float32), -3.0, 3.0)
    row_ids = jnp.arange(row_count)
    gain_rows = (row_ids == 0) | (row_ids == 2)
    return jnp.where(gain_rows[:, None], 1.0 + 0.25 * normal_draw, 0.3 * normal_draw).astype(jnp.float32)


def spiked(drawn, rng, source, target, shards_of, factor):
    def block_of(position):
        return (jnp.arange(drawn.shape[position]) // (drawn.shape[position] // shards_of)).reshape((-1,) + (1,) * (drawn.ndim - 1 - position))

    first = jax.random.permutation(rng, shards_of)[block_of(target)]
    second = (block_of(target) + shards_of // 2) % shards_of
    return jnp.where((block_of(source) == first) | (block_of(source) == second), factor * drawn, drawn)


def block_levels(key, extent, split, smallest, largest):
    level, own = 1.0, jax.random.fold_in(key, 6)
    for position, parts in split:
        heights = jnp.exp(jax.random.uniform(jax.random.fold_in(own, position), (parts,), jnp.float32, smallest / len(split), largest / len(split)))
        level = level * jnp.repeat(heights, extent[position] // parts).reshape([-1 if axis == position else 1 for axis in range(len(extent))])
    return level


def scatter_about(rng, dims, scale, limit, cuts=(), held_as=jnp.bfloat16):
    level = block_levels(rng, dims, cuts, -0.22, 0.18) if cuts else 1.0
    values = jax.random.normal(rng, dims, jnp.float32) * scale * level
    return jnp.minimum(jnp.maximum(values, -limit), limit).astype(held_as)


def heavy_noise(rng, extent, scale, limit, cuts, heavy, held_as=jnp.bfloat16):
    array = scale * jax.random.normal(rng, extent, jnp.float32)
    if cuts:
        array = array * block_levels(rng, extent, cuts, -0.22, 0.18)
    return jnp.clip(spiked(array, jax.random.fold_in(rng, 3), *heavy), -limit, limit).astype(held_as)


def setup_inputs(seed: int = 0) -> dict:
    seeds = jax.random.split(jax.random.key(seed), 9)
    return {
        "tokens": scatter_about(seeds[0], (NSEQ, SEQ, D), 1.0, 6.0, ((0, 8), (1, 4))),
        "segments": draw_segments(jax.random.fold_in(seeds[8], 71), 0),
        "qkv_weight": scatter_about(seeds[2], (3, D, D), (D // 2) ** -0.5, 0.3125, ((1, 8), (2, 4))),
        "out_weight": scatter_about(seeds[3], (D, D), (D // 8) ** -0.5, 0.625, ((0, 4), (1, 8))),
        "in_weight": scatter_about(seeds[4], (D, FF), D ** -0.5, 0.21875, ((0, 8), (1, 4))),
        "down_weight": scatter_about(seeds[5], (FF, D), (FF // 2) ** -0.5, 0.15625, ((0, 4), (1, 8))),
        "vectors": draw_vectors(jax.random.fold_in(seeds[8], 71), 0),
        "cotangent": heavy_noise(seeds[7], (NSEQ, SEQ, D), 1.0, 6.0, ((0, 8), (1, 4)), (0, 2, 8, 2.0)),
    }


@jax.custom_vjp
def low(v):
    return lax.optimization_barrier(v.astype(jnp.bfloat16)).astype(jnp.float32)

@jax.custom_vjp
def low_back(v):
    return v

def low_keep(v):
    return (low(v), None)

def low_pass(kept, grad):
    return (grad,)

def back_keep(v):
    return (v, None)

def back_low(kept, grad):
    return (low(grad),)
low.defvjp(low_keep, low_pass)
low_back.defvjp(back_keep, back_low)
epsilon = 1e-05
masked_score = -1e+30
highest_precision = lax.Precision.HIGHEST

def both_ways(values):
    return low_back(low(values))

def normalize(values, gain_row, shift_row):
    average = lax.optimization_barrier(jnp.mean(values, axis=-1, keepdims=True))
    centered = values - average
    variance = lax.optimization_barrier(jnp.mean(centered * centered, axis=-1, keepdims=True))
    return centered * lax.rsqrt(variance + epsilon) * gain_row + shift_row

def attend(queries, keys, values, seg_ids):
    seq_count, length, head_count, head_dim = queries.shape
    blocks = length // QBLK
    score_scale = head_dim ** (-0.5)
    query_blocks = queries.reshape(seq_count, blocks, QBLK, head_count, head_dim).transpose(1, 0, 2, 3, 4)
    seg_blocks = seg_ids.reshape(seq_count, blocks, QBLK).transpose(1, 0, 2)

    def one_block(pieces):
        query_blk, seg_blk = pieces
        scores = jnp.einsum('sqhd,skhd->shqk', query_blk, keys, precision=highest_precision) * score_scale
        scores = low_back(scores)
        allowed = seg_blk[:, None, :, None] == seg_ids[:, None, None, :]
        scores = jnp.where(allowed, scores, masked_score)
        highest = lax.optimization_barrier(jnp.max(scores, axis=-1, keepdims=True))
        weights = jnp.exp(scores - highest)
        probabilities = low(weights / lax.optimization_barrier(jnp.sum(weights, axis=-1, keepdims=True)))
        return jnp.einsum('shqk,skhd->sqhd', probabilities, values, precision=highest_precision)
    context = lax.map(jax.checkpoint(one_block), (query_blocks, seg_blocks))
    return context.transpose(1, 0, 2, 3, 4).reshape(seq_count, length, head_count, head_dim)

def forward_group(inputs, seg_ids, qkv_weight, out_weight, in_weight, down_weight, vectors):
    seq_count = inputs.shape[0]
    head_cols = D // HGROUPS
    unit_cols = FF // HGROUPS
    inputs_low = low(inputs)
    copies = jnp.stack([low_back(inputs_low) for copy_index in range(HGROUPS)])
    qkv_split = qkv_weight.reshape(3, D, HGROUPS, head_cols)
    bias_rows = jnp.stack([vectors[6], jnp.zeros_like(vectors[6]), vectors[7]]).reshape(3, HGROUPS, head_cols)
    projected = jnp.einsum('tsld,jdtc->jstlc', copies, qkv_split, precision=highest_precision)
    projected = both_ways(projected + bias_rows[:, None, :, None, :])
    heads_form = projected.reshape(3, seq_count, HGROUPS, SEQ, head_cols // HD, HD)
    heads_form = heads_form.transpose(0, 1, 3, 2, 4, 5).reshape(3, seq_count, SEQ, H, HD)
    context = both_ways(attend(heads_form[0], heads_form[1], heads_form[2], seg_ids))
    context_split = context.reshape(seq_count, SEQ, HGROUPS, head_cols)
    out_split = out_weight.reshape(HGROUPS, head_cols, D)
    attn_parts = jnp.einsum('sltc,tcd->tsld', context_split, out_split, precision=highest_precision)
    attn_sum = low_back(lax.optimization_barrier(jnp.sum(low(attn_parts), axis=0)))
    first_sum = inputs + attn_sum + vectors[4]
    normed = normalize(first_sum, vectors[0], vectors[1])
    normed_low = low(normed)
    normed_copies = jnp.stack([low_back(normed_low) for copy_index in range(HGROUPS)])
    in_split = in_weight.reshape(D, HGROUPS, unit_cols)
    hidden_bias = vectors[8:].reshape(HGROUPS, unit_cols)
    pre_act = jnp.einsum('tsld,dtf->tslf', normed_copies, in_split, precision=highest_precision)
    pre_act = low_back(pre_act + hidden_bias[:, None, None, :])
    activated = low(jax.nn.gelu(pre_act, approximate=False))
    down_split = down_weight.reshape(HGROUPS, unit_cols, D)
    ffn_parts = jnp.einsum('tslf,tfd->tsld', activated, down_split, precision=highest_precision)
    ffn_sum = low_back(lax.optimization_barrier(jnp.sum(low(ffn_parts), axis=0)))
    second_sum = normed + ffn_sum + vectors[5]
    return normalize(second_sum, vectors[2], vectors[3])

def reference(tokens, segments, qkv_weight, out_weight, in_weight, down_weight, vectors, cotangent):
    weights = (qkv_weight.astype(jnp.float32), out_weight.astype(jnp.float32), in_weight.astype(jnp.float32), down_weight.astype(jnp.float32), vectors.astype(jnp.float32))
    token_groups = tokens.astype(jnp.float32).reshape(N_DP, SEQS_DEV, SEQ, D)
    seg_groups = segments.reshape(N_DP, SEQS_DEV, SEQ)
    cot_groups = cotangent.astype(jnp.float32).reshape(N_DP, SEQS_DEV, SEQ, D)

    def one_group(running, group_data):
        inputs, seg_ids, upstream = group_data

        def forward(inputs_now, qkv_now, out_now, in_now, down_now, vectors_now):
            return forward_group(inputs_now, seg_ids, qkv_now, out_now, in_now, down_now, vectors_now)
        result, pull_back = jax.vjp(forward, inputs, weights[0], weights[1], weights[2], weights[3], weights[4])
        gradients = pull_back(upstream)
        running = tuple((running_sum + grad_piece for running_sum, grad_piece in zip(running, gradients[1:])))
        return (running, (result.astype(jnp.bfloat16), gradients[0].astype(jnp.bfloat16)))
    start_sums = tuple((jnp.zeros_like(weight_piece) for weight_piece in weights))
    totals, (outputs, grad_tokens) = lax.scan(one_group, start_sums, (token_groups, seg_groups, cot_groups))
    return (outputs.reshape(NSEQ, SEQ, D), grad_tokens.reshape(NSEQ, SEQ, D), totals[0], totals[1], totals[2], totals[3], totals[4])
```

```python
import functools

import jax
import jax.numpy as jnp
from jax import lax
from jax.experimental import pallas as pl
from jax.experimental.pallas import tpu as pltpu
from jax.sharding import PartitionSpec as P

HD = 64
PAIR = 2 * HD
EPS = 1e-05
MASKED = -1e30
BF = jnp.bfloat16
F32 = jnp.float32
ALL = ("dp", "tensor")

NT = (((1,), (1,)), ((), ()))
NN = (((1,), (0,)), ((), ()))
TN = (((0,), (0,)), ((), ()))


def mm(a, b, dims=NN):
    return lax.dot_general(a, b, dims, preferred_element_type=F32)


def lane_split(value, head):
    lanes = lax.broadcasted_iota(jnp.int32, value.shape, 1)
    keep = (lanes < HD) if head == 0 else (lanes >= HD)
    return jnp.where(keep, value, jnp.zeros_like(value))


def attn_fwd_kernel(q_ref, k_ref, v_ref, segc_ref, segr_ref, o_ref, lse_ref):
    length = q_ref.shape[0]
    block = 256
    keys = k_ref[...]
    vals = [lane_split(v_ref[...], h) for h in range(2)]
    seg_row = segr_ref[...]

    def step(i, carry):
        rows = pl.ds(pl.multiple_of(i * block, block), block)
        same = segc_ref[rows, :] == seg_row
        q = q_ref[rows, :] * jnp.asarray(HD**-0.5, BF)
        total = jnp.zeros((block, PAIR), F32)
        scale = []
        for h in range(2):
            s = mm(lane_split(q, h), keys, NT)
            s = jnp.where(same, s, MASKED)
            top = jnp.max(s, axis=1, keepdims=True)
            w = jnp.exp(s - top)
            z = jnp.sum(w, axis=1, keepdims=True)
            inv = 1.0 / z
            total = total + mm((w * inv).astype(BF), vals[h])
            lse_ref[rows, h : h + 1] = top + jnp.log(z)
        o_ref[rows, :] = total.astype(BF)
        return carry

    lax.fori_loop(0, length // block, step, 0)


def attn_fwd(q, k, v, seg):
    length, width = q.shape
    pairs = width // PAIR
    spec = pl.BlockSpec((length, PAIR), lambda p: (0, p))
    return pl.pallas_call(
        attn_fwd_kernel,
        grid=(pairs,),
        in_specs=[
            spec,
            spec,
            spec,
            pl.BlockSpec((length, 1), lambda p: (0, 0)),
            pl.BlockSpec((1, length), lambda p: (0, 0)),
        ],
        out_specs=[spec, pl.BlockSpec((None, length, 2), lambda p: (p, 0, 0))],
        out_shape=[
            jax.ShapeDtypeStruct((length, width), BF),
            jax.ShapeDtypeStruct((pairs, length, 2), F32),
        ],
        compiler_params=pltpu.CompilerParams(vmem_limit_bytes=48 << 20),
        name="attn_fwd",
    )(q, k, v, seg.reshape(length, 1), seg.reshape(1, length))


def attn_bwd_kernel(q_ref, k_ref, v_ref, do_ref, lse_ref, delta_ref, segc_ref, segr_ref, dq_ref, dk_ref, dv_ref, acc_ref):
    length = q_ref.shape[0]
    block = 256
    scale = HD**-0.5
    q = q_ref[...] * jnp.asarray(scale, BF)
    do = do_ref[...]
    qs = [lane_split(q, h) for h in range(2)]
    dos = [lane_split(do, h) for h in range(2)]
    seg_row = segr_ref[...]
    acc_ref[...] = jnp.zeros_like(acc_ref)

    def step(i, carry):
        rows = pl.ds(pl.multiple_of(i * block, block), block)
        same = segc_ref[rows, :] == seg_row
        kb = k_ref[rows, :]
        vb = v_ref[rows, :]
        dk = jnp.zeros((block, PAIR), F32)
        dv = jnp.zeros((block, PAIR), F32)
        for h in range(2):
            s = mm(kb, qs[h], NT)
            s = jnp.where(same, s, MASKED)
            p = jnp.exp(s - lse_ref[h : h + 1, :])
            dv = dv + mm(p.astype(BF), dos[h])
            dp = mm(vb, dos[h], NT)
            ds = (p * (dp - delta_ref[h : h + 1, :])).astype(BF)
            dk = dk + mm(ds, qs[h])
            acc_ref[...] += mm(lane_split(kb, h), ds, TN)
        dk_ref[rows, :] = dk.astype(BF)
        dv_ref[rows, :] = dv.astype(BF)
        return carry

    lax.fori_loop(0, length // block, step, 0)
    dq_ref[...] = (acc_ref[...].T * scale).astype(BF)


def attn_bwd(q, k, v, do, lse, delta, seg):
    length, width = q.shape
    pairs = width // PAIR
    spec = pl.BlockSpec((length, PAIR), lambda p: (0, p))
    row = pl.BlockSpec((None, 2, length), lambda p: (p, 0, 0))
    out = jax.ShapeDtypeStruct((length, width), BF)
    return pl.pallas_call(
        attn_bwd_kernel,
        grid=(pairs,),
        in_specs=[
            spec,
            spec,
            spec,
            spec,
            row,
            row,
            pl.BlockSpec((length, 1), lambda p: (0, 0)),
            pl.BlockSpec((1, length), lambda p: (0, 0)),
        ],
        out_specs=[spec, spec, spec],
        out_shape=[out, out, out],
        scratch_shapes=[pltpu.VMEM((PAIR, length), F32)],
        compiler_params=pltpu.CompilerParams(vmem_limit_bytes=48 << 20),
        name="attn_bwd",
    )(q, k, v, do, lse, delta, seg.reshape(length, 1), seg.reshape(1, length))


def normalize(values, gain_row, shift_row):
    average = jnp.mean(values, axis=-1, keepdims=True)
    centered = values - average
    variance = jnp.mean(centered * centered, axis=-1, keepdims=True)
    inverse = lax.rsqrt(variance + EPS)
    unit_rows = centered * inverse
    return unit_rows * gain_row + shift_row, unit_rows, inverse


def normalize_back(upstream, unit_rows, inverse, gain_row):
    d_unit = upstream * gain_row
    first = jnp.mean(d_unit, axis=-1, keepdims=True)
    second = jnp.mean(d_unit * unit_rows, axis=-1, keepdims=True)
    return (
        inverse * (d_unit - first - unit_rows * second),
        jnp.sum(upstream * unit_rows, axis=0),
        jnp.sum(upstream, axis=0),
    )


def local(tokens, segments, qkv_weight, out_weight, in_weight, down_weight, vectors, cotangent):
    n_dp, n_t = lax.axis_size("dp"), lax.axis_size("tensor")
    rank = lax.axis_index("tensor")
    seqs, rows, width = tokens.shape
    length = rows * n_t
    per = seqs // n_t
    assert per == 1
    hc = qkv_weight.shape[2]
    depth = qkv_weight.shape[1]
    uc = in_weight.shape[1]
    n_v = vectors.shape[0]

    def to_seq(v):
        return lax.all_to_all(v, "tensor", split_axis=0, concat_axis=1, tiled=True)[0]

    def to_rows(v):
        return lax.all_to_all(v[None], "tensor", split_axis=1, concat_axis=0, tiled=True)

    x = to_seq(tokens)
    cot = to_seq(cotangent)
    seg = lax.dynamic_slice_in_dim(segments, rank, 1, 0)[0]
    vec = lax.all_gather(vectors, ALL, axis=1, tiled=True)

    a_shard = jnp.concatenate([qkv_weight[0], qkv_weight[1], qkv_weight[2], out_weight.T], axis=1)
    shard = jnp.stack([a_shard, in_weight, down_weight.T])
    full = lax.all_gather(shard, ALL, axis=0, tiled=False)
    full = full.reshape(n_dp, n_t, 3, depth, uc).transpose(2, 0, 3, 1, 4).reshape(3, width, n_t, uc)
    attn_w = full[0].reshape(width, n_t, 4, hc).transpose(2, 0, 1, 3).reshape(4, width, n_t * hc)
    in_w = full[1].reshape(width, n_t * uc)
    down_t = full[2].reshape(width, n_t * uc)
    out_t = attn_w[3]

    q = (mm(x, attn_w[0]) + vec[6]).astype(BF)
    k = mm(x, attn_w[1]).astype(BF)
    v = (mm(x, attn_w[2]) + vec[7]).astype(BF)
    ctx, lse = attn_fwd(q, k, v, seg)
    lse = lse.transpose(0, 2, 1)
    h1 = x.astype(F32) + mm(ctx, out_t, NT) + vec[4]
    y1, u1, r1 = normalize(h1, vec[0], vec[1])
    y1_low = y1.astype(BF)
    pre = mm(y1_low, in_w) + vec[8:].reshape(-1)
    act, pull = jax.vjp(lambda t: jax.nn.gelu(t, approximate=False), pre)
    act = act.astype(BF)
    h2 = y1 + mm(act, down_t, NT) + vec[5]
    output, u2, r2 = normalize(h2, vec[2], vec[3])
    out_rows = to_rows(output.astype(BF))

    up = cot.astype(F32)
    g_h2, d_gain2, d_shift2 = normalize_back(up, u2, r2, vec[2])
    d_down_bias = jnp.sum(g_h2, axis=0)
    g2 = g_h2.astype(BF)
    d_down_t = mm(g2, act, TN).astype(BF)
    d_pre = pull(mm(g2, down_t))[0].astype(BF)
    d_hidden = jnp.sum(d_pre, axis=0, dtype=F32)
    d_in = mm(y1_low, d_pre, TN).astype(BF)
    g_y1 = g_h2 + mm(d_pre, in_w, NT)
    g_h1, d_gain1, d_shift1 = normalize_back(g_y1, u1, r1, vec[0])
    d_out_bias = jnp.sum(g_h1, axis=0)
    g1 = g_h1.astype(BF)
    d_out_t = mm(g1, ctx, TN).astype(BF)
    d_ctx = mm(g1, out_t).astype(BF)
    delta = jnp.sum((d_ctx.astype(F32) * ctx.astype(F32)).reshape(length, width // PAIR, 2, HD), axis=-1)
    dq, dk, dv = attn_bwd(q, k, v, d_ctx, lse, delta.transpose(1, 2, 0), seg)
    d_attn = [mm(x, g, TN).astype(BF) for g in (dq, dk, dv)] + [d_out_t]
    g_x = g_h1 + mm(dq, attn_w[0], NT) + mm(dk, attn_w[1], NT) + mm(dv, attn_w[2], NT)
    g_rows = to_rows(g_x.astype(BF))

    d_attn = jnp.stack(d_attn).reshape(4, width, n_t, hc).transpose(1, 2, 0, 3).reshape(width, n_t * uc)
    grads = jnp.stack([d_attn, d_in, d_down_t]).reshape(3, n_dp, depth, n_t, uc).transpose(1, 3, 0, 2, 4)
    mine = lax.psum_scatter(grads.reshape(n_dp * n_t, 3, depth, uc), ALL, scatter_dimension=0, tiled=True)[0]
    mine = mine.astype(F32)
    small = jnp.concatenate(
        [
            jnp.stack(
                [
                    d_gain1,
                    d_shift1,
                    d_gain2,
                    d_shift2,
                    d_out_bias,
                    d_down_bias,
                    jnp.sum(dq, axis=0, dtype=F32),
                    jnp.sum(dv, axis=0, dtype=F32),
                ]
            ),
            d_hidden.reshape(-1, width),
        ],
        axis=0,
    )
    g_vec = lax.psum_scatter(small, ALL, scatter_dimension=1, tiled=True)
    d_a = mine[0].reshape(depth, 4, hc).transpose(1, 0, 2)
    return out_rows, g_rows, d_a[:3], d_a[3].T, mine[1], mine[2].T, g_vec


def solution(mesh):
    in_specs = (
        P("dp", "tensor", None),
        P("dp", None),
        P(None, "dp", "tensor"),
        P("tensor", "dp"),
        P("dp", "tensor"),
        P("tensor", "dp"),
        P(None, ("dp", "tensor")),
        P("dp", "tensor", None),
    )
    out_specs = (
        P("dp", "tensor", None),
        P("dp", "tensor", None),
        P(None, "dp", "tensor"),
        P("tensor", "dp"),
        P("dp", "tensor"),
        P("tensor", "dp"),
        P(None, ("dp", "tensor")),
    )
    return jax.shard_map(local, mesh=mesh, in_specs=in_specs, out_specs=out_specs, check_vma=False)
```

```python
import functools

import jax
import jax.numpy as jnp
from jax import lax
from jax.experimental import pallas as pl
from jax.experimental.pallas import tpu as pltpu
from jax.sharding import PartitionSpec as P

HD = 64
LANES = 128
EPS = 1e-05
MASKED = -1e30
SEGS = 32
TOP = 35
LOG2E = 1.4426950408889634
QSCALE = LOG2E * HD**-0.5
BF = jnp.bfloat16
F32 = jnp.float32
ALL = ("dp", "tensor")
MESH = pl.DeviceIdType.MESH
ANY = pl.BlockSpec(memory_space=pl.ANY)
VMEM = pl.BlockSpec(memory_space=pltpu.VMEM)
NT = (((1,), (1,)), ((), ()))
NN = (((1,), (0,)), ((), ()))
TN = (((0,), (0,)), ((), ()))
SLOTS = ((0, (0, 1)), (1, (2,)))


def mm(a, b, dims=NN):
    return lax.dot_general(a, b, dims, preferred_element_type=F32)


def lane_ids(shape):
    return lax.broadcasted_iota(jnp.int32, shape, 1)


def low_half(shape):
    return lane_ids(shape) < HD


def swap_halves(value):
    return pltpu.roll(value, HD, 1)


def tile(ref, t, i, rows=slice(None)):
    return ref[t, rows, i * LANES : (i + 1) * LANES]


def flat(value):
    return value.reshape(-1, value.shape[-1])


def at_tick(step, ticks):
    for when, work in ticks:
        pl.when(step == when)(functools.partial(work))


def group_biases(vt):
    length = vt.shape[0]
    groups = length // (3 * HD)
    lanes = lane_ids((length, LANES))
    q, v = vt[:, 6:7], vt[:, 7:8]
    zero = jnp.zeros((LANES, 1), F32)
    out = jnp.zeros((length, LANES), F32)
    for t in range(groups):
        a, b, c = 3 * HD * t, 3 * HD * t + LANES, 3 * HD * (t + 1)
        column = jnp.concatenate([q[a:b], zero, v[a:b], q[b:c], zero[:HD], zero, v[b:c], zero[:HD]], axis=0)
        out = jnp.where(lanes == t, column, out)
    return out.T


def fwd_setup(vt_v, seg, vec_rows, bias_v, oh_v, km_v):
    vt = flat(vt_v[...])
    vec_rows[...] = vt.T[: vec_rows.shape[0]]
    biases = group_biases(vt)
    for t in range(bias_v.shape[0]):
        bias_v[t] = biases[t : t + 1]
    place = lane_ids(oh_v.shape) % HD
    same = seg[...] == place
    oh_v[...] = jnp.where(same, 1.0, 0.0).astype(BF)
    km_v[...] = key_marks(seg, km_v.shape)


def key_marks(seg, shape):
    place = lane_ids(shape) % HD
    marks = jnp.where(place < SEGS, jnp.where(seg[...] == place, 0.0, MASKED), 1.0)
    return jnp.where(place < TOP, marks, 0.0).astype(BF)


def fwd_group(t, x_v, a_v, bias_v, km_v, qkv_v, ka_v, va_v):
    x = flat(x_v[...])
    w = flat(a_v[...])
    low = low_half((x.shape[0], LANES))
    for i in range(6):
        cols = slice(i * LANES, (i + 1) * LANES)
        out = mm(x, w[:, cols]) + bias_v[t, :, cols]
        if i % 3 == 0:
            out = out * QSCALE
        out = out.astype(BF)
        qkv_v[t, :, cols] = out
        one = jnp.ones_like(out)
        if i == 1:
            ka_v[0] = jnp.where(low, out, km_v[...])
            ka_v[1] = jnp.where(low, km_v[...], out)
        if i == 2:
            va_v[0] = jnp.where(low, out, one)
            va_v[1] = jnp.where(low, one, out)
        if i == 4:
            ka_v[2] = jnp.where(low, out, km_v[...])
        if i == 5:
            va_v[2] = jnp.where(low, out, one)


def fwd_block(t, rows, block, qkv_v, ka_v, va_v, oh_v, ctx_v, lse_ref):
    shape = (block, LANES)
    low = low_half(shape)
    lanes = lane_ids(shape)
    marks = oh_v[rows, :]
    lse = lse_ref[rows, :]
    parts = []
    for h in range(3):
        q = tile(qkv_v, t, 0 if h < 2 else 3, rows)
        q = jnp.where(low, marks, q) if h == 1 else jnp.where(low, q, marks)
        s = mm(q, ka_v[h], NT)
        top = jnp.max(s, axis=1, keepdims=True)
        w = jnp.exp2(s - top).astype(BF)
        o = mm(w, va_v[h])
        total = o[:, HD : HD + 1] if h != 1 else o[:, 0:1]
        lse = jnp.where(lanes == 3 * t + h, top + jnp.log2(total), lse)
        parts.append(o)
    lse_ref[rows, :] = lse
    sums = swap_halves(jnp.where(low, parts[1], parts[0]))
    pair = jnp.where(low, parts[0], parts[1]) / sums
    last = parts[2] / swap_halves(parts[2])
    zero = jnp.zeros(shape, F32)
    tiles = (pair, swap_halves(pair), swap_halves(last))
    for i, value in enumerate(tiles):
        ctx_v[t, rows, i * LANES : (i + 1) * LANES] = jnp.where(low, zero, value).astype(BF)


def spread(base, value, lanes):
    hi = value.astype(BF).astype(F32)
    rest = value - hi
    mid = rest.astype(BF).astype(F32)
    low = rest - mid
    place = lanes % HD
    out = jnp.where(place == SEGS, hi, jnp.where(place == SEGS + 1, mid, jnp.where(place == SEGS + 2, low, 0.0)))
    return jnp.where(place < SEGS, base, out.astype(BF))


def bwd_group(t, qkv, ctx, dctx, lse, oh_v, km_v, qa_v, ka_v, va_v, da_v, kt_v, dqt_v):
    length = oh_v.shape[0]
    shape = (length, LANES)
    low = low_half(shape)
    lanes = lane_ids(shape)
    oh, km = oh_v[...], km_v[...]
    ones = jnp.where((lanes % HD >= SEGS) & (lanes % HD < TOP), 1.0, 0.0).astype(BF)

    def cols(ref, i):
        return ref[:, i * LANES : (i + 1) * LANES]

    q, k, v = cols(qkv, 0), cols(qkv, 1), cols(qkv, 2)
    q2, k2, v2 = cols(qkv, 3), cols(qkv, 4), cols(qkv, 5)
    c_pair = jnp.where(low, swap_halves(cols(ctx, 1)), cols(ctx, 0))
    d_pair = jnp.where(low, swap_halves(cols(dctx, 1)), cols(dctx, 0))
    c_last = swap_halves(cols(ctx, 2))
    d_last = swap_halves(cols(dctx, 2))
    prod = c_pair.astype(F32) * d_pair.astype(F32)
    prod2 = c_last.astype(F32) * d_last.astype(F32)
    lse_all = lse[...]
    zero = jnp.zeros_like(prod)
    for h in range(3):
        mine = low if h != 1 else jnp.logical_not(low)
        delta = jnp.sum(jnp.where(mine, prod2 if h == 2 else prod, zero), axis=1, keepdims=True)
        top = jnp.sum(jnp.where(lanes == 3 * t + h, lse_all, zero), axis=1, keepdims=True)
        qa_v[h] = jnp.where(mine, q2 if h == 2 else q, spread(oh, -top, lanes))
        da_v[h] = jnp.where(mine, d_last if h == 2 else d_pair, spread(jnp.zeros_like(oh), -delta, lanes))
        ka_v[h] = jnp.where(mine, k2 if h == 2 else k, km)
        va_v[h] = jnp.where(mine, v2 if h == 2 else v, ones)
    kt_v[0] = k.T
    kt_v[1] = k2.T
    dqt_v[...] = jnp.zeros_like(dqt_v)


def bwd_block(rows, block, qa_v, ka_v, va_v, da_v, kt_v, dqt_v, out):
    low = low_half((block, LANES))
    dk, dv = [], []
    for h in range(3):
        s = mm(ka_v[h, rows, :], qa_v[h], NT)
        p = jnp.exp2(s)
        dv.append(mm(p.astype(BF), da_v[h]))
        dp = mm(va_v[h, rows, :], da_v[h], NT)
        ds = (p * dp).astype(BF)
        dk.append(mm(ds, qa_v[h]) * (1.0 / LOG2E))
        slot, half = h // 2, slice((h % 2) * HD, (h % 2 + 1) * HD)
        dqt_v[slot, half, :] += mm(kt_v[slot, half, rows], ds)
    zero = jnp.zeros((block, LANES), F32)
    tiles = {
        1: jnp.where(low, dk[0], dk[1]),
        2: jnp.where(low, dv[0], dv[1]),
        4: jnp.where(low, dk[2], zero),
        5: jnp.where(low, dv[2], zero),
    }
    for i, value in tiles.items():
        out[rows, i * LANES : (i + 1) * LANES] = value.astype(BF)


def bwd_finish(dqt_v, out):
    scale = HD**-0.5
    low = low_half((out.shape[0], LANES))
    out[:, 0:LANES] = (dqt_v[0].T * scale).astype(BF)
    last = dqt_v[1].T * scale
    out[:, 3 * LANES : 4 * LANES] = jnp.where(low, last, jnp.zeros_like(last)).astype(BF)


def normalize(values, gain_row, shift_row):
    average = jnp.mean(values, axis=-1, keepdims=True)
    centered = values - average
    variance = jnp.mean(centered * centered, axis=-1, keepdims=True)
    inverse = lax.rsqrt(variance + EPS)
    unit = centered * inverse
    return unit * gain_row + shift_row, unit, inverse


def normalize_back(upstream, unit, inverse, gain_row):
    d_unit = upstream * gain_row
    first = jnp.mean(d_unit, axis=-1, keepdims=True)
    second = jnp.mean(d_unit * unit, axis=-1, keepdims=True)
    return inverse * (d_unit - first - unit * second)


def eighths(value):
    return jnp.sum(value.reshape(-1, 8, value.shape[-1]), axis=0)


def gelu_both(x):
    a = jnp.abs(x)
    tail = jnp.exp2(x * x * (-0.5 * LOG2E))
    t = 1.0 / (1.0 + (0.3275911 * 0.5**0.5) * a)
    poly = ((((1.061405429 * t - 1.453152027) * t + 1.421413741) * t - 0.284496736) * t + 0.254829592) * t
    rest = 0.5 * poly * tail
    cdf = jnp.where(x < 0, rest, 1.0 - rest)
    return x * cdf, cdf + x * tail * 0.3989422804014327


def mid_rows(i, block, refs):
    (x_v, cot_v, ctx_v, ao_v, in_v, dn_v, vec, act_v, dact_v, dpre_v, y1_v, g2_v, out_v, gh1_v, dctx_v, sums_v) = refs
    rows = pl.ds(pl.multiple_of(i * block, block), block)
    groups = in_v.shape[0]

    def row(k):
        return vec[k : k + 1, :]

    def note(k, value):
        sums_v[k] += eighths(value)

    attn = mm(ctx_v[0, rows, :], ao_v[0], NT)
    for t in range(1, groups):
        attn = attn + mm(ctx_v[t, rows, :], ao_v[t], NT)
    h1 = x_v[i].astype(F32) + attn + row(4)
    y1, u1, r1 = normalize(h1, row(0), row(1))
    y1_low = y1.astype(BF)
    y1_v[rows, :] = y1_low
    ffn = row(5) + y1
    for t in range(groups):
        pre = mm(y1_low, in_v[t]) + row(8 + t)
        act, slope = gelu_both(pre)
        act = act.astype(BF)
        act_v[t, rows, :] = act
        dact_v[t] = slope.astype(BF)
        ffn = ffn + mm(act, dn_v[t], NT)
    out, u2, r2 = normalize(ffn, row(2), row(3))
    out_v[i] = out.astype(BF)
    up = cot_v[i].astype(F32)
    g_h2 = normalize_back(up, u2, r2, row(2))
    note(2, up * u2)
    note(3, up)
    note(5, g_h2)
    g2 = g_h2.astype(BF)
    g2_v[rows, :] = g2
    g_y1 = g_h2
    for t in range(groups):
        dpre = (mm(g2, dn_v[t]) * dact_v[t].astype(F32)).astype(BF)
        dpre_v[t, rows, :] = dpre
        note(8 + t, dpre.astype(F32))
        g_y1 = g_y1 + mm(dpre, in_v[t], NT)
    note(0, g_y1 * u1)
    note(1, g_y1)
    g_h1 = normalize_back(g_y1, u1, r1, row(0))
    note(4, g_h1)
    gh1_v[i] = g_h1
    g1 = g_h1.astype(BF)
    for t in range(groups):
        dctx_v[t, rows, :] = mm(g1, ao_v[t]).astype(BF)

STEP = {"z2": 4, "z1": 2, "y": 1, "x": 2, "c": 1}
BLOCKS = ("x", "c", "z2", "z1", "y")
FEATURES = ("z2", "z1", "y", "x", "c")
P_Y = ("z2", "z1", "x", "y")
P_Z = ("z2", "x", "y", "z1")
P_X = ("z2", "y", "z1", "x")


class Place:
    def __init__(self):
        self.d = lax.axis_index("dp")
        self.t = lax.axis_index("tensor")
        self.bit = {
            "x": self.t // 2,
            "c": self.t % 2,
            "z2": self.d // 4,
            "z1": (self.d // 2) % 2,
            "y": self.d % 2,
        }

    def flip(self, dim):
        return 1 - self.bit[dim]

    def peer(self, dim):
        move = STEP[dim] * (1 - 2 * self.bit[dim])
        if dim in ("x", "c"):
            return (self.d, self.t + move)
        return (self.d + move, self.t)

    def row_peer(self, k):
        t = self.t
        if k in (1, 3):
            t = t + (1 - 2 * self.bit["c"])
        if k in (2, 3):
            t = t + 2 * (1 - 2 * self.bit["x"])
        return t

    def index(self, dims, **chosen):
        return tuple(chosen.get(dim, self.bit[dim]) for dim in dims)


def enter(place):
    bar = pltpu.get_barrier_semaphore()
    peers = [place.peer(dim) for dim in BLOCKS] + [(place.d, place.row_peer(3))]
    for peer in peers:
        pl.semaphore_signal(bar, inc=1, device_id=peer, device_id_type=MESH)
    pl.semaphore_wait(bar, len(peers))


class Copies:
    def __init__(self, send, recv, local):
        self.send, self.recv, self.local = send, recv, local
        self.count = self.locals = 0

    def remote(self, ends):
        i = self.count
        self.count += 1

        def copy():
            src, dst, peer = ends()
            return pltpu.make_async_remote_copy(
                src_ref=src,
                dst_ref=dst,
                send_sem=self.send.at[i],
                recv_sem=self.recv.at[i],
                device_id=peer,
                device_id_type=MESH,
            )

        copy().start()
        return lambda: copy().wait()

    def here(self, ends):
        i = self.locals
        self.locals += 1

        def copy():
            src, dst = ends()
            return pltpu.make_async_copy(src, dst, self.local.at[i])

        copy().start()
        return lambda: copy().wait()


ALLBITS = slice(None)


class GatherPart:
    def __init__(self, place, copies, own, full, order, rows, dims=BLOCKS):
        self.place, self.copies, self.own, self.full, self.order = place, copies, own, full, order
        self.rows, self.dims = rows, dims
        self.stage = 0
        self.side = []

    def at(self, **chosen):
        return self.full.at[self.place.index(self.dims, **chosen) + (self.rows,)]

    def begin(self):
        p, c = self.place, self.copies
        self.current = c.remote(lambda: (self.own.at[self.rows], self.at(), p.peer(self.order[0])))
        self.side.append(c.remote(lambda: (self.own.at[self.rows], self.at(), p.peer("c"))))
        self.keep = c.here(lambda: (self.own.at[self.rows], self.at()))

    def held(self, s):
        return self.at(**{dim: ALLBITS for dim in self.order[:s]})

    def arrived(self, s):
        dim = self.order[s]
        return self.at(**{other: ALLBITS for other in self.order[:s]}, **{dim: self.place.flip(dim)})

    def advance(self):
        p, c, s = self.place, self.copies, self.stage
        self.current()
        if s == 0:
            self.keep()
        if s + 1 < len(self.order):
            self.current = c.remote(lambda: (self.held(s + 1), self.held(s + 1), p.peer(self.order[s + 1])))
        self.side.append(c.remote(lambda: (self.arrived(s), self.arrived(s), p.peer("c"))))
        self.stage = s + 1

    def finish(self):
        wait_all(self.side)


def every(count, work):
    if count == 0:
        work(())
        return

    def body(i, carry):
        work(tuple((i // 2**j) % 2 for j in reversed(range(count))))
        return carry

    lax.fori_loop(0, 2**count, body, 0)


def blockwise(ref):
    return ref.reshape(2 ** (len(ref.shape) - 2), *ref.shape[-2:])


def spot(bits):
    place = 0
    for bit in bits:
        place = 2 * place + bit
    return place


class ReducePart:
    def __init__(self, place, copies, src, total, arrive, out, order, rows, dims=BLOCKS):
        self.place, self.copies, self.src, self.total, self.arrive = place, copies, src, total, arrive
        self.out, self.order, self.rows, self.dims = out, order, rows, dims
        self.inner = tuple(dim for dim in dims if dim != "c")
        self.kept = self.inner
        if total is None:
            self.total, self.kept = src, dims
        self.stage = 0

    def source(self, **chosen):
        return self.src.at[self.place.index(self.dims, **chosen) + (self.rows,)]

    def sums(self, **chosen):
        return self.total.at[self.place.index(self.kept, **chosen) + (self.rows,)]

    def half(self, bit):
        p, first = self.place, self.order[0]

        def ends():
            free = {dim: ALLBITS for dim in self.inner}
            free[first] = bit()
            dst = self.arrive[0].at[p.index(self.inner, **free) + (self.rows,)]
            return self.source(c=p.flip("c"), **free), dst, p.peer("c")

        return self.copies.remote(ends)

    def begin(self):
        p, first = self.place, self.order[0]
        self.side = [self.half(lambda: p.flip(first)), self.half(lambda: p.bit[first])]
        if self.kept is self.inner:
            free = {dim: ALLBITS for dim in self.inner}
            self.keep = self.copies.here(lambda: (self.source(**free), self.sums(**free)))

    def add(self, fixed, bit):
        s = self.stage
        left = [dim for dim in self.inner if dim not in self.order[:s]] if s else list(self.inner)
        loose = [dim for dim in left if dim != fixed]

        total, arrive = blockwise(self.total), blockwise(self.arrive[s])

        def work(bits):
            chosen = dict(zip(loose, bits))
            chosen[fixed] = bit
            mine = spot(self.place.index(self.kept, **chosen))
            there = spot(tuple(chosen[dim] for dim in left))
            both = total[mine, self.rows, :].astype(F32) + arrive[there, self.rows, :].astype(F32)
            total[mine, self.rows, :] = both.astype(total.dtype)

        every(len(loose), work)

    def send(self):
        p, s = self.place, self.stage
        dim = self.order[s]
        free = {other: ALLBITS for other in self.order[s + 1 :]}

        def ends():
            src = self.sums(**free, **{dim: p.flip(dim)})
            dst = self.arrive[s + 1].at[(ALLBITS,) * len(free) + (self.rows,)]
            return src, dst, p.peer(dim)

        return self.copies.remote(ends)

    def advance(self):
        p, s = self.place, self.stage
        if s == 0:
            if self.kept is self.inner:
                self.keep()
            self.side[0]()
        else:
            self.current()
        if s < len(self.order):
            dim = self.order[s]
            self.add(dim, p.flip(dim))
            self.current = self.send()
            if s == 0:
                self.side[1]()
            self.add(dim, p.bit[dim])
        else:
            mine = spot(self.place.index(self.kept))
            self.out[self.rows, :] = blockwise(self.total)[mine, self.rows, :].astype(F32) + self.arrive[s][self.rows, :].astype(F32)
        self.stage = s + 1


def arrivals(rows, cols, dtype):
    return [pltpu.VMEM((2,) * n + (rows, cols), dtype) for n in (4, 3, 2, 1, 0)]


def start_row(place, copies, src, dst, k):
    def ends():
        to = place.row_peer(k)
        return src.at[to], dst.at[place.t], (place.d, to)

    return copies.remote(ends)


def keep_row(place, copies, src, dst):
    return copies.here(lambda: (src.at[place.t], dst.at[place.t]))


def start_rows(place, copies, src, dst):
    return [start_row(place, copies, src, dst, k) for k in (2, 3, 1)] + [keep_row(place, copies, src, dst)]


def wait_all(waits):
    for wait in waits:
        wait()


def params(collective=None):
    more = {} if collective is None else {"collective_id": collective, "has_side_effects": True}
    return pltpu.CompilerParams(vmem_limit_bytes=60 << 20, **more)


def sems(count):
    return [pltpu.SemaphoreType.DMA((count,))] * 2


def fwd_core(group_ref, x_v, vt_v, seg, qkv, ctx, lse, vec_rows, s, ticks):
    (a_v, bias_v, oh_v, km_v, qkv_v, ka_v, va_v, ctx_v, a_sem, out_sem) = s
    groups, length = qkv.shape[:2]
    block = 256
    blocks = length // block

    def load(t):
        return pltpu.make_async_copy(group_ref(t), a_v.at[t % 2], a_sem.at[t % 2])

    load(0).start()
    fwd_setup(vt_v, seg, vec_rows, bias_v, oh_v, km_v)
    lse[...] = jnp.zeros_like(lse)

    def step(i, carry):
        t, b = i // blocks, i % blocks
        at_tick(i, ticks)

        @pl.when(b == 0)
        def _():
            load(t).wait()

            @pl.when(t + 1 < groups)
            def _():
                load(t + 1).start()

            fwd_group(t, x_v, a_v.at[t % 2], bias_v, km_v, qkv_v, ka_v, va_v)
            pltpu.make_async_copy(qkv_v.at[t], qkv.at[t], out_sem.at[0, t]).start()

        rows = pl.ds(pl.multiple_of(b * block, block), block)
        fwd_block(t, rows, block, qkv_v, ka_v, va_v, oh_v, ctx_v, lse)

        @pl.when(b == blocks - 1)
        def _():
            pltpu.make_async_copy(ctx_v.at[t], ctx.at[t], out_sem.at[1, t]).start()

        return carry

    lax.fori_loop(0, groups * blocks, step, 0)
    for t in range(groups):
        pltpu.make_async_copy(qkv_v.at[t], qkv.at[t], out_sem.at[0, t]).wait()
        pltpu.make_async_copy(ctx_v.at[t], ctx.at[t], out_sem.at[1, t]).wait()


def fwd_scratch(groups, length, width):
    return [
        pltpu.VMEM((2, 2, 2, 2, width // 8, width), BF),
        pltpu.VMEM((groups, 1, width), F32),
        pltpu.VMEM((length, LANES), BF),
        pltpu.VMEM((length, LANES), BF),
        pltpu.VMEM((groups, length, width), BF),
        pltpu.VMEM((3, length, LANES), BF),
        pltpu.VMEM((3, length, LANES), BF),
        pltpu.VMEM((groups, length, 3 * LANES), BF),
        pltpu.SemaphoreType.DMA((2,)),
        pltpu.SemaphoreType.DMA((2, groups)),
    ]


def fwd_shapes(groups, length, width):
    return [
        jax.ShapeDtypeStruct((groups, length, width), BF),
        jax.ShapeDtypeStruct((groups, length, 3 * LANES), BF),
        jax.ShapeDtypeStruct((length, LANES), F32),
        jax.ShapeDtypeStruct((16, width), F32),
    ]


def fwd_comm_kernel(shard, vec, tok, cot, seg, g, x, co, qkv, ctx, lse, vec_rows, x_v, vt_v, send, recv, loc, *s):
    place = Place()
    enter(place)
    copies = Copies(send, recv, loc)
    mk = functools.partial(GatherPart, place, copies)
    n = shard.shape[1]
    third, half = n // 3, n // 2
    first = [
        mk(shard.at[0], g.at[0], P_Y, pl.ds(0, third)),
        mk(shard.at[0], g.at[0], P_Z, pl.ds(third, third)),
        mk(shard.at[0], g.at[0], P_X, pl.ds(2 * third, third)),
        mk(vec, vt_v, P_Y, pl.ds(0, vec.shape[0]), FEATURES),
    ]
    later = [
        mk(shard.at[1], g.at[1], P_Y, pl.ds(0, half)),
        mk(shard.at[1], g.at[1], P_Z, pl.ds(half, half)),
        mk(shard.at[2], g.at[2], P_Y, pl.ds(0, half)),
        mk(shard.at[2], g.at[2], P_Z, pl.ds(half, half)),
    ]
    for part in first:
        part.begin()
    rows = start_rows(place, copies, tok, x_v)
    for stage in range(4):
        for part in first:
            part.advance()
        if stage == 0:
            for part in later:
                part.begin()
    for part in first:
        part.finish()
    wait_all(rows)
    keep = copies.here(lambda: (x_v, x))
    moved = []

    def advance(parts):
        for part in parts:
            part.advance()

    def cot_rows():
        moved.extend(start_rows(place, copies, cot, co))

    ticks = [
        (0, lambda: advance(later)),
        (1, cot_rows),
        (4, lambda: advance(later)),
        (8, lambda: advance(later)),
    ]
    fwd_core(lambda t: g.at[0, t // 2, t % 2], x_v, vt_v, seg, qkv, ctx, lse, vec_rows, s, ticks)
    advance(later)
    for part in later:
        part.finish()
    wait_all(moved)
    keep()


def fwd_comm(shard, vec, tok, cot, seg):
    groups, block, width = tok.shape
    length = groups * block
    bits = (2,) * 5
    return pl.pallas_call(
        fwd_comm_kernel,
        in_specs=[ANY] * 4 + [VMEM],
        out_specs=[ANY] * 5 + [VMEM] * 2,
        out_shape=[
            jax.ShapeDtypeStruct((3,) + bits + shard.shape[1:], BF),
            jax.ShapeDtypeStruct(tok.shape, BF),
            jax.ShapeDtypeStruct(cot.shape, BF),
        ]
        + fwd_shapes(groups, length, width),
        scratch_shapes=[
            pltpu.VMEM(tok.shape, BF),
            pltpu.VMEM(bits + vec.shape, F32),
            *sems(80),
            pltpu.SemaphoreType.DMA((20,)),
        ]
        + fwd_scratch(groups, length, width),
        compiler_params=params(0),
        name="attention_forward",
    )(shard, vec, tok, cot, seg)


def fwd_plain_kernel(g, x, vt, seg, qkv, ctx, lse, vec_rows, sem, x_v, *s):
    copy = pltpu.make_async_copy(x, x_v, sem)
    copy.start()
    copy.wait()
    fwd_core(lambda t: g.at[0, t // 2, t % 2], x_v, vt, seg, qkv, ctx, lse, vec_rows, s, [])


def fwd_plain(g, x, vt, seg):
    groups, block, width = x.shape
    length = groups * block
    return pl.pallas_call(
        fwd_plain_kernel,
        in_specs=[ANY, ANY, VMEM, VMEM],
        out_specs=[ANY] * 2 + [VMEM] * 2,
        out_shape=fwd_shapes(groups, length, width),
        scratch_shapes=[pltpu.SemaphoreType.DMA, pltpu.VMEM(x.shape, BF)] + fwd_scratch(groups, length, width),
        compiler_params=params(),
        name="attention_forward",
    )(g, x, vt, seg)


def mid_kernel(g, x, cot, ctx, vec, out, grad, gh1, dctx, sums, x_v, cot_v, ctx_v, ao_v, in_v, dn_v, act_v, dact_v, dpre_v, y1_v, g2_v, out_v, gh1_v, dctx_v, t_v, sem, out_sem):
    groups, length = ctx.shape[:2]
    width = x.shape[2]
    half = width // 2
    blocks, block = x.shape[:2]

    def copy(src, dst, i):
        return pltpu.make_async_copy(src, dst, sem.at[i])

    loads = [copy(x, x_v, 0), copy(ctx, ctx_v, 1), copy(g.at[0, :, :, half:], ao_v, 2)]
    loads += [copy(g.at[1], in_v, 3), copy(g.at[2], dn_v, 4), copy(cot, cot_v, 5)]
    for load in loads:
        load.start()
    sums[...] = jnp.zeros_like(sums)
    for load in loads:
        load.wait()
    refs = (x_v, cot_v, ctx_v, ao_v, in_v, dn_v, vec, act_v, dact_v, dpre_v, y1_v, g2_v, out_v, gh1_v, dctx_v, sums)

    def step(i, carry):
        mid_rows(i, block, refs)
        pltpu.make_async_copy(out_v.at[i], out.at[i], out_sem.at[0, i]).start()
        pltpu.make_async_copy(gh1_v.at[i], gh1.at[i], out_sem.at[1, i]).start()
        return carry

    lax.fori_loop(0, blocks, step, 0)
    send = copy(dctx_v, dctx, 0)
    send.start()
    t_v[...] = y1_v[...].T

    def in_step(t, carry):
        in_v[t] = mm(t_v[...], dpre_v[t]).astype(BF)
        pltpu.make_async_copy(in_v.at[t], grad.at[0, t], out_sem.at[2, t]).start()
        return carry

    lax.fori_loop(0, groups, in_step, 0)
    t_v[...] = g2_v[...].T

    def dn_step(t, carry):
        dn_v[t] = mm(t_v[...], act_v[t]).astype(BF)
        pltpu.make_async_copy(dn_v.at[t], grad.at[1, t], out_sem.at[3, t]).start()
        return carry

    lax.fori_loop(0, groups, dn_step, 0)
    send.wait()
    for i in range(blocks):
        pltpu.make_async_copy(out_v.at[i], out.at[i], out_sem.at[0, i]).wait()
        pltpu.make_async_copy(gh1_v.at[i], gh1.at[i], out_sem.at[1, i]).wait()
    for t in range(groups):
        pltpu.make_async_copy(in_v.at[t], grad.at[0, t], out_sem.at[2, t]).wait()
        pltpu.make_async_copy(dn_v.at[t], grad.at[1, t], out_sem.at[3, t]).wait()


def middle(g, x, cot, ctx, vec):
    groups, length, _ = ctx.shape
    blocks, block, width = x.shape
    flats = (groups, width, width)
    return pl.pallas_call(
        mid_kernel,
        in_specs=[ANY] * 4 + [VMEM],
        out_specs=[ANY] * 4 + [VMEM],
        out_shape=[
            jax.ShapeDtypeStruct(x.shape, BF),
            jax.ShapeDtypeStruct((2,) + flats, BF),
            jax.ShapeDtypeStruct(x.shape, F32),
            jax.ShapeDtypeStruct(ctx.shape, BF),
            jax.ShapeDtypeStruct((8 + groups, 8, width), F32),
        ],
        scratch_shapes=[
            pltpu.VMEM(x.shape, BF),
            pltpu.VMEM(x.shape, BF),
            pltpu.VMEM(ctx.shape, BF),
            pltpu.VMEM((groups, width, width // 2), BF),
            pltpu.VMEM(flats, BF),
            pltpu.VMEM(flats, BF),
            pltpu.VMEM((groups, length, width), BF),
            pltpu.VMEM((groups, block, width), BF),
            pltpu.VMEM((groups, length, width), BF),
            pltpu.VMEM((length, width), BF),
            pltpu.VMEM((length, width), BF),
            pltpu.VMEM(x.shape, BF),
            pltpu.VMEM(x.shape, F32),
            pltpu.VMEM(ctx.shape, BF),
            pltpu.VMEM((width, length), BF),
            pltpu.SemaphoreType.DMA((6,)),
            pltpu.SemaphoreType.DMA((4, max(groups, blocks))),
        ],
        compiler_params=params(),
        name="feed_forward",
    )(g, x, cot, ctx, vec)


def bwd_core(qkv, ctx, dctx, lse, seg, dqkv, s, ticks):
    (qkv_v, ctx_v, dctx_v, oh_v, km_v, qa_v, ka_v, va_v, da_v, kt_v, dqt_v, out_v, in_sem, out_sem) = s
    groups, length = qkv.shape[:2]
    block = 256
    blocks = length // block

    def loads(t):
        slot = t % 2
        return [
            pltpu.make_async_copy(qkv.at[t], qkv_v.at[slot], in_sem.at[0, slot]),
            pltpu.make_async_copy(ctx.at[t], ctx_v.at[slot], in_sem.at[1, slot]),
            pltpu.make_async_copy(dctx.at[t], dctx_v.at[slot], in_sem.at[2, slot]),
        ]

    for load in loads(0):
        load.start()
    oh_v[...] = jnp.where(seg[...] == lane_ids(oh_v.shape) % HD, 1.0, 0.0).astype(BF)
    km_v[...] = key_marks(seg, km_v.shape)

    def step(i, carry):
        t, b = i // blocks, i % blocks
        slot = t % 2
        at_tick(i, ticks)

        @pl.when(b == 0)
        def _():
            for load in loads(t):
                load.wait()

            @pl.when(t + 1 < groups)
            def _():
                for load in loads(t + 1):
                    load.start()

            bwd_group(t, qkv_v.at[slot], ctx_v.at[slot], dctx_v.at[slot], lse, oh_v, km_v, qa_v, ka_v, va_v, da_v, kt_v, dqt_v)

        rows = pl.ds(pl.multiple_of(b * block, block), block)
        bwd_block(rows, block, qa_v, ka_v, va_v, da_v, kt_v, dqt_v, out_v.at[t])

        @pl.when(b == blocks - 1)
        def _():
            bwd_finish(dqt_v, out_v.at[t])
            pltpu.make_async_copy(out_v.at[t], dqkv.at[t], out_sem.at[t]).start()

        return carry

    lax.fori_loop(0, groups * blocks, step, 0)
    for t in range(groups):
        pltpu.make_async_copy(out_v.at[t], dqkv.at[t], out_sem.at[t]).wait()


def bwd_scratch(groups, length, width):
    half = 3 * LANES
    return [
        pltpu.VMEM((2, length, width), BF),
        pltpu.VMEM((2, length, half), BF),
        pltpu.VMEM((2, length, half), BF),
        pltpu.VMEM((length, LANES), BF),
        pltpu.VMEM((length, LANES), BF),
        pltpu.VMEM((3, length, LANES), BF),
        pltpu.VMEM((3, length, LANES), BF),
        pltpu.VMEM((3, length, LANES), BF),
        pltpu.VMEM((3, length, LANES), BF),
        pltpu.VMEM((2, LANES, length), BF),
        pltpu.VMEM((2, LANES, length), F32),
        pltpu.VMEM((groups, length, width), BF),
        pltpu.SemaphoreType.DMA((3, 2)),
        pltpu.SemaphoreType.DMA((groups,)),
    ]


def bwd_comm_kernel(qkv, ctx, dctx, lse, seg, grad, out, dqkv, own, out_rows, total, r0, r1, r2, r3, r4, r5, r6, r7, r8, r9, send, recv, loc, *s):
    place = Place()
    enter(place)
    copies = Copies(send, recv, loc)
    n = own.shape[1]
    half = n // 2
    arrive = ((r0, r1, r2, r3, r4), (r5, r6, r7, r8, r9))
    parts = []
    for w in range(2):
        for i, order in enumerate((P_Y, P_Z)):
            rows = pl.ds(i * half, half)
            parts.append(ReducePart(place, copies, grad.at[w], total.at[w], arrive[w], own.at[w], order[::-1], rows))
    for part in parts:
        part.begin()
    moved = []

    def advance():
        for part in parts:
            part.advance()

    def rows():
        moved.extend(start_rows(place, copies, out, out_rows))

    ticks = [(1, advance), (2, rows), (6, advance), (9, advance), (12, advance), (15, advance)]
    bwd_core(qkv, ctx, dctx, lse, seg, dqkv, s, ticks)
    wait_all(moved)


def bwd_comm(qkv, ctx, dctx, lse, seg, grad, out):
    groups, length, width = qkv.shape
    n = grad.shape[6]
    arrive = arrivals(n, width, BF)
    return pl.pallas_call(
        bwd_comm_kernel,
        in_specs=[ANY] * 3 + [VMEM] * 2 + [ANY] * 2,
        out_specs=[ANY, VMEM, ANY],
        out_shape=[
            jax.ShapeDtypeStruct(qkv.shape, BF),
            jax.ShapeDtypeStruct((2, n, width), F32),
            jax.ShapeDtypeStruct(out.shape, BF),
        ],
        scratch_shapes=[
            pltpu.VMEM((2, 2, 2, 2, 2, n, width), BF),
            *arrive,
            *arrive,
            *sems(40),
            pltpu.SemaphoreType.DMA((10,)),
        ]
        + bwd_scratch(groups, length, width),
        compiler_params=params(1),
        name="attention_backward",
    )(qkv, ctx, dctx, lse, seg, grad, out)


def bwd_plain_kernel(qkv, ctx, dctx, lse, seg, dqkv, *s):
    bwd_core(qkv, ctx, dctx, lse, seg, dqkv, s, [])


def bwd_plain(qkv, ctx, dctx, lse, seg):
    groups, length, width = qkv.shape
    return pl.pallas_call(
        bwd_plain_kernel,
        in_specs=[ANY] * 3 + [VMEM] * 2,
        out_specs=ANY,
        out_shape=jax.ShapeDtypeStruct(qkv.shape, BF),
        scratch_shapes=bwd_scratch(groups, length, width),
        compiler_params=params(),
        name="attention_backward",
    )(qkv, ctx, dctx, lse, seg)


def end_loads(g, x, ctx, gh1, dqkv, refs, sem):
    a_v, x_v, ctx_v, gh1_v, dqkv_v = refs
    pairs = ((x, x_v), (gh1, gh1_v), (ctx, ctx_v), (dqkv, dqkv_v), (g.at[0], a_v))
    copies = [pltpu.make_async_copy(src, dst, sem.at[i]) for i, (src, dst) in enumerate(pairs)]
    for copy in copies:
        copy.start()
    return copies


def end_turn(x_v, gh1_v, xt_v, gt_v):
    xt_v[...] = flat(x_v[...]).T
    gt_v[...] = flat(gh1_v[...]).astype(BF).T


def end_group(t, xt_v, gt_v, ctx_v, dqkv_v, da_v, qsum_v):
    half = 3 * LANES
    d = dqkv_v[t]
    lead = d[:, :half]
    rest = d[:, half:]
    whole = da_v.reshape(dqkv_v.shape[0], *xt_v.shape[:1], d.shape[1])
    whole[t, :, :half] = mm(xt_v[...], lead).astype(BF)
    rest = mm(xt_v[...], rest) + mm(gt_v[...], ctx_v[t])
    whole[t, :, half:] = rest.astype(BF)
    qsum_v[t] = mm(jnp.ones((8, d.shape[0]), BF), d)


def end_rows(r, block, gh1_v, dqkv_v, a_v, gx_v):
    rows = pl.ds(pl.multiple_of(r * block, block), block)
    total = gh1_v[r]
    for t in range(dqkv_v.shape[0]):
        total = total + mm(dqkv_v[t, rows, :], a_v[t], NT)
    gx_v[r] = total.astype(BF)


def end_vectors(sums, qsum_v, tab_v):
    groups = qsum_v.shape[0]
    tab_v[...] = jnp.zeros_like(tab_v)
    for t in range(groups):
        tab_v[t : t + 1, :] = qsum_v[t][:1]
    parts = tab_v[...].T
    for k in range(sums.shape[0]):
        tab_v[k : k + 1, :] = jnp.sum(sums[k], axis=0, keepdims=True)
    table = tab_v[...].T
    q, v = [], []
    for t in range(groups):
        col = parts[:, t : t + 1]
        q += [col[:LANES], col[3 * LANES : 3 * LANES + HD]]
        v += [col[2 * LANES : 3 * LANES], col[5 * LANES : 5 * LANES + HD]]
    lanes = lane_ids(table.shape)
    table = jnp.where(lanes == 6, jnp.concatenate(q, axis=0), table)
    table = jnp.where(lanes == 7, jnp.concatenate(v, axis=0), table)
    return table


def sum_comm_kernel(da, vt, gx, own, vec_own, gx_rows, total, vtot, r0, r1, r2, r3, r4, r5, r6, r7, r8, r9, send, recv, loc):
    place = Place()
    enter(place)
    copies = Copies(send, recv, loc)
    third = own.shape[0] // 3
    parts = []
    for i, order in enumerate((P_Y, P_Z, P_X)):
        rows = pl.ds(i * third, third)
        parts.append(ReducePart(place, copies, da, total, (r0, r1, r2, r3, r4), own, order[::-1], rows))
    rows = pl.ds(0, vec_own.shape[0])
    parts.append(ReducePart(place, copies, vt, vtot, (r5, r6, r7, r8, r9), vec_own, P_Y[::-1], rows, FEATURES))
    for part in parts:
        part.begin()
    moved = start_rows(place, copies, gx, gx_rows)
    for stage in range(5):
        for part in parts:
            part.advance()
    wait_all(moved)


def end_scratch(x, ctx, dqkv, width):
    groups, length, _ = dqkv.shape
    return [
        pltpu.VMEM((groups, width, width), BF),
        pltpu.VMEM(x.shape, BF),
        pltpu.VMEM(ctx.shape, BF),
        pltpu.VMEM(x.shape, F32),
        pltpu.VMEM(dqkv.shape, BF),
        pltpu.VMEM((width, length), BF),
        pltpu.VMEM((width, length), BF),
        pltpu.VMEM((2,) * 5 + (width // 8, width), BF),
        pltpu.VMEM((groups, 8, width), F32),
        pltpu.VMEM(x.shape, BF),
        pltpu.VMEM((LANES, width), F32),
    ]


def sum_comm(da, vt, gx):
    n, width = da.shape[-2:]
    fine = vt.shape[-2]
    return pl.pallas_call(
        sum_comm_kernel,
        in_specs=[ANY] * 3,
        out_specs=[VMEM, VMEM, ANY],
        out_shape=[
            jax.ShapeDtypeStruct((n, width), F32),
            jax.ShapeDtypeStruct((fine, LANES), F32),
            jax.ShapeDtypeStruct(gx.shape, BF),
        ],
        scratch_shapes=[
            pltpu.VMEM((2,) * 4 + (n, width), BF),
            pltpu.VMEM((2,) * 4 + (fine, LANES), F32),
            *arrivals(n, width, BF),
            *arrivals(fine, LANES, F32),
            *sems(40),
            pltpu.SemaphoreType.DMA((10,)),
        ],
        compiler_params=params(2),
        name="weight_sums",
    )(da, vt, gx)


def end_plain_kernel(g, x, ctx, gh1, dqkv, sums, da, vt, gx, a_v, x_v, ctx_v, gh1_v, dqkv_v, xt_v, gt_v, da_v, qsum_v, gx_v, tab_v, load_sem, out_sem):
    loads = end_loads(g, x, ctx, gh1, dqkv, (a_v, x_v, ctx_v, gh1_v, dqkv_v), load_sem)
    for load in loads:
        load.wait()
    end_turn(x_v, gh1_v, xt_v, gt_v)

    def group(t, carry):
        end_group(t, xt_v, gt_v, ctx_v, dqkv_v, da_v, qsum_v)
        return carry

    lax.fori_loop(0, dqkv_v.shape[0], group, 0)
    block = gx_v.shape[1]

    def rows(r, carry):
        end_rows(r, block, gh1_v, dqkv_v, a_v, gx_v)
        return carry

    lax.fori_loop(0, gx_v.shape[0], rows, 0)
    vt[...] = end_vectors(sums, qsum_v, tab_v)
    copies = [pltpu.make_async_copy(da_v, da, out_sem.at[0]), pltpu.make_async_copy(gx_v, gx, out_sem.at[1])]
    for copy in copies:
        copy.start()
    for copy in copies:
        copy.wait()


def end_plain(g, x, ctx, gh1, dqkv, sums):
    width = x.shape[2]
    return pl.pallas_call(
        end_plain_kernel,
        in_specs=[ANY] * 5 + [VMEM],
        out_specs=[ANY, VMEM, ANY],
        out_shape=[
            jax.ShapeDtypeStruct((2,) * 5 + (width // 8, width), BF),
            jax.ShapeDtypeStruct((width, LANES), F32),
            jax.ShapeDtypeStruct(x.shape, BF),
        ],
        scratch_shapes=end_scratch(x, ctx, dqkv, width) + [pltpu.SemaphoreType.DMA((5,)), pltpu.SemaphoreType.DMA((2,))],
        compiler_params=params(),
        name="weight_gradients",
    )(g, x, ctx, gh1, dqkv, sums)


def pack(qkv_weight, out_weight, in_weight, down_weight):
    q, k, v = qkv_weight[0], qkv_weight[1], qkv_weight[2]
    o = out_weight.T
    a = [q[:, :LANES], k[:, :LANES], v[:, :LANES]]
    a += [q[:, LANES:], o[:, HD:LANES], k[:, LANES:], o[:, :HD], v[:, LANES:], o[:, LANES:]]
    return jnp.stack([jnp.concatenate(a, axis=1), in_weight, down_weight.T])


def unpack(a):
    def cut(i, half):
        start = i * LANES + half * HD
        return a[:, start : start + HD]

    heads = [jnp.concatenate([cut(i, 0), cut(i, 1), cut(3 + i, 0)], axis=1) for i in range(3)]
    out = jnp.concatenate([cut(4, 1), cut(3, 1), cut(5, 1)], axis=1)
    return jnp.stack(heads), out.T


def local(tokens, segments, qkv_weight, out_weight, in_weight, down_weight, vectors, cotangent):
    n_dp, n_t = lax.axis_size("dp"), lax.axis_size("tensor")
    groups, block, width = tokens.shape
    length = groups * block
    n = in_weight.shape[0]
    fine = vectors.shape[1]
    n_v = vectors.shape[0]
    seg = lax.dynamic_slice_in_dim(segments, lax.axis_index("tensor"), 1, 0).reshape(length, 1)
    shard = pack(qkv_weight, out_weight, in_weight, down_weight)
    vec = jnp.pad(vectors.T, ((0, 0), (0, LANES - n_v)))
    kernels = n_dp == 8 and n_t == 4
    bits = (2,) * 5
    if kernels:
        g, x, cot, qkv, ctx, lse, rows = fwd_comm(shard, vec, tokens, cotangent, seg)
    else:
        full = lax.all_gather(shard, ALL, axis=0, tiled=False).reshape(n_dp, n_t, 3, n, width)
        g = full.transpose(2, 1, 0, 3, 4).reshape((3,) + bits + (width // 8, width))
        vt = lax.all_gather(vec, ALL, axis=0, tiled=True)
        x = lax.all_to_all(tokens, "tensor", split_axis=0, concat_axis=0, tiled=True)
        cot = lax.all_to_all(cotangent, "tensor", split_axis=0, concat_axis=0, tiled=True)
        qkv, ctx, lse, rows = fwd_plain(g, x, vt, seg)
    g = g.reshape(3, groups, width, width)
    out, grad, gh1, dctx, sums = middle(g, x, cot, ctx, rows)
    if kernels:
        grad = grad.reshape((2,) + bits + (n, width))
        dqkv, own, out_rows = bwd_comm(qkv, ctx, dctx, lse, seg, grad, out)
        da, vt, gx = end_plain(g, x, ctx, gh1, dqkv, sums)
        own_a, own_v, gx_rows = sum_comm(da, vt.reshape(bits + (fine, LANES)), gx)
    else:
        dqkv = bwd_plain(qkv, ctx, dctx, lse, seg)
        da, vt, gx = end_plain(g, x, ctx, gh1, dqkv, sums)
        every_grad = jnp.concatenate([da.reshape(1, n_t, n_dp, n, width), grad.reshape(2, n_t, n_dp, n, width)])
        every_grad = every_grad.transpose(2, 1, 0, 3, 4).reshape(n_dp * n_t, 3, n, width)
        own = lax.psum_scatter(every_grad, ALL, scatter_dimension=0, tiled=True)[0].astype(F32)
        own_a, own = own[0], own[1:]
        own_v = lax.psum_scatter(vt[:, :n_v], ALL, scatter_dimension=0, tiled=True)
        out_rows = lax.all_to_all(out, "tensor", split_axis=0, concat_axis=0, tiled=True)
        gx_rows = lax.all_to_all(gx, "tensor", split_axis=0, concat_axis=0, tiled=True)
    d_qkv, d_out = unpack(own_a)
    return out_rows, gx_rows, d_qkv, d_out, own[0], own[1].T, own_v[:, :n_v].T


def solution(mesh):
    rows = P("dp", "tensor", None)
    weights = (P(None, "dp", "tensor"), P("tensor", "dp"), P("dp", "tensor"), P("tensor", "dp"), P(None, ("dp", "tensor")))
    in_specs = (rows, P("dp", None), *weights, rows)
    out_specs = (rows, rows, *weights)
    return jax.shard_map(local, mesh=mesh, in_specs=in_specs, out_specs=out_specs, check_vma=False)
```

```python
import functools

import jax
import jax.numpy as jnp
from jax import lax
from jax.experimental import pallas as pl
from jax.experimental.pallas import tpu as pltpu
from jax.sharding import PartitionSpec as P

HD = 64
LANES = 128
EPS = 1e-05
MASKED = -1e30
SEGS = 32
TOP = 35
LOG2E = 1.4426950408889634
QSCALE = LOG2E * HD**-0.5
BF = jnp.bfloat16
F32 = jnp.float32
ALL = ("dp", "tensor")
MESH = pl.DeviceIdType.MESH
ANY = pl.BlockSpec(memory_space=pl.ANY)
VMEM = pl.BlockSpec(memory_space=pltpu.VMEM)
NT = (((1,), (1,)), ((), ()))
NN = (((1,), (0,)), ((), ()))
TN = (((0,), (0,)), ((), ()))
SLOTS = ((0, (0, 1)), (1, (2,)))


def mm(a, b, dims=NN):
    return lax.dot_general(a, b, dims, preferred_element_type=F32)


def lane_ids(shape):
    return lax.broadcasted_iota(jnp.int32, shape, 1)


def low_half(shape):
    return lane_ids(shape) < HD


def swap_halves(value):
    return pltpu.roll(value, HD, 1)


def tile(ref, t, i, rows=slice(None)):
    return ref[t, rows, i * LANES : (i + 1) * LANES]


def flat(value):
    return value.reshape(-1, value.shape[-1])


def at_tick(step, ticks):
    for when, work in ticks:
        pl.when(step == when)(functools.partial(work))


def group_biases(vt):
    length = vt.shape[0]
    groups = length // (3 * HD)
    lanes = lane_ids((length, LANES))
    q, v = vt[:, 6:7], vt[:, 7:8]
    zero = jnp.zeros((LANES, 1), F32)
    out = jnp.zeros((length, LANES), F32)
    for t in range(groups):
        a, b, c = 3 * HD * t, 3 * HD * t + LANES, 3 * HD * (t + 1)
        column = jnp.concatenate([q[a:b], zero, v[a:b], q[b:c], zero[:HD], zero, v[b:c], zero[:HD]], axis=0)
        out = jnp.where(lanes == t, column, out)
    return out.T


def fwd_setup(vt_v, seg, vec_rows, bias_v, oh_v, km_v):
    vt = flat(vt_v[...])
    vec_rows[...] = vt.T[: vec_rows.shape[0]]
    biases = group_biases(vt)
    for t in range(bias_v.shape[0]):
        bias_v[t] = biases[t : t + 1]
    place = lane_ids(oh_v.shape) % HD
    same = seg[...] == place
    oh_v[...] = jnp.where(same, 1.0, 0.0).astype(BF)
    km_v[...] = key_marks(seg, km_v.shape)


def key_marks(seg, shape):
    place = lane_ids(shape) % HD
    marks = jnp.where(place < SEGS, jnp.where(seg[...] == place, 0.0, MASKED), 1.0)
    return jnp.where(place < TOP, marks, 0.0).astype(BF)


def fwd_group(t, x_v, a_v, bias_v, km_v, qkv_v, ka_v, va_v):
    x = flat(x_v[...])
    w = flat(a_v[...])
    low = low_half((x.shape[0], LANES))
    for i in range(6):
        cols = slice(i * LANES, (i + 1) * LANES)
        out = mm(x, w[:, cols]) + bias_v[t, :, cols]
        if i % 3 == 0:
            out = out * QSCALE
        out = out.astype(BF)
        qkv_v[t, :, cols] = out
        one = jnp.ones_like(out)
        if i == 1:
            ka_v[0] = jnp.where(low, out, km_v[...])
            ka_v[1] = jnp.where(low, km_v[...], out)
        if i == 2:
            va_v[0] = jnp.where(low, out, one)
            va_v[1] = jnp.where(low, one, out)
        if i == 4:
            ka_v[2] = jnp.where(low, out, km_v[...])
        if i == 5:
            va_v[2] = jnp.where(low, out, one)


def fwd_block(t, rows, block, qkv_v, ka_v, va_v, oh_v, ctx_v, lse_ref):
    shape = (block, LANES)
    low = low_half(shape)
    lanes = lane_ids(shape)
    marks = oh_v[rows, :]
    lse = lse_ref[rows, :]
    parts = []
    for h in range(3):
        q = tile(qkv_v, t, 0 if h < 2 else 3, rows)
        q = jnp.where(low, marks, q) if h == 1 else jnp.where(low, q, marks)
        s = mm(q, ka_v[h], NT)
        top = jnp.max(s, axis=1, keepdims=True)
        w = jnp.exp2(s - top).astype(BF)
        o = mm(w, va_v[h])
        total = o[:, HD : HD + 1] if h != 1 else o[:, 0:1]
        lse = jnp.where(lanes == 3 * t + h, top + jnp.log2(total), lse)
        parts.append(o)
    lse_ref[rows, :] = lse
    sums = swap_halves(jnp.where(low, parts[1], parts[0]))
    pair = jnp.where(low, parts[0], parts[1]) / sums
    last = parts[2] / swap_halves(parts[2])
    zero = jnp.zeros(shape, F32)
    tiles = (pair, swap_halves(pair), swap_halves(last))
    for i, value in enumerate(tiles):
        ctx_v[t, rows, i * LANES : (i + 1) * LANES] = jnp.where(low, zero, value).astype(BF)


def spread(base, value, lanes):
    hi = value.astype(BF).astype(F32)
    rest = value - hi
    mid = rest.astype(BF).astype(F32)
    low = rest - mid
    place = lanes % HD
    out = jnp.where(place == SEGS, hi, jnp.where(place == SEGS + 1, mid, jnp.where(place == SEGS + 2, low, 0.0)))
    return jnp.where(place < SEGS, base, out.astype(BF))


def bwd_group(t, qkv, ctx, dctx, lse, oh_v, km_v, qa_v, ka_v, va_v, da_v, kt_v, dqt_v):
    length = oh_v.shape[0]
    shape = (length, LANES)
    low = low_half(shape)
    lanes = lane_ids(shape)
    oh, km = oh_v[...], km_v[...]
    ones = jnp.where((lanes % HD >= SEGS) & (lanes % HD < TOP), 1.0, 0.0).astype(BF)

    def cols(ref, i):
        return ref[:, i * LANES : (i + 1) * LANES]

    q, k, v = cols(qkv, 0), cols(qkv, 1), cols(qkv, 2)
    q2, k2, v2 = cols(qkv, 3), cols(qkv, 4), cols(qkv, 5)
    c_pair = jnp.where(low, swap_halves(cols(ctx, 1)), cols(ctx, 0))
    d_pair = jnp.where(low, swap_halves(cols(dctx, 1)), cols(dctx, 0))
    c_last = swap_halves(cols(ctx, 2))
    d_last = swap_halves(cols(dctx, 2))
    prod = c_pair.astype(F32) * d_pair.astype(F32)
    prod2 = c_last.astype(F32) * d_last.astype(F32)
    lse_all = lse[...]
    zero = jnp.zeros_like(prod)
    for h in range(3):
        mine = low if h != 1 else jnp.logical_not(low)
        delta = jnp.sum(jnp.where(mine, prod2 if h == 2 else prod, zero), axis=1, keepdims=True)
        top = jnp.sum(jnp.where(lanes == 3 * t + h, lse_all, zero), axis=1, keepdims=True)
        qa_v[h] = jnp.where(mine, q2 if h == 2 else q, spread(oh, -top, lanes))
        da_v[h] = jnp.where(mine, d_last if h == 2 else d_pair, spread(jnp.zeros_like(oh), -delta, lanes))
        ka_v[h] = jnp.where(mine, k2 if h == 2 else k, km)
        va_v[h] = jnp.where(mine, v2 if h == 2 else v, ones)
    kt_v[0] = k.T
    kt_v[1] = k2.T
    dqt_v[...] = jnp.zeros_like(dqt_v)


def bwd_block(rows, block, qa_v, ka_v, va_v, da_v, kt_v, dqt_v, out):
    low = low_half((block, LANES))
    dk, dv = [], []
    for h in range(3):
        s = mm(ka_v[h, rows, :], qa_v[h], NT)
        p = jnp.exp2(s)
        dv.append(mm(p.astype(BF), da_v[h]))
        dp = mm(va_v[h, rows, :], da_v[h], NT)
        ds = (p * dp).astype(BF)
        dk.append(mm(ds, qa_v[h]) * (1.0 / LOG2E))
        slot, half = h // 2, slice((h % 2) * HD, (h % 2 + 1) * HD)
        dqt_v[slot, half, :] += mm(kt_v[slot, half, rows], ds)
    zero = jnp.zeros((block, LANES), F32)
    tiles = {
        1: jnp.where(low, dk[0], dk[1]),
        2: jnp.where(low, dv[0], dv[1]),
        4: jnp.where(low, dk[2], zero),
        5: jnp.where(low, dv[2], zero),
    }
    for i, value in tiles.items():
        out[rows, i * LANES : (i + 1) * LANES] = value.astype(BF)


def bwd_finish(dqt_v, out):
    scale = HD**-0.5
    low = low_half((out.shape[0], LANES))
    out[:, 0:LANES] = (dqt_v[0].T * scale).astype(BF)
    last = dqt_v[1].T * scale
    out[:, 3 * LANES : 4 * LANES] = jnp.where(low, last, jnp.zeros_like(last)).astype(BF)


def normalize(values, gain_row, shift_row):
    average = jnp.mean(values, axis=-1, keepdims=True)
    centered = values - average
    variance = jnp.mean(centered * centered, axis=-1, keepdims=True)
    inverse = lax.rsqrt(variance + EPS)
    unit = centered * inverse
    return unit * gain_row + shift_row, unit, inverse


def normalize_back(upstream, unit, inverse, gain_row):
    d_unit = upstream * gain_row
    first = jnp.mean(d_unit, axis=-1, keepdims=True)
    second = jnp.mean(d_unit * unit, axis=-1, keepdims=True)
    return inverse * (d_unit - first - unit * second)


def eighths(value):
    return jnp.sum(value.reshape(-1, 8, value.shape[-1]), axis=0)


def gelu_both(x):
    a = jnp.abs(x)
    tail = jnp.exp2(x * x * (-0.5 * LOG2E))
    t = 1.0 / (1.0 + (0.3275911 * 0.5**0.5) * a)
    poly = ((((1.061405429 * t - 1.453152027) * t + 1.421413741) * t - 0.284496736) * t + 0.254829592) * t
    rest = 0.5 * poly * tail
    cdf = jnp.where(x < 0, rest, 1.0 - rest)
    return x * cdf, cdf + x * tail * 0.3989422804014327


def mid_rows(i, block, refs):
    (x_v, cot_v, ctx_v, ao_v, in_v, dn_v, vec, act_v, dact_v, dpre_v, y1_v, g2_v, out_v, gh1_v, dctx_v, sums_v) = refs
    rows = pl.ds(pl.multiple_of(i * block, block), block)
    groups = in_v.shape[0]

    def row(k):
        return vec[k : k + 1, :]

    def note(k, value):
        sums_v[k] += eighths(value)

    attn = mm(ctx_v[0, rows, :], ao_v[0], NT)
    for t in range(1, groups):
        attn = attn + mm(ctx_v[t, rows, :], ao_v[t], NT)
    h1 = x_v[i].astype(F32) + attn + row(4)
    y1, u1, r1 = normalize(h1, row(0), row(1))
    y1_low = y1.astype(BF)
    y1_v[rows, :] = y1_low
    ffn = row(5) + y1
    for t in range(groups):
        pre = mm(y1_low, in_v[t]) + row(8 + t)
        act, slope = gelu_both(pre)
        act = act.astype(BF)
        act_v[t, rows, :] = act
        dact_v[t] = slope.astype(BF)
        ffn = ffn + mm(act, dn_v[t], NT)
    out, u2, r2 = normalize(ffn, row(2), row(3))
    out_v[i] = out.astype(BF)
    up = cot_v[i].astype(F32)
    g_h2 = normalize_back(up, u2, r2, row(2))
    note(2, up * u2)
    note(3, up)
    note(5, g_h2)
    g2 = g_h2.astype(BF)
    g2_v[rows, :] = g2
    g_y1 = g_h2
    for t in range(groups):
        dpre = (mm(g2, dn_v[t]) * dact_v[t].astype(F32)).astype(BF)
        dpre_v[t, rows, :] = dpre
        note(8 + t, dpre.astype(F32))
        g_y1 = g_y1 + mm(dpre, in_v[t], NT)
    note(0, g_y1 * u1)
    note(1, g_y1)
    g_h1 = normalize_back(g_y1, u1, r1, row(0))
    note(4, g_h1)
    gh1_v[i] = g_h1
    g1 = g_h1.astype(BF)
    for t in range(groups):
        dctx_v[t, rows, :] = mm(g1, ao_v[t]).astype(BF)

STEP = {"z2": 4, "z1": 2, "y": 1, "x": 2, "c": 1}
BLOCKS = ("x", "c", "z2", "z1", "y")
FEATURES = ("z2", "z1", "y", "x", "c")
P_Y = ("z2", "z1", "x", "y")
P_Z = ("z2", "x", "y", "z1")
Q_Y = ("z2", "x", "z1", "y")
Q_Z = ("z2", "x", "y", "z1")
Q_X = ("x", "z2", "z1", "y")
Q_M = ("y", "z2", "x", "z1")


class Place:
    def __init__(self):
        self.d = lax.axis_index("dp")
        self.t = lax.axis_index("tensor")
        self.bit = {
            "x": self.t // 2,
            "c": self.t % 2,
            "z2": self.d // 4,
            "z1": (self.d // 2) % 2,
            "y": self.d % 2,
        }

    def flip(self, dim):
        return 1 - self.bit[dim]

    def peer(self, dim):
        move = STEP[dim] * (1 - 2 * self.bit[dim])
        if dim in ("x", "c"):
            return (self.d, self.t + move)
        return (self.d + move, self.t)

    def row_peer(self, k):
        t = self.t
        if k in (1, 3):
            t = t + (1 - 2 * self.bit["c"])
        if k in (2, 3):
            t = t + 2 * (1 - 2 * self.bit["x"])
        return t

    def index(self, dims, **chosen):
        return tuple(chosen.get(dim, self.bit[dim]) for dim in dims)


def enter(place):
    bar = pltpu.get_barrier_semaphore()
    peers = [place.peer(dim) for dim in BLOCKS] + [(place.d, place.row_peer(3))]
    for peer in peers:
        pl.semaphore_signal(bar, inc=1, device_id=peer, device_id_type=MESH)
    pl.semaphore_wait(bar, len(peers))


class Copies:
    def __init__(self, send, recv, local):
        self.send, self.recv, self.local = send, recv, local
        self.count = self.locals = 0

    def remote(self, ends):
        i = self.count
        self.count += 1

        def copy():
            src, dst, peer = ends()
            return pltpu.make_async_remote_copy(
                src_ref=src,
                dst_ref=dst,
                send_sem=self.send.at[i],
                recv_sem=self.recv.at[i],
                device_id=peer,
                device_id_type=MESH,
            )

        copy().start()
        return lambda: copy().wait()

    def here(self, ends):
        i = self.locals
        self.locals += 1

        def copy():
            src, dst = ends()
            return pltpu.make_async_copy(src, dst, self.local.at[i])

        copy().start()
        return lambda: copy().wait()


ALLBITS = slice(None)


class GatherPart:
    def __init__(self, place, copies, own, full, order, rows, dims=BLOCKS):
        self.place, self.copies, self.own, self.full, self.order = place, copies, own, full, order
        self.rows, self.dims = rows, dims
        self.stage = 0
        self.side = []

    def at(self, **chosen):
        return self.full.at[self.place.index(self.dims, **chosen) + (self.rows,)]

    def begin(self):
        p, c = self.place, self.copies
        self.current = c.remote(lambda: (self.own.at[self.rows], self.at(), p.peer(self.order[0])))
        self.side.append(c.remote(lambda: (self.own.at[self.rows], self.at(), p.peer("c"))))
        self.keep = c.here(lambda: (self.own.at[self.rows], self.at()))

    def held(self, s):
        return self.at(**{dim: ALLBITS for dim in self.order[:s]})

    def arrived(self, s):
        dim = self.order[s]
        return self.at(**{other: ALLBITS for other in self.order[:s]}, **{dim: self.place.flip(dim)})

    def advance(self):
        p, c, s = self.place, self.copies, self.stage
        self.current()
        if s == 0:
            self.keep()
        if s + 1 < len(self.order):
            self.current = c.remote(lambda: (self.held(s + 1), self.held(s + 1), p.peer(self.order[s + 1])))
        self.side.append(c.remote(lambda: (self.arrived(s), self.arrived(s), p.peer("c"))))
        self.stage = s + 1

    def finish(self):
        wait_all(self.side)


def every(count, work):
    if count == 0:
        work(())
        return

    def body(i, carry):
        work(tuple((i // 2**j) % 2 for j in reversed(range(count))))
        return carry

    lax.fori_loop(0, 2**count, body, 0)


def blockwise(ref):
    return ref.reshape(2 ** (len(ref.shape) - 2), *ref.shape[-2:])


def spot(bits):
    place = 0
    for bit in bits:
        place = 2 * place + bit
    return place


class ReducePart:
    def __init__(self, place, copies, src, total, arrive, out, order, rows, dims=BLOCKS):
        self.place, self.copies, self.src, self.total, self.arrive = place, copies, src, total, arrive
        self.out, self.order, self.rows, self.dims = out, order, rows, dims
        self.inner = tuple(dim for dim in dims if dim != "c")
        self.kept = self.inner
        if total is None:
            self.total, self.kept = src, dims
        self.stage = 0

    def source(self, **chosen):
        return self.src.at[self.place.index(self.dims, **chosen) + (self.rows,)]

    def sums(self, **chosen):
        return self.total.at[self.place.index(self.kept, **chosen) + (self.rows,)]

    def half(self, bit):
        p, first = self.place, self.order[0]

        def ends():
            free = {dim: ALLBITS for dim in self.inner}
            free[first] = bit()
            dst = self.arrive[0].at[p.index(self.inner, **free) + (self.rows,)]
            return self.source(c=p.flip("c"), **free), dst, p.peer("c")

        return self.copies.remote(ends)

    def begin(self):
        p, first = self.place, self.order[0]
        self.side = [self.half(lambda: p.flip(first)), self.half(lambda: p.bit[first])]
        if self.kept is self.inner:
            free = {dim: ALLBITS for dim in self.inner}
            self.keep = self.copies.here(lambda: (self.source(**free), self.sums(**free)))

    def add(self, fixed, bit):
        s = self.stage
        left = [dim for dim in self.inner if dim not in self.order[:s]] if s else list(self.inner)
        loose = [dim for dim in left if dim != fixed]

        total, arrive = blockwise(self.total), blockwise(self.arrive[s])

        def work(bits):
            chosen = dict(zip(loose, bits))
            chosen[fixed] = bit
            mine = spot(self.place.index(self.kept, **chosen))
            there = spot(tuple(chosen[dim] for dim in left))
            both = total[mine, self.rows, :].astype(F32) + arrive[there, self.rows, :].astype(F32)
            total[mine, self.rows, :] = both.astype(total.dtype)

        every(len(loose), work)

    def send(self):
        p, s = self.place, self.stage
        dim = self.order[s]
        free = {other: ALLBITS for other in self.order[s + 1 :]}

        def ends():
            src = self.sums(**free, **{dim: p.flip(dim)})
            dst = self.arrive[s + 1].at[(ALLBITS,) * len(free) + (self.rows,)]
            return src, dst, p.peer(dim)

        return self.copies.remote(ends)

    def advance(self):
        p, s = self.place, self.stage
        if s == 0:
            if self.kept is self.inner:
                self.keep()
            self.side[0]()
        else:
            self.current()
        if s < len(self.order):
            dim = self.order[s]
            self.add(dim, p.flip(dim))
            self.current = self.send()
            if s == 0:
                self.side[1]()
            self.add(dim, p.bit[dim])
        else:
            mine = spot(self.place.index(self.kept))
            self.out[self.rows, :] = blockwise(self.total)[mine, self.rows, :].astype(F32) + self.arrive[s][self.rows, :].astype(F32)
        self.stage = s + 1


def arrivals(rows, cols, dtype):
    return [pltpu.VMEM((2,) * n + (rows, cols), dtype) for n in (4, 3, 2, 1, 0)]


def start_row(place, copies, src, dst, k):
    def ends():
        to = place.row_peer(k)
        return src.at[to], dst.at[place.t], (place.d, to)

    return copies.remote(ends)


def keep_row(place, copies, src, dst):
    return copies.here(lambda: (src.at[place.t], dst.at[place.t]))


def start_rows(place, copies, src, dst):
    return [start_row(place, copies, src, dst, k) for k in (2, 3, 1)] + [keep_row(place, copies, src, dst)]


def wait_all(waits):
    for wait in waits:
        wait()


def params(collective=None):
    more = {} if collective is None else {"collective_id": collective, "has_side_effects": True}
    return pltpu.CompilerParams(vmem_limit_bytes=60 << 20, **more)


def sems(count):
    return [pltpu.SemaphoreType.DMA((count,))] * 2


def fwd_core(group_ref, x_v, vt_v, seg, qkv, ctx, lse, vec_rows, s, ticks):
    (a_v, bias_v, oh_v, km_v, qkv_v, ka_v, va_v, ctx_v, a_sem, out_sem) = s
    groups, length = qkv.shape[:2]
    block = 256
    blocks = length // block

    def load(t):
        return pltpu.make_async_copy(group_ref(t), a_v.at[t % 2], a_sem.at[t % 2])

    load(0).start()
    fwd_setup(vt_v, seg, vec_rows, bias_v, oh_v, km_v)
    lse[...] = jnp.zeros_like(lse)

    def step(i, carry):
        t, b = i // blocks, i % blocks
        at_tick(i, ticks)

        @pl.when(b == 0)
        def _():
            load(t).wait()

            @pl.when(t + 1 < groups)
            def _():
                load(t + 1).start()

            fwd_group(t, x_v, a_v.at[t % 2], bias_v, km_v, qkv_v, ka_v, va_v)
            pltpu.make_async_copy(qkv_v.at[t], qkv.at[t], out_sem.at[0, t]).start()

        rows = pl.ds(pl.multiple_of(b * block, block), block)
        fwd_block(t, rows, block, qkv_v, ka_v, va_v, oh_v, ctx_v, lse)

        @pl.when(b == blocks - 1)
        def _():
            pltpu.make_async_copy(ctx_v.at[t], ctx.at[t], out_sem.at[1, t]).start()

        return carry

    lax.fori_loop(0, groups * blocks, step, 0)
    for t in range(groups):
        pltpu.make_async_copy(qkv_v.at[t], qkv.at[t], out_sem.at[0, t]).wait()
        pltpu.make_async_copy(ctx_v.at[t], ctx.at[t], out_sem.at[1, t]).wait()


def fwd_scratch(groups, length, width):
    return [
        pltpu.VMEM((2, 2, 2, 2, width // 8, width), BF),
        pltpu.VMEM((groups, 1, width), F32),
        pltpu.VMEM((length, LANES), BF),
        pltpu.VMEM((length, LANES), BF),
        pltpu.VMEM((groups, length, width), BF),
        pltpu.VMEM((3, length, LANES), BF),
        pltpu.VMEM((3, length, LANES), BF),
        pltpu.VMEM((groups, length, 3 * LANES), BF),
        pltpu.SemaphoreType.DMA((2,)),
        pltpu.SemaphoreType.DMA((2, groups)),
    ]


def fwd_shapes(groups, length, width):
    return [
        jax.ShapeDtypeStruct((groups, length, width), BF),
        jax.ShapeDtypeStruct((groups, length, 3 * LANES), BF),
        jax.ShapeDtypeStruct((length, LANES), F32),
        jax.ShapeDtypeStruct((16, width), F32),
    ]


def fwd_comm_kernel(shard, vec, tok, cot, seg, g, x, co, qkv, ctx, lse, vec_rows, x_v, vt_v, send, recv, loc, *s):
    place = Place()
    enter(place)
    copies = Copies(send, recv, loc)
    mk = functools.partial(GatherPart, place, copies)
    n = shard.shape[1]
    third, half = n // 3, n // 2
    first = [
        mk(shard.at[0], g.at[0], Q_X, pl.ds(0, third)),
        mk(shard.at[0], g.at[0], Q_Y, pl.ds(third, third)),
        mk(shard.at[0], g.at[0], Q_Z, pl.ds(2 * third, third)),
        mk(vec, vt_v, Q_Y, pl.ds(0, vec.shape[0]), FEATURES),
    ]
    later = [
        mk(shard.at[1], g.at[1], Q_Y, pl.ds(0, half)),
        mk(shard.at[1], g.at[1], Q_Z, pl.ds(half, half)),
        mk(shard.at[2], g.at[2], Q_M, pl.ds(0, half)),
        mk(shard.at[2], g.at[2], Q_Y, pl.ds(half, half)),
    ]
    moved = []

    def advance(*which):
        for i in which:
            later[i].advance()

    def cot_rows():
        moved.extend(start_rows(place, copies, cot, co))

    for part in first:
        part.begin()
    rows = start_rows(place, copies, tok, x_v)
    for stage in range(4):
        for part in first:
            part.advance()
        if stage == 1:
            for part in later:
                part.begin()
        if stage > 1:
            advance(0, 1, 2, 3)
    for part in first:
        part.finish()
    wait_all(rows)
    keep = copies.here(lambda: (x_v, x))
    ticks = [
        (0, cot_rows),
        (4, functools.partial(advance, 1)),
        (7, functools.partial(advance, 0, 2, 3)),
        (15, functools.partial(advance, 1)),
    ]
    fwd_core(lambda t: g.at[0, t // 2, t % 2], x_v, vt_v, seg, qkv, ctx, lse, vec_rows, s, ticks)
    advance(2, 0, 3)
    for part in later:
        part.finish()
    wait_all(moved)
    keep()


def fwd_comm(shard, vec, tok, cot, seg):
    groups, block, width = tok.shape
    length = groups * block
    bits = (2,) * 5
    return pl.pallas_call(
        fwd_comm_kernel,
        in_specs=[ANY] * 4 + [VMEM],
        out_specs=[ANY] * 5 + [VMEM] * 2,
        out_shape=[
            jax.ShapeDtypeStruct((3,) + bits + shard.shape[1:], BF),
            jax.ShapeDtypeStruct(tok.shape, BF),
            jax.ShapeDtypeStruct(cot.shape, BF),
        ]
        + fwd_shapes(groups, length, width),
        scratch_shapes=[
            pltpu.VMEM(tok.shape, BF),
            pltpu.VMEM(bits + vec.shape, F32),
            *sems(80),
            pltpu.SemaphoreType.DMA((20,)),
        ]
        + fwd_scratch(groups, length, width),
        compiler_params=params(0),
        name="attention_forward",
    )(shard, vec, tok, cot, seg)


def fwd_plain_kernel(g, x, vt, seg, qkv, ctx, lse, vec_rows, sem, x_v, *s):
    copy = pltpu.make_async_copy(x, x_v, sem)
    copy.start()
    copy.wait()
    fwd_core(lambda t: g.at[0, t // 2, t % 2], x_v, vt, seg, qkv, ctx, lse, vec_rows, s, [])


def fwd_plain(g, x, vt, seg):
    groups, block, width = x.shape
    length = groups * block
    return pl.pallas_call(
        fwd_plain_kernel,
        in_specs=[ANY, ANY, VMEM, VMEM],
        out_specs=[ANY] * 2 + [VMEM] * 2,
        out_shape=fwd_shapes(groups, length, width),
        scratch_shapes=[pltpu.SemaphoreType.DMA, pltpu.VMEM(x.shape, BF)] + fwd_scratch(groups, length, width),
        compiler_params=params(),
        name="attention_forward",
    )(g, x, vt, seg)


def mid_kernel(g, x, cot, ctx, vec, out, grad, gh1, dctx, sums, x_v, cot_v, ctx_v, ao_v, in_v, dn_v, act_v, dact_v, dpre_v, y1_v, g2_v, out_v, gh1_v, dctx_v, t_v, sem, out_sem):
    groups, length = ctx.shape[:2]
    width = x.shape[2]
    half = width // 2
    blocks, block = x.shape[:2]

    def copy(src, dst, i):
        return pltpu.make_async_copy(src, dst, sem.at[i])

    loads = [copy(x, x_v, 0), copy(ctx, ctx_v, 1), copy(g.at[0, :, :, half:], ao_v, 2)]
    loads += [copy(g.at[1], in_v, 3), copy(g.at[2], dn_v, 4), copy(cot, cot_v, 5)]
    for load in loads:
        load.start()
    sums[...] = jnp.zeros_like(sums)
    for load in loads:
        load.wait()
    refs = (x_v, cot_v, ctx_v, ao_v, in_v, dn_v, vec, act_v, dact_v, dpre_v, y1_v, g2_v, out_v, gh1_v, dctx_v, sums)

    def step(i, carry):
        mid_rows(i, block, refs)
        pltpu.make_async_copy(out_v.at[i], out.at[i], out_sem.at[0, i]).start()
        pltpu.make_async_copy(gh1_v.at[i], gh1.at[i], out_sem.at[1, i]).start()
        return carry

    lax.fori_loop(0, blocks, step, 0)
    send = copy(dctx_v, dctx, 0)
    send.start()
    t_v[...] = y1_v[...].T

    def in_step(t, carry):
        in_v[t] = mm(t_v[...], dpre_v[t]).astype(BF)
        pltpu.make_async_copy(in_v.at[t], grad.at[0, t], out_sem.at[2, t]).start()
        return carry

    lax.fori_loop(0, groups, in_step, 0)
    t_v[...] = g2_v[...].T

    def dn_step(t, carry):
        dn_v[t] = mm(t_v[...], act_v[t]).astype(BF)
        pltpu.make_async_copy(dn_v.at[t], grad.at[1, t], out_sem.at[3, t]).start()
        return carry

    lax.fori_loop(0, groups, dn_step, 0)
    send.wait()
    for i in range(blocks):
        pltpu.make_async_copy(out_v.at[i], out.at[i], out_sem.at[0, i]).wait()
        pltpu.make_async_copy(gh1_v.at[i], gh1.at[i], out_sem.at[1, i]).wait()
    for t in range(groups):
        pltpu.make_async_copy(in_v.at[t], grad.at[0, t], out_sem.at[2, t]).wait()
        pltpu.make_async_copy(dn_v.at[t], grad.at[1, t], out_sem.at[3, t]).wait()


def middle(g, x, cot, ctx, vec):
    groups, length, _ = ctx.shape
    blocks, block, width = x.shape
    flats = (groups, width, width)
    return pl.pallas_call(
        mid_kernel,
        in_specs=[ANY] * 4 + [VMEM],
        out_specs=[ANY] * 4 + [VMEM],
        out_shape=[
            jax.ShapeDtypeStruct(x.shape, BF),
            jax.ShapeDtypeStruct((2,) + flats, BF),
            jax.ShapeDtypeStruct(x.shape, F32),
            jax.ShapeDtypeStruct(ctx.shape, BF),
            jax.ShapeDtypeStruct((8 + groups, 8, width), F32),
        ],
        scratch_shapes=[
            pltpu.VMEM(x.shape, BF),
            pltpu.VMEM(x.shape, BF),
            pltpu.VMEM(ctx.shape, BF),
            pltpu.VMEM((groups, width, width // 2), BF),
            pltpu.VMEM(flats, BF),
            pltpu.VMEM(flats, BF),
            pltpu.VMEM((groups, length, width), BF),
            pltpu.VMEM((groups, block, width), BF),
            pltpu.VMEM((groups, length, width), BF),
            pltpu.VMEM((length, width), BF),
            pltpu.VMEM((length, width), BF),
            pltpu.VMEM(x.shape, BF),
            pltpu.VMEM(x.shape, F32),
            pltpu.VMEM(ctx.shape, BF),
            pltpu.VMEM((width, length), BF),
            pltpu.SemaphoreType.DMA((6,)),
            pltpu.SemaphoreType.DMA((4, max(groups, blocks))),
        ],
        compiler_params=params(),
        name="feed_forward",
    )(g, x, cot, ctx, vec)


def bwd_core(qkv, ctx, dctx, lse, seg, x, gh1, g, da, gx, qsum, s, ticks):
    (qkv_v, ctx_v, dctx_v, a_v, oh_v, km_v, qa_v, ka_v, va_v, da_v, kt_v, dqt_v, dqkv_v, x_v, gx_v, xt_v, gt_v, dw_v, in_sem, out_sem, x_sem) = s
    groups, length = qkv.shape[:2]
    block = 256
    blocks = length // block
    half = 3 * LANES

    def loads(t):
        slot = t % 2
        return [
            pltpu.make_async_copy(qkv.at[t], qkv_v.at[slot], in_sem.at[0, slot]),
            pltpu.make_async_copy(ctx.at[t], ctx_v.at[slot], in_sem.at[1, slot]),
            pltpu.make_async_copy(dctx.at[t], dctx_v.at[slot], in_sem.at[2, slot]),
            pltpu.make_async_copy(g.at[0, t], a_v.at[slot], in_sem.at[3, slot]),
        ]

    def result(t):
        return pltpu.make_async_copy(dw_v.at[t], da.at[t], out_sem.at[t])

    more = [pltpu.make_async_copy(x, x_v, x_sem.at[0]), pltpu.make_async_copy(gh1, gx_v, x_sem.at[1])]
    for load in loads(0) + more:
        load.start()
    oh_v[...] = jnp.where(seg[...] == lane_ids(oh_v.shape) % HD, 1.0, 0.0).astype(BF)
    km_v[...] = key_marks(seg, km_v.shape)
    for load in more:
        load.wait()
    xt_v[...] = flat(x_v[...]).T
    gt_v[...] = flat(gx_v[...]).astype(BF).T

    def weights(t, slot):
        def chunk(r, inner):
            part = pl.ds(pl.multiple_of(r * block, block), block)
            dw_v[t, part, :half] = mm(xt_v[part, :], dqkv_v[:, :half]).astype(BF)
            dw_v[t, part, half:] = (mm(xt_v[part, :], dqkv_v[:, half:]) + mm(gt_v[part, :], ctx_v[slot])).astype(BF)
            return inner

        lax.fori_loop(0, dw_v.shape[1] // block, chunk, 0)
        qsum[t] = mm(jnp.ones((8, length), BF), dqkv_v[...])

    def rows(b, slot):
        part = pl.ds(pl.multiple_of(b * block, block), block)
        gx_v[b] = gx_v[b] + mm(dqkv_v[part, :], a_v[slot], NT)

    def step(i, carry):
        t, b = i // blocks, i % blocks
        slot = t % 2
        at_tick(i, ticks)

        @pl.when(b == 0)
        def _():
            for load in loads(t):
                load.wait()

            @pl.when(t + 1 < groups)
            def _():
                for load in loads(t + 1):
                    load.start()

            bwd_group(t, qkv_v.at[slot], ctx_v.at[slot], dctx_v.at[slot], lse, oh_v, km_v, qa_v, ka_v, va_v, da_v, kt_v, dqt_v)

        part = pl.ds(pl.multiple_of(b * block, block), block)
        bwd_block(part, block, qa_v, ka_v, va_v, da_v, kt_v, dqt_v, dqkv_v)

        @pl.when(b == blocks - 1)
        def _():
            bwd_finish(dqt_v, dqkv_v)
            weights(t, slot)
            result(t).start()

            def row_step(r, inner):
                rows(r, slot)
                return inner

            lax.fori_loop(0, blocks, row_step, 0)

        return carry

    lax.fori_loop(0, groups * blocks, step, 0)

    def low_step(r, carry):
        x_v[r] = gx_v[r].astype(BF)
        return carry

    lax.fori_loop(0, blocks, low_step, 0)
    last = pltpu.make_async_copy(x_v, gx, x_sem.at[0])
    last.start()
    for t in range(groups):
        result(t).wait()
    last.wait()


def bwd_scratch(groups, length, width, x):
    half = 3 * LANES
    return [
        pltpu.VMEM((2, length, width), BF),
        pltpu.VMEM((2, length, half), BF),
        pltpu.VMEM((2, length, half), BF),
        pltpu.VMEM((2, width, width), BF),
        pltpu.VMEM((length, LANES), BF),
        pltpu.VMEM((length, LANES), BF),
        pltpu.VMEM((3, length, LANES), BF),
        pltpu.VMEM((3, length, LANES), BF),
        pltpu.VMEM((3, length, LANES), BF),
        pltpu.VMEM((3, length, LANES), BF),
        pltpu.VMEM((2, LANES, length), BF),
        pltpu.VMEM((2, LANES, length), F32),
        pltpu.VMEM((length, width), BF),
        pltpu.VMEM(x, BF),
        pltpu.VMEM(x, F32),
        pltpu.VMEM((width, length), BF),
        pltpu.VMEM((width, length), BF),
        pltpu.VMEM((groups, width, width), BF),
        pltpu.SemaphoreType.DMA((4, 2)),
        pltpu.SemaphoreType.DMA((groups,)),
        pltpu.SemaphoreType.DMA((2,)),
    ]


def bwd_shapes(groups, width, x):
    return [
        jax.ShapeDtypeStruct((groups, width, width), BF),
        jax.ShapeDtypeStruct(x, BF),
        jax.ShapeDtypeStruct((groups, 8, width), F32),
    ]


def bwd_comm_kernel(qkv, ctx, dctx, lse, seg, x, gh1, g, grad, out, da, gx, qsum, own, out_rows, total, r0, r1, r2, r3, r4, r5, r6, r7, r8, r9, send, recv, loc, *s):
    place = Place()
    enter(place)
    copies = Copies(send, recv, loc)
    half = own.shape[1] // 2
    arrive = ((r0, r1, r2, r3, r4), (r5, r6, r7, r8, r9))
    parts = []
    for w, orders in enumerate(((P_Y, P_Z), (Q_Y, Q_Z))):
        for i, order in enumerate(orders):
            rows = pl.ds(i * half, half)
            parts.append(ReducePart(place, copies, grad.at[w], total.at[w], arrive[w], own.at[w], order[::-1], rows))
    for part in parts:
        part.begin()
    moved = []

    def advance(*which):
        for i in which:
            parts[i].advance()

    def rows():
        moved.extend(start_rows(place, copies, out, out_rows))

    ticks = [
        (2, functools.partial(advance, 0, 1, 2, 3)),
        (3, rows),
        (9, functools.partial(advance, 0, 1, 2, 3)),
        (12, functools.partial(advance, 0, 2)),
        (13, functools.partial(advance, 1, 3)),
        (14, functools.partial(advance, 0, 2)),
        (15, functools.partial(advance, 1, 3)),
    ]
    bwd_core(qkv, ctx, dctx, lse, seg, x, gh1, g, da, gx, qsum, s, ticks)
    advance(0, 1, 2, 3)
    wait_all(moved)


def bwd_comm(qkv, ctx, dctx, lse, seg, x, gh1, g, grad, out):
    groups, length, width = qkv.shape
    n = grad.shape[6]
    arrive = arrivals(n, width, BF)
    return pl.pallas_call(
        bwd_comm_kernel,
        in_specs=[ANY] * 3 + [VMEM] * 2 + [ANY] * 5,
        out_specs=[ANY, ANY, VMEM, VMEM, ANY],
        out_shape=bwd_shapes(groups, width, x.shape)
        + [
            jax.ShapeDtypeStruct((2, n, width), F32),
            jax.ShapeDtypeStruct(out.shape, BF),
        ],
        scratch_shapes=[
            pltpu.VMEM((2, 2, 2, 2, 2, n, width), BF),
            *arrive,
            *arrive,
            *sems(40),
            pltpu.SemaphoreType.DMA((10,)),
        ]
        + bwd_scratch(groups, length, width, x.shape),
        compiler_params=params(1),
        name="attention_backward",
    )(qkv, ctx, dctx, lse, seg, x, gh1, g, grad, out)


def bwd_plain_kernel(qkv, ctx, dctx, lse, seg, x, gh1, g, da, gx, qsum, *s):
    bwd_core(qkv, ctx, dctx, lse, seg, x, gh1, g, da, gx, qsum, s, [])


def bwd_plain(qkv, ctx, dctx, lse, seg, x, gh1, g):
    groups, length, width = qkv.shape
    return pl.pallas_call(
        bwd_plain_kernel,
        in_specs=[ANY] * 3 + [VMEM] * 2 + [ANY] * 3,
        out_specs=[ANY, ANY, VMEM],
        out_shape=bwd_shapes(groups, width, x.shape),
        scratch_shapes=bwd_scratch(groups, length, width, x.shape),
        compiler_params=params(),
        name="attention_backward",
    )(qkv, ctx, dctx, lse, seg, x, gh1, g)


def end_vectors(sums, qsum_v, tab_v):
    groups = qsum_v.shape[0]
    tab_v[...] = jnp.zeros_like(tab_v)
    for t in range(groups):
        tab_v[t : t + 1, :] = qsum_v[t][:1]
    parts = tab_v[...].T
    for k in range(sums.shape[0]):
        tab_v[k : k + 1, :] = jnp.sum(sums[k], axis=0, keepdims=True)
    table = tab_v[...].T
    q, v = [], []
    for t in range(groups):
        col = parts[:, t : t + 1]
        q += [col[:LANES], col[3 * LANES : 3 * LANES + HD]]
        v += [col[2 * LANES : 3 * LANES], col[5 * LANES : 5 * LANES + HD]]
    lanes = lane_ids(table.shape)
    table = jnp.where(lanes == 6, jnp.concatenate(q, axis=0), table)
    table = jnp.where(lanes == 7, jnp.concatenate(v, axis=0), table)
    return table


def sum_comm_kernel(da, vt, gx, own, vec_own, gx_rows, total, vtot, r0, r1, r2, r3, r4, r5, r6, r7, r8, r9, send, recv, loc):
    place = Place()
    enter(place)
    copies = Copies(send, recv, loc)
    third = own.shape[0] // 3
    parts = []
    for i, order in enumerate((Q_X, Q_Y, Q_Z)):
        rows = pl.ds(i * third, third)
        parts.append(ReducePart(place, copies, da, total, (r0, r1, r2, r3, r4), own, order[::-1], rows))
    rows = pl.ds(0, vec_own.shape[0])
    parts.append(ReducePart(place, copies, vt, vtot, (r5, r6, r7, r8, r9), vec_own, P_Y[::-1], rows, FEATURES))
    for part in parts:
        part.begin()
    moved = start_rows(place, copies, gx, gx_rows)
    for stage in range(5):
        for part in parts:
            part.advance()
    wait_all(moved)


def sum_comm(da, vt, gx):
    n, width = da.shape[-2:]
    fine = vt.shape[-2]
    return pl.pallas_call(
        sum_comm_kernel,
        in_specs=[ANY] * 3,
        out_specs=[VMEM, VMEM, ANY],
        out_shape=[
            jax.ShapeDtypeStruct((n, width), F32),
            jax.ShapeDtypeStruct((fine, LANES), F32),
            jax.ShapeDtypeStruct(gx.shape, BF),
        ],
        scratch_shapes=[
            pltpu.VMEM((2,) * 4 + (n, width), BF),
            pltpu.VMEM((2,) * 4 + (fine, LANES), F32),
            *arrivals(n, width, BF),
            *arrivals(fine, LANES, F32),
            *sems(40),
            pltpu.SemaphoreType.DMA((10,)),
        ],
        compiler_params=params(2),
        name="weight_sums",
    )(da, vt, gx)


def vector_kernel(sums, qsum, vt, tab_v):
    vt[...] = end_vectors(sums, qsum, tab_v)


def vector_table(sums, qsum):
    width = sums.shape[2]
    return pl.pallas_call(
        vector_kernel,
        in_specs=[VMEM] * 2,
        out_specs=VMEM,
        out_shape=jax.ShapeDtypeStruct((width, LANES), F32),
        scratch_shapes=[pltpu.VMEM((LANES, width), F32)],
        name="vector_table",
    )(sums, qsum)


def pack(qkv_weight, out_weight, in_weight, down_weight):
    q, k, v = qkv_weight[0], qkv_weight[1], qkv_weight[2]
    o = out_weight.T
    a = [q[:, :LANES], k[:, :LANES], v[:, :LANES]]
    a += [q[:, LANES:], o[:, HD:LANES], k[:, LANES:], o[:, :HD], v[:, LANES:], o[:, LANES:]]
    return jnp.stack([jnp.concatenate(a, axis=1), in_weight, down_weight.T])


def unpack(a):
    def cut(i, half):
        start = i * LANES + half * HD
        return a[:, start : start + HD]

    heads = [jnp.concatenate([cut(i, 0), cut(i, 1), cut(3 + i, 0)], axis=1) for i in range(3)]
    out = jnp.concatenate([cut(4, 1), cut(3, 1), cut(5, 1)], axis=1)
    return jnp.stack(heads), out.T


def local(tokens, segments, qkv_weight, out_weight, in_weight, down_weight, vectors, cotangent):
    n_dp, n_t = lax.axis_size("dp"), lax.axis_size("tensor")
    groups, block, width = tokens.shape
    length = groups * block
    n = in_weight.shape[0]
    fine = vectors.shape[1]
    n_v = vectors.shape[0]
    seg = lax.dynamic_slice_in_dim(segments, lax.axis_index("tensor"), 1, 0).reshape(length, 1)
    shard = pack(qkv_weight, out_weight, in_weight, down_weight)
    vec = jnp.pad(vectors.T, ((0, 0), (0, LANES - n_v)))
    kernels = n_dp == 8 and n_t == 4
    bits = (2,) * 5
    if kernels:
        g, x, cot, qkv, ctx, lse, rows = fwd_comm(shard, vec, tokens, cotangent, seg)
    else:
        full = lax.all_gather(shard, ALL, axis=0, tiled=False).reshape(n_dp, n_t, 3, n, width)
        g = full.transpose(2, 1, 0, 3, 4).reshape((3,) + bits + (width // 8, width))
        vt = lax.all_gather(vec, ALL, axis=0, tiled=True)
        x = lax.all_to_all(tokens, "tensor", split_axis=0, concat_axis=0, tiled=True)
        cot = lax.all_to_all(cotangent, "tensor", split_axis=0, concat_axis=0, tiled=True)
        qkv, ctx, lse, rows = fwd_plain(g, x, vt, seg)
    g = g.reshape(3, groups, width, width)
    out, grad, gh1, dctx, sums = middle(g, x, cot, ctx, rows)
    if kernels:
        grad = grad.reshape((2,) + bits + (n, width))
        da, gx, qsum, own, out_rows = bwd_comm(qkv, ctx, dctx, lse, seg, x, gh1, g, grad, out)
        vt = vector_table(sums, qsum).reshape(bits + (fine, LANES))
        own_a, own_v, gx_rows = sum_comm(da.reshape(bits + (n, width)), vt, gx)
    else:
        da, gx, qsum = bwd_plain(qkv, ctx, dctx, lse, seg, x, gh1, g)
        vt = vector_table(sums, qsum)
        every_grad = jnp.concatenate([da.reshape(1, n_t, n_dp, n, width), grad.reshape(2, n_t, n_dp, n, width)])
        every_grad = every_grad.transpose(2, 1, 0, 3, 4).reshape(n_dp * n_t, 3, n, width)
        own = lax.psum_scatter(every_grad, ALL, scatter_dimension=0, tiled=True)[0].astype(F32)
        own_a, own = own[0], own[1:]
        own_v = lax.psum_scatter(vt[:, :n_v], ALL, scatter_dimension=0, tiled=True)
        out_rows = lax.all_to_all(out, "tensor", split_axis=0, concat_axis=0, tiled=True)
        gx_rows = lax.all_to_all(gx, "tensor", split_axis=0, concat_axis=0, tiled=True)
    d_qkv, d_out = unpack(own_a)
    return out_rows, gx_rows, d_qkv, d_out, own[0], own[1].T, own_v[:, :n_v].T


def solution(mesh):
    rows = P("dp", "tensor", None)
    weights = (P(None, "dp", "tensor"), P("tensor", "dp"), P("dp", "tensor"), P("tensor", "dp"), P(None, ("dp", "tensor")))
    in_specs = (rows, P("dp", None), *weights, rows)
    out_specs = (rows, rows, *weights)
    return jax.shard_map(local, mesh=mesh, in_specs=in_specs, out_specs=out_specs, check_vma=False)
```

```python
import functools

import jax
import jax.numpy as jnp
from jax import lax
from jax.experimental import pallas as pl
from jax.experimental.pallas import tpu as pltpu
from jax.sharding import PartitionSpec as P

HD = 64
LANES = 128
EPS = 1e-05
MASKED = -1e30
SEGS = 32
TOP = 35
LOG2E = 1.4426950408889634
QSCALE = LOG2E * HD**-0.5
BF = jnp.bfloat16
F32 = jnp.float32
ALL = ("dp", "tensor")
MESH = pl.DeviceIdType.MESH
ANY = pl.BlockSpec(memory_space=pl.ANY)
VMEM = pl.BlockSpec(memory_space=pltpu.VMEM)
NT = (((1,), (1,)), ((), ()))
NN = (((1,), (0,)), ((), ()))
TN = (((0,), (0,)), ((), ()))
SLOTS = ((0, (0, 1)), (1, (2,)))


def mm(a, b, dims=NN):
    return lax.dot_general(a, b, dims, preferred_element_type=F32)


def lane_ids(shape):
    return lax.broadcasted_iota(jnp.int32, shape, 1)


def low_half(shape):
    return lane_ids(shape) < HD


def swap_halves(value):
    return pltpu.roll(value, HD, 1)


def tile(ref, t, i, rows=slice(None)):
    return ref[t, rows, i * LANES : (i + 1) * LANES]


def flat(value):
    return value.reshape(-1, value.shape[-1])


def at_tick(step, ticks):
    for when, work in ticks:
        pl.when(step == when)(functools.partial(work))


def group_biases(vt):
    length = vt.shape[0]
    groups = length // (3 * HD)
    lanes = lane_ids((length, LANES))
    q, v = vt[:, 6:7], vt[:, 7:8]
    zero = jnp.zeros((LANES, 1), F32)
    out = jnp.zeros((length, LANES), F32)
    for t in range(groups):
        a, b, c = 3 * HD * t, 3 * HD * t + LANES, 3 * HD * (t + 1)
        column = jnp.concatenate([q[a:b], zero, v[a:b], q[b:c], zero[:HD], zero, v[b:c], zero[:HD]], axis=0)
        out = jnp.where(lanes == t, column, out)
    return out.T


def fwd_setup(vt_v, seg, vec_rows, bias_v, oh_v, km_v):
    vt = flat(vt_v[...])
    vec_rows[...] = vt.T[: vec_rows.shape[0]]
    biases = group_biases(vt)
    for t in range(bias_v.shape[0]):
        bias_v[t] = biases[t : t + 1]
    place = lane_ids(oh_v.shape) % HD
    same = seg[...] == place
    oh_v[...] = jnp.where(same, 1.0, 0.0).astype(BF)
    km_v[...] = key_marks(seg, km_v.shape)


def key_marks(seg, shape):
    place = lane_ids(shape) % HD
    marks = jnp.where(place < SEGS, jnp.where(seg[...] == place, 0.0, MASKED), 1.0)
    return jnp.where(place < TOP, marks, 0.0).astype(BF)


def fwd_group(t, x_v, a_v, bias_v, km_v, qkv_v, ka_v, va_v):
    x = flat(x_v[...])
    w = flat(a_v[...])
    low = low_half((x.shape[0], LANES))
    for i in range(6):
        cols = slice(i * LANES, (i + 1) * LANES)
        out = mm(x, w[:, cols]) + bias_v[t, :, cols]
        if i % 3 == 0:
            out = out * QSCALE
        out = out.astype(BF)
        qkv_v[t, :, cols] = out
        one = jnp.ones_like(out)
        if i == 1:
            ka_v[0] = jnp.where(low, out, km_v[...])
            ka_v[1] = jnp.where(low, km_v[...], out)
        if i == 2:
            va_v[0] = jnp.where(low, out, one)
            va_v[1] = jnp.where(low, one, out)
        if i == 4:
            ka_v[2] = jnp.where(low, out, km_v[...])
        if i == 5:
            va_v[2] = jnp.where(low, out, one)


def fwd_block(t, rows, block, qkv_v, ka_v, va_v, oh_v, ctx_v, lse_ref):
    shape = (block, LANES)
    low = low_half(shape)
    lanes = lane_ids(shape)
    marks = oh_v[rows, :]
    lse = lse_ref[rows, :]
    parts = []
    for h in range(3):
        q = tile(qkv_v, t, 0 if h < 2 else 3, rows)
        q = jnp.where(low, marks, q) if h == 1 else jnp.where(low, q, marks)
        s = mm(q, ka_v[h], NT)
        top = jnp.max(s, axis=1, keepdims=True)
        w = jnp.exp2(s - top).astype(BF)
        o = mm(w, va_v[h])
        total = o[:, HD : HD + 1] if h != 1 else o[:, 0:1]
        lse = jnp.where(lanes == 3 * t + h, top + jnp.log2(total), lse)
        parts.append(o)
    lse_ref[rows, :] = lse
    sums = swap_halves(jnp.where(low, parts[1], parts[0]))
    pair = jnp.where(low, parts[0], parts[1]) / sums
    last = parts[2] / swap_halves(parts[2])
    zero = jnp.zeros(shape, F32)
    tiles = (pair, swap_halves(pair), swap_halves(last))
    for i, value in enumerate(tiles):
        ctx_v[t, rows, i * LANES : (i + 1) * LANES] = jnp.where(low, zero, value).astype(BF)


def spread(base, value, lanes):
    hi = value.astype(BF).astype(F32)
    rest = value - hi
    mid = rest.astype(BF).astype(F32)
    low = rest - mid
    place = lanes % HD
    out = jnp.where(place == SEGS, hi, jnp.where(place == SEGS + 1, mid, jnp.where(place == SEGS + 2, low, 0.0)))
    return jnp.where(place < SEGS, base, out.astype(BF))


def bwd_group(t, qkv, ctx, dctx, lse, oh_v, km_v, qa_v, ka_v, va_v, da_v, kt_v, dqt_v):
    length = oh_v.shape[0]
    shape = (length, LANES)
    low = low_half(shape)
    lanes = lane_ids(shape)
    oh, km = oh_v[...], km_v[...]
    ones = jnp.where((lanes % HD >= SEGS) & (lanes % HD < TOP), 1.0, 0.0).astype(BF)

    def cols(ref, i):
        return ref[:, i * LANES : (i + 1) * LANES]

    q, k, v = cols(qkv, 0), cols(qkv, 1), cols(qkv, 2)
    q2, k2, v2 = cols(qkv, 3), cols(qkv, 4), cols(qkv, 5)
    c_pair = jnp.where(low, swap_halves(cols(ctx, 1)), cols(ctx, 0))
    d_pair = jnp.where(low, swap_halves(cols(dctx, 1)), cols(dctx, 0))
    c_last = swap_halves(cols(ctx, 2))
    d_last = swap_halves(cols(dctx, 2))
    prod = c_pair.astype(F32) * d_pair.astype(F32)
    prod2 = c_last.astype(F32) * d_last.astype(F32)
    lse_all = lse[...]
    zero = jnp.zeros_like(prod)
    for h in range(3):
        mine = low if h != 1 else jnp.logical_not(low)
        delta = jnp.sum(jnp.where(mine, prod2 if h == 2 else prod, zero), axis=1, keepdims=True)
        top = jnp.sum(jnp.where(lanes == 3 * t + h, lse_all, zero), axis=1, keepdims=True)
        qa_v[h] = jnp.where(mine, q2 if h == 2 else q, spread(oh, -top, lanes))
        da_v[h] = jnp.where(mine, d_last if h == 2 else d_pair, spread(jnp.zeros_like(oh), -delta, lanes))
        ka_v[h] = jnp.where(mine, k2 if h == 2 else k, km)
        va_v[h] = jnp.where(mine, v2 if h == 2 else v, ones)
    kt_v[0] = k.T
    kt_v[1] = k2.T
    dqt_v[...] = jnp.zeros_like(dqt_v)


def bwd_block(rows, block, qa_v, ka_v, va_v, da_v, kt_v, dqt_v, out):
    low = low_half((block, LANES))
    dk, dv = [], []
    for h in range(3):
        s = mm(ka_v[h, rows, :], qa_v[h], NT)
        p = jnp.exp2(s)
        dv.append(mm(p.astype(BF), da_v[h]))
        dp = mm(va_v[h, rows, :], da_v[h], NT)
        ds = (p * dp).astype(BF)
        dk.append(mm(ds, qa_v[h]) * (1.0 / LOG2E))
        slot, half = h // 2, slice((h % 2) * HD, (h % 2 + 1) * HD)
        dqt_v[slot, half, :] += mm(kt_v[slot, half, rows], ds)
    zero = jnp.zeros((block, LANES), F32)
    tiles = {
        1: jnp.where(low, dk[0], dk[1]),
        2: jnp.where(low, dv[0], dv[1]),
        4: jnp.where(low, dk[2], zero),
        5: jnp.where(low, dv[2], zero),
    }
    for i, value in tiles.items():
        out[rows, i * LANES : (i + 1) * LANES] = value.astype(BF)


def bwd_finish(dqt_v, out):
    scale = HD**-0.5
    low = low_half((out.shape[0], LANES))
    out[:, 0:LANES] = (dqt_v[0].T * scale).astype(BF)
    last = dqt_v[1].T * scale
    out[:, 3 * LANES : 4 * LANES] = jnp.where(low, last, jnp.zeros_like(last)).astype(BF)


def normalize(values, gain_row, shift_row):
    average = jnp.mean(values, axis=-1, keepdims=True)
    centered = values - average
    variance = jnp.mean(centered * centered, axis=-1, keepdims=True)
    inverse = lax.rsqrt(variance + EPS)
    unit = centered * inverse
    return unit * gain_row + shift_row, unit, inverse


def normalize_back(upstream, unit, inverse, gain_row):
    d_unit = upstream * gain_row
    first = jnp.mean(d_unit, axis=-1, keepdims=True)
    second = jnp.mean(d_unit * unit, axis=-1, keepdims=True)
    return inverse * (d_unit - first - unit * second)


def eighths(value):
    return jnp.sum(value.reshape(-1, 8, value.shape[-1]), axis=0)


def gelu_both(x):
    a = jnp.abs(x)
    tail = jnp.exp2(x * x * (-0.5 * LOG2E))
    t = 1.0 / (1.0 + (0.3275911 * 0.5**0.5) * a)
    poly = ((((1.061405429 * t - 1.453152027) * t + 1.421413741) * t - 0.284496736) * t + 0.254829592) * t
    rest = 0.5 * poly * tail
    cdf = jnp.where(x < 0, rest, 1.0 - rest)
    return x * cdf, cdf + x * tail * 0.3989422804014327


def mid_rows(i, block, refs, late):
    (x_v, cot_v, ctx_v, ao_v, in_v, dn_v, vec, act_v, dact_v, dpre_v, y1_v, g2_v, out_v, gh1_v, dctx_v, sums_v) = refs
    rows = pl.ds(pl.multiple_of(i * block, block), block)
    groups = in_v.shape[0]

    def row(k):
        return vec[k : k + 1, :]

    def note(k, value):
        sums_v[k] += eighths(value)

    attn = mm(ctx_v[0, rows, :], ao_v[0], NT)
    for t in range(1, groups):
        attn = attn + mm(ctx_v[t, rows, :], ao_v[t], NT)
    h1 = x_v[i].astype(F32) + attn + row(4)
    y1, u1, r1 = normalize(h1, row(0), row(1))
    y1_low = y1.astype(BF)
    y1_v[rows, :] = y1_low
    ffn = row(5) + y1
    pl.when(i == 0)(lambda: wait_all(late))
    for t in range(groups):
        pre = mm(y1_low, in_v[t]) + row(8 + t)
        act, slope = gelu_both(pre)
        act = act.astype(BF)
        act_v[t, rows, :] = act
        dact_v[t] = slope.astype(BF)
        ffn = ffn + mm(act, dn_v[t], NT)
    out, u2, r2 = normalize(ffn, row(2), row(3))
    out_v[i] = out.astype(BF)
    up = cot_v[i].astype(F32)
    g_h2 = normalize_back(up, u2, r2, row(2))
    note(2, up * u2)
    note(3, up)
    note(5, g_h2)
    g2 = g_h2.astype(BF)
    g2_v[rows, :] = g2
    g_y1 = g_h2
    for t in range(groups):
        dpre = (mm(g2, dn_v[t]) * dact_v[t].astype(F32)).astype(BF)
        dpre_v[t, rows, :] = dpre
        note(8 + t, dpre.astype(F32))
        g_y1 = g_y1 + mm(dpre, in_v[t], NT)
    note(0, g_y1 * u1)
    note(1, g_y1)
    g_h1 = normalize_back(g_y1, u1, r1, row(0))
    note(4, g_h1)
    gh1_v[i] = g_h1
    g1 = g_h1.astype(BF)
    for t in range(groups):
        dctx_v[t, rows, :] = mm(g1, ao_v[t]).astype(BF)

STEP = {"z2": 4, "z1": 2, "y": 1, "x": 2, "c": 1}
BLOCKS = ("x", "c", "z2", "z1", "y")
FEATURES = ("z2", "z1", "y", "x", "c")
P_Y = ("z2", "z1", "x", "y")
P_Z = ("z2", "x", "y", "z1")
Q_Y = ("z2", "x", "z1", "y")
Q_Z = ("z2", "x", "y", "z1")
P_X = ("z2", "y", "z1", "x")
Q_X = ("x", "z2", "z1", "y")


class Place:
    def __init__(self):
        self.d = lax.axis_index("dp")
        self.t = lax.axis_index("tensor")
        self.bit = {
            "x": self.t // 2,
            "c": self.t % 2,
            "z2": self.d // 4,
            "z1": (self.d // 2) % 2,
            "y": self.d % 2,
        }

    def flip(self, dim):
        return 1 - self.bit[dim]

    def peer(self, dim):
        move = STEP[dim] * (1 - 2 * self.bit[dim])
        if dim in ("x", "c"):
            return (self.d, self.t + move)
        return (self.d + move, self.t)

    def row_peer(self, k):
        t = self.t
        if k in (1, 3):
            t = t + (1 - 2 * self.bit["c"])
        if k in (2, 3):
            t = t + 2 * (1 - 2 * self.bit["x"])
        return t

    def index(self, dims, **chosen):
        return tuple(chosen.get(dim, self.bit[dim]) for dim in dims)


def enter(place):
    bar = pltpu.get_barrier_semaphore()
    peers = [place.peer(dim) for dim in BLOCKS] + [(place.d, place.row_peer(3))]
    for peer in peers:
        pl.semaphore_signal(bar, inc=1, device_id=peer, device_id_type=MESH)
    pl.semaphore_wait(bar, len(peers))


class Copies:
    def __init__(self, send, recv, local):
        self.send, self.recv, self.local = send, recv, local
        self.count = self.locals = 0

    def remote(self, ends):
        i = self.count
        self.count += 1

        def copy():
            src, dst, peer = ends()
            return pltpu.make_async_remote_copy(
                src_ref=src,
                dst_ref=dst,
                send_sem=self.send.at[i],
                recv_sem=self.recv.at[i],
                device_id=peer,
                device_id_type=MESH,
            )

        copy().start()
        return lambda: copy().wait()

    def here(self, ends):
        i = self.locals
        self.locals += 1

        def copy():
            src, dst = ends()
            return pltpu.make_async_copy(src, dst, self.local.at[i])

        copy().start()
        return lambda: copy().wait()


ALLBITS = slice(None)


class GatherPart:
    def __init__(self, place, copies, own, full, order, rows, dims=BLOCKS):
        self.place, self.copies, self.own, self.full, self.order = place, copies, own, full, order
        self.rows, self.dims = rows, dims
        self.stage = 0
        self.side = []

    def at(self, **chosen):
        return self.full.at[self.place.index(self.dims, **chosen) + (self.rows,)]

    def begin(self):
        p, c = self.place, self.copies
        self.current = c.remote(lambda: (self.own.at[self.rows], self.at(), p.peer(self.order[0])))
        self.side.append(c.remote(lambda: (self.own.at[self.rows], self.at(), p.peer("c"))))
        self.keep = c.here(lambda: (self.own.at[self.rows], self.at()))

    def held(self, s):
        return self.at(**{dim: ALLBITS for dim in self.order[:s]})

    def arrived(self, s):
        dim = self.order[s]
        return self.at(**{other: ALLBITS for other in self.order[:s]}, **{dim: self.place.flip(dim)})

    def advance(self):
        p, c, s = self.place, self.copies, self.stage
        self.current()
        if s == 0:
            self.keep()
        if s + 1 < len(self.order):
            self.current = c.remote(lambda: (self.held(s + 1), self.held(s + 1), p.peer(self.order[s + 1])))
        self.side.append(c.remote(lambda: (self.arrived(s), self.arrived(s), p.peer("c"))))
        self.stage = s + 1

    def finish(self):
        wait_all(self.side)


def every(count, work):
    if count == 0:
        work(())
        return

    def body(i, carry):
        work(tuple((i // 2**j) % 2 for j in reversed(range(count))))
        return carry

    lax.fori_loop(0, 2**count, body, 0)


def blockwise(ref):
    return ref.reshape(2 ** (len(ref.shape) - 2), *ref.shape[-2:])


def spot(bits):
    place = 0
    for bit in bits:
        place = 2 * place + bit
    return place


class ReducePart:
    def __init__(self, place, copies, src, total, arrive, out, order, rows, dims=BLOCKS, paired=False):
        self.paired = paired
        self.place, self.copies, self.src, self.total, self.arrive = place, copies, src, total, arrive
        self.out, self.order, self.rows, self.dims = out, order, rows, dims
        self.inner = tuple(dim for dim in dims if dim != "c")
        self.kept = self.inner
        if total is None:
            self.total, self.kept = src, dims
        self.stage = 0

    def source(self, **chosen):
        return self.src.at[self.place.index(self.dims, **chosen) + (self.rows,)]

    def sums(self, **chosen):
        return self.total.at[self.place.index(self.kept, **chosen) + (self.rows,)]

    def half(self, bit):
        p, first = self.place, self.order[0]

        def ends():
            free = {dim: ALLBITS for dim in self.inner}
            free[first] = bit()
            dst = self.arrive[0].at[p.index(self.inner, **free) + (self.rows,)]
            return self.source(c=p.flip("c"), **free), dst, p.peer("c")

        return self.copies.remote(ends)

    def begin(self):
        p, first = self.place, self.order[0]
        if self.paired:
            self.keep = self.copies.here(lambda: (self.src.at[(ALLBITS,) * 4 + (self.rows,)], self.total.at[(ALLBITS,) * 4 + (self.rows,)]))
            return
        self.side = [self.half(lambda: p.flip(first)), self.half(lambda: p.bit[first])]
        if self.kept is self.inner:
            free = {dim: ALLBITS for dim in self.inner}
            self.keep = self.copies.here(lambda: (self.source(**free), self.sums(**free)))

    def add(self, fixed, bit):
        s = self.stage
        left = [dim for dim in self.inner if dim not in self.order[:s]] if s else list(self.inner)
        loose = [dim for dim in left if dim != fixed]

        total, arrive = blockwise(self.total), blockwise(self.arrive[s])

        def work(bits):
            chosen = dict(zip(loose, bits))
            chosen[fixed] = bit
            mine = spot(self.place.index(self.kept, **chosen))
            there = spot(tuple(chosen[dim] for dim in left))
            both = total[mine, self.rows, :].astype(F32) + arrive[there, self.rows, :].astype(F32)
            total[mine, self.rows, :] = both.astype(total.dtype)

        every(len(loose), work)

    def send(self):
        p, s = self.place, self.stage
        dim = self.order[s]
        free = {other: ALLBITS for other in self.order[s + 1 :]}

        def ends():
            src = self.sums(**free, **{dim: p.flip(dim)})
            dst = self.arrive[s + 1].at[(ALLBITS,) * len(free) + (self.rows,)]
            return src, dst, p.peer(dim)

        return self.copies.remote(ends)

    def advance(self):
        p, s = self.place, self.stage
        if s == 0:
            if self.kept is self.inner:
                self.keep()
            if not self.paired:
                self.side[0]()
        else:
            self.current()
        if s < len(self.order):
            dim = self.order[s]
            if s == 0 and self.paired:
                self.current = self.send()
                self.stage = 1
                return
            self.add(dim, p.flip(dim))
            self.current = self.send()
            if s == 0:
                self.side[1]()
            self.add(dim, p.bit[dim])
        else:
            mine = spot(self.place.index(self.kept))
            self.out[self.rows, :] = blockwise(self.total)[mine, self.rows, :].astype(F32) + self.arrive[s][self.rows, :].astype(F32)
        self.stage = s + 1


def arrivals(rows, cols, dtype):
    return [pltpu.VMEM((2,) * n + (rows, cols), dtype) for n in (4, 3, 2, 1, 0)]


def start_row(place, copies, src, dst, k):
    def ends():
        to = place.row_peer(k)
        return src.at[to], dst.at[place.t], (place.d, to)

    return copies.remote(ends)


def keep_row(place, copies, src, dst):
    return copies.here(lambda: (src.at[place.t], dst.at[place.t]))


def start_rows(place, copies, src, dst):
    return [start_row(place, copies, src, dst, k) for k in (2, 3, 1)] + [keep_row(place, copies, src, dst)]


def wait_all(waits):
    for wait in waits:
        wait()


def params(collective=None):
    more = {} if collective is None else {"collective_id": collective, "has_side_effects": True}
    return pltpu.CompilerParams(vmem_limit_bytes=60 << 20, **more)


def sems(count):
    return [pltpu.SemaphoreType.DMA((count,))] * 2


def fwd_core(group_ref, x_v, vt_v, seg, qkv, ctx, xt, lse, vec_rows, s, ticks):
    (a_v, bias_v, oh_v, km_v, qkv_v, ka_v, va_v, ctx_v, xt_v, a_sem, out_sem) = s
    groups, length = qkv.shape[:2]
    block = 256
    blocks = length // block

    def load(t):
        return pltpu.make_async_copy(group_ref(t), a_v.at[t % 2], a_sem.at[t % 2])

    load(0).start()
    fwd_setup(vt_v, seg, vec_rows, bias_v, oh_v, km_v)
    lse[...] = jnp.zeros_like(lse)

    def step(i, carry):
        t, b = i // blocks, i % blocks
        at_tick(i, ticks)

        @pl.when(b == 0)
        def _():
            load(t).wait()

            @pl.when(t + 1 < groups)
            def _():
                load(t + 1).start()

            fwd_group(t, x_v, a_v.at[t % 2], bias_v, km_v, qkv_v, ka_v, va_v)
            pltpu.make_async_copy(qkv_v.at[t], qkv.at[t], out_sem.at[0, t]).start()

        rows = pl.ds(pl.multiple_of(b * block, block), block)
        fwd_block(t, rows, block, qkv_v, ka_v, va_v, oh_v, ctx_v, lse)

        @pl.when(b == blocks - 1)
        def _():
            pltpu.make_async_copy(ctx_v.at[t], ctx.at[t], out_sem.at[1, t]).start()

        return carry

    lax.fori_loop(0, groups * blocks, step, 0)
    xt_v[...] = flat(x_v[...]).T
    turned = pltpu.make_async_copy(xt_v, xt, a_sem.at[0])
    turned.start()
    turned.wait()
    for t in range(groups):
        pltpu.make_async_copy(qkv_v.at[t], qkv.at[t], out_sem.at[0, t]).wait()
        pltpu.make_async_copy(ctx_v.at[t], ctx.at[t], out_sem.at[1, t]).wait()


def fwd_scratch(groups, length, width):
    return [
        pltpu.VMEM((2, 2, 2, 2, width // 8, width), BF),
        pltpu.VMEM((groups, 1, width), F32),
        pltpu.VMEM((length, LANES), BF),
        pltpu.VMEM((length, LANES), BF),
        pltpu.VMEM((groups, length, width), BF),
        pltpu.VMEM((3, length, LANES), BF),
        pltpu.VMEM((3, length, LANES), BF),
        pltpu.VMEM((groups, length, 3 * LANES), BF),
        pltpu.VMEM((width, length), BF),
        pltpu.SemaphoreType.DMA((2,)),
        pltpu.SemaphoreType.DMA((2, groups)),
    ]


def fwd_shapes(groups, length, width):
    return [
        jax.ShapeDtypeStruct((groups, length, width), BF),
        jax.ShapeDtypeStruct((groups, length, 3 * LANES), BF),
        jax.ShapeDtypeStruct((width, length), BF),
        jax.ShapeDtypeStruct((length, LANES), F32),
        jax.ShapeDtypeStruct((16, width), F32),
    ]


def fwd_comm_kernel(shard, vec, tok, cot, seg, g, x, co, qkv, ctx, xt, lse, vec_rows, x_v, vt_v, send, recv, loc, *s):
    place = Place()
    enter(place)
    copies = Copies(send, recv, loc)
    mk = functools.partial(GatherPart, place, copies)
    n = shard.shape[1]
    third, half = n // 3, n // 2
    first = [mk(vec, vt_v, Q_Z, pl.ds(0, vec.shape[0]), FEATURES)]
    first += [mk(shard.at[0], g.at[0], order, pl.ds(i * third, third)) for i, order in enumerate((Q_Y, Q_Z, P_X))]
    later = [mk(shard.at[1], g.at[1], order, pl.ds(i * half, half)) for i, order in enumerate((Q_Y, Q_Z))]
    later += [mk(shard.at[2], g.at[2], order, pl.ds(i * third, third)) for i, order in enumerate((Q_Y, Q_Z, P_X))]
    moved = []

    def advance():
        for part in later:
            part.advance()

    def cot_rows():
        advance()
        moved.extend(start_rows(place, copies, cot, co))

    for part in first:
        part.begin()
    rows = [start_row(place, copies, tok, x_v, k) for k in (2, 1)] + [keep_row(place, copies, tok, x_v)]
    for stage in range(4):
        for part in first:
            part.advance()
        if stage == 0:
            rows.append(start_row(place, copies, tok, x_v, 3))
        if stage == 2:
            for part in later:
                part.begin()
    for part in first:
        part.finish()
    wait_all(rows)
    keep = copies.here(lambda: (x_v, x))
    ticks = [(1, cot_rows), (4, advance), (8, advance)]
    fwd_core(lambda t: g.at[0, t // 2, t % 2], x_v, vt_v, seg, qkv, ctx, xt, lse, vec_rows, s, ticks)
    advance()
    for part in later:
        part.finish()
    wait_all(moved)
    keep()


def fwd_comm(shard, vec, tok, cot, seg):
    groups, block, width = tok.shape
    length = groups * block
    bits = (2,) * 5
    return pl.pallas_call(
        fwd_comm_kernel,
        in_specs=[ANY] * 4 + [VMEM],
        out_specs=[ANY] * 6 + [VMEM] * 2,
        out_shape=[
            jax.ShapeDtypeStruct((3,) + bits + shard.shape[1:], BF),
            jax.ShapeDtypeStruct(tok.shape, BF),
            jax.ShapeDtypeStruct(cot.shape, BF),
        ]
        + fwd_shapes(groups, length, width),
        scratch_shapes=[
            pltpu.VMEM(tok.shape, BF),
            pltpu.VMEM(bits + vec.shape, F32),
            *sems(96),
            pltpu.SemaphoreType.DMA((20,)),
        ]
        + fwd_scratch(groups, length, width),
        compiler_params=params(0),
        name="attention_forward",
    )(shard, vec, tok, cot, seg)


def fwd_plain_kernel(g, x, vt, seg, qkv, ctx, xt, lse, vec_rows, sem, x_v, *s):
    copy = pltpu.make_async_copy(x, x_v, sem)
    copy.start()
    copy.wait()
    fwd_core(lambda t: g.at[0, t // 2, t % 2], x_v, vt, seg, qkv, ctx, xt, lse, vec_rows, s, [])


def fwd_plain(g, x, vt, seg):
    groups, block, width = x.shape
    length = groups * block
    return pl.pallas_call(
        fwd_plain_kernel,
        in_specs=[ANY, ANY, VMEM, VMEM],
        out_specs=[ANY] * 3 + [VMEM] * 2,
        out_shape=fwd_shapes(groups, length, width),
        scratch_shapes=[pltpu.SemaphoreType.DMA, pltpu.VMEM(x.shape, BF)] + fwd_scratch(groups, length, width),
        compiler_params=params(),
        name="attention_forward",
    )(g, x, vt, seg)


def mid_kernel(g, x, cot, ctx, vec, out, grad, gh1, dctx, sums, x_v, cot_v, ctx_v, ao_v, in_v, dn_v, act_v, dact_v, dpre_v, y1_v, g2_v, out_v, gh1_v, dctx_v, t_v, sem, out_sem):
    groups, length = ctx.shape[:2]
    width = x.shape[2]
    half = width // 2
    blocks, block = x.shape[:2]

    def copy(src, dst, i):
        return pltpu.make_async_copy(src, dst, sem.at[i])

    loads = [copy(x, x_v, 0), copy(ctx, ctx_v, 1), copy(g.at[0, :, :, half:], ao_v, 2)]
    loads += [copy(g.at[1], in_v, 3), copy(g.at[2], dn_v, 4), copy(cot, cot_v, 5)]
    for load in loads:
        load.start()
    sums[...] = jnp.zeros_like(sums)
    for load in loads[:3]:
        load.wait()
    refs = (x_v, cot_v, ctx_v, ao_v, in_v, dn_v, vec, act_v, dact_v, dpre_v, y1_v, g2_v, out_v, gh1_v, dctx_v, sums)

    def step(i, carry):
        mid_rows(i, block, refs, [load.wait for load in loads[3:]])
        pltpu.make_async_copy(out_v.at[i], out.at[i], out_sem.at[0, i]).start()
        pltpu.make_async_copy(gh1_v.at[i], gh1.at[i], out_sem.at[1, i]).start()
        return carry

    lax.fori_loop(0, blocks, step, 0)
    send = copy(dctx_v, dctx, 0)
    send.start()
    t_v[...] = y1_v[...].T

    def in_step(t, carry):
        in_v[t] = mm(t_v[...], dpre_v[t]).astype(BF)
        pltpu.make_async_copy(in_v.at[t], grad.at[0, t], out_sem.at[2, t]).start()
        return carry

    lax.fori_loop(0, groups, in_step, 0)
    t_v[...] = g2_v[...].T

    def dn_step(t, carry):
        dn_v[t] = mm(t_v[...], act_v[t]).astype(BF)
        pltpu.make_async_copy(dn_v.at[t], grad.at[1, t], out_sem.at[3, t]).start()
        return carry

    lax.fori_loop(0, groups, dn_step, 0)
    send.wait()
    for i in range(blocks):
        pltpu.make_async_copy(out_v.at[i], out.at[i], out_sem.at[0, i]).wait()
        pltpu.make_async_copy(gh1_v.at[i], gh1.at[i], out_sem.at[1, i]).wait()
    for t in range(groups):
        pltpu.make_async_copy(in_v.at[t], grad.at[0, t], out_sem.at[2, t]).wait()
        pltpu.make_async_copy(dn_v.at[t], grad.at[1, t], out_sem.at[3, t]).wait()


def middle(g, x, cot, ctx, vec):
    groups, length, _ = ctx.shape
    blocks, block, width = x.shape
    flats = (groups, width, width)
    return pl.pallas_call(
        mid_kernel,
        in_specs=[ANY] * 4 + [VMEM],
        out_specs=[ANY] * 4 + [VMEM],
        out_shape=[
            jax.ShapeDtypeStruct(x.shape, BF),
            jax.ShapeDtypeStruct((2,) + flats, BF),
            jax.ShapeDtypeStruct(x.shape, F32),
            jax.ShapeDtypeStruct(ctx.shape, BF),
            jax.ShapeDtypeStruct((8 + groups, 8, width), F32),
        ],
        scratch_shapes=[
            pltpu.VMEM(x.shape, BF),
            pltpu.VMEM(x.shape, BF),
            pltpu.VMEM(ctx.shape, BF),
            pltpu.VMEM((groups, width, width // 2), BF),
            pltpu.VMEM(flats, BF),
            pltpu.VMEM(flats, BF),
            pltpu.VMEM((groups, length, width), BF),
            pltpu.VMEM((groups, block, width), BF),
            pltpu.VMEM((groups, length, width), BF),
            pltpu.VMEM((length, width), BF),
            pltpu.VMEM((length, width), BF),
            pltpu.VMEM(x.shape, BF),
            pltpu.VMEM(x.shape, F32),
            pltpu.VMEM(ctx.shape, BF),
            pltpu.VMEM((width, length), BF),
            pltpu.SemaphoreType.DMA((6,)),
            pltpu.SemaphoreType.DMA((4, max(groups, blocks))),
        ],
        compiler_params=params(),
        name="feed_forward",
    )(g, x, cot, ctx, vec)


def bwd_core(qkv, ctx, dctx, lse, seg, xt, gh1, g, da, gx, qsum, s, ticks, place=None):
    (qkv_v, ctx_v, dctx_v, a_v, oh_v, km_v, qa_v, ka_v, va_v, da_v, kt_v, dqt_v, dqkv_v, x_v, gx_v, xt_v, gt_v, dw_v, pair_v, in_sem, out_sem, x_sem, pair_sem) = s
    groups, length = qkv.shape[:2]
    block = 256
    blocks = length // block
    half = 3 * LANES

    early = groups if place is None else groups // 2

    def group(i):
        if place is None:
            return i
        core = place.bit["c"]
        return 2 * (i % 2) + core + (1 - i // 2) * (1 - 2 * core)

    def loads(i):
        t, slot = group(i), i % 2
        return [
            pltpu.make_async_copy(qkv.at[t], qkv_v.at[slot], in_sem.at[0, slot]),
            pltpu.make_async_copy(ctx.at[t], ctx_v.at[slot], in_sem.at[1, slot]),
            pltpu.make_async_copy(dctx.at[t], dctx_v.at[slot], in_sem.at[2, slot]),
            pltpu.make_async_copy(g.at[0, t], a_v.at[slot], in_sem.at[3, slot]),
        ]

    def result(i):
        if place is None:
            return pltpu.make_async_copy(dw_v.at[i], da.at[i], out_sem.at[i])
        return pltpu.make_async_copy(dw_v.at[i], da.at[i - early], out_sem.at[i])

    def hand_over(i):
        return pltpu.make_async_remote_copy(
            src_ref=dw_v.at[i],
            dst_ref=pair_v.at[i],
            send_sem=pair_sem.at[0, i],
            recv_sem=pair_sem.at[1, i],
            device_id=place.peer("c"),
            device_id_type=MESH,
        )

    more = [pltpu.make_async_copy(xt, xt_v, x_sem.at[0]), pltpu.make_async_copy(gh1, gx_v, x_sem.at[1])]
    for load in loads(0) + more:
        load.start()
    oh_v[...] = jnp.where(seg[...] == lane_ids(oh_v.shape) % HD, 1.0, 0.0).astype(BF)
    km_v[...] = key_marks(seg, km_v.shape)

    def ready():
        for load in more:
            load.wait()
        gt_v[...] = flat(gx_v[...]).astype(BF).T

    def weights(i, slot, add):
        def chunk(r, inner):
            part = pl.ds(pl.multiple_of(r * block, block), block)
            lead = mm(xt_v[part, :], dqkv_v[:, :half])
            rest = mm(xt_v[part, :], dqkv_v[:, half:]) + mm(gt_v[part, :], ctx_v[slot])
            if add:
                lead = lead + pair_v[i - early, part, :half].astype(F32)
                rest = rest + pair_v[i - early, part, half:].astype(F32)
            dw_v[i, part, :half] = lead.astype(BF)
            dw_v[i, part, half:] = rest.astype(BF)
            return inner

        lax.fori_loop(0, dw_v.shape[1] // block, chunk, 0)

    def rows(b, slot):
        part = pl.ds(pl.multiple_of(b * block, block), block)
        gx_v[b] = gx_v[b] + mm(dqkv_v[part, :], a_v[slot], NT)

    def step(i, carry):
        at, b = i // blocks, i % blocks
        slot = at % 2
        at_tick(i, ticks)
        pl.when(i == 1)(ready)

        @pl.when(b == 0)
        def _():
            for load in loads(at):
                load.wait()

            @pl.when(at + 1 < groups)
            def _():
                for load in loads(at + 1):
                    load.start()

            bwd_group(group(at), qkv_v.at[slot], ctx_v.at[slot], dctx_v.at[slot], lse, oh_v, km_v, qa_v, ka_v, va_v, da_v, kt_v, dqt_v)

        part = pl.ds(pl.multiple_of(b * block, block), block)
        bwd_block(part, block, qa_v, ka_v, va_v, da_v, kt_v, dqt_v, dqkv_v)

        @pl.when(b == blocks - 1)
        def _():
            bwd_finish(dqt_v, dqkv_v)
            qsum[group(at)] = mm(jnp.ones((8, length), BF), dqkv_v[...])
            if place is None:
                weights(at, slot, False)
                result(at).start()
            else:

                @pl.when(at < early)
                def _():
                    weights(at, slot, False)
                    hand_over(at).start()

                @pl.when(at >= early)
                def _():
                    hand_over(at - early).wait()
                    weights(at, slot, True)
                    result(at).start()

            def row_step(r, inner):
                rows(r, slot)
                return inner

            lax.fori_loop(0, blocks, row_step, 0)

        return carry

    lax.fori_loop(0, groups * blocks, step, 0)

    def low_step(r, carry):
        x_v[r] = gx_v[r].astype(BF)
        return carry

    lax.fori_loop(0, blocks, low_step, 0)
    last = pltpu.make_async_copy(x_v, gx, x_sem.at[0])
    last.start()
    for i in range(0 if place is None else early, groups):
        result(i).wait()
    last.wait()


def bwd_scratch(groups, length, width, x):
    half = 3 * LANES
    return [
        pltpu.VMEM((2, length, width), BF),
        pltpu.VMEM((2, length, half), BF),
        pltpu.VMEM((2, length, half), BF),
        pltpu.VMEM((2, width, width), BF),
        pltpu.VMEM((length, LANES), BF),
        pltpu.VMEM((length, LANES), BF),
        pltpu.VMEM((3, length, LANES), BF),
        pltpu.VMEM((3, length, LANES), BF),
        pltpu.VMEM((3, length, LANES), BF),
        pltpu.VMEM((3, length, LANES), BF),
        pltpu.VMEM((2, LANES, length), BF),
        pltpu.VMEM((2, LANES, length), F32),
        pltpu.VMEM((length, width), BF),
        pltpu.VMEM(x, BF),
        pltpu.VMEM(x, F32),
        pltpu.VMEM((width, length), BF),
        pltpu.VMEM((width, length), BF),
        pltpu.VMEM((groups, width, width), BF),
        pltpu.VMEM((groups // 2, width, width), BF),
        pltpu.SemaphoreType.DMA((4, 2)),
        pltpu.SemaphoreType.DMA((groups,)),
        pltpu.SemaphoreType.DMA((2,)),
        pltpu.SemaphoreType.DMA((2, groups // 2)),
    ]


def bwd_shapes(groups, width, x, held):
    return [
        jax.ShapeDtypeStruct((held, width, width), BF),
        jax.ShapeDtypeStruct(x, BF),
        jax.ShapeDtypeStruct((groups, 8, width), F32),
    ]


def bwd_comm_kernel(qkv, ctx, dctx, lse, seg, xt, gh1, g, grad, out, da, gx, qsum, own, out_rows, total, r0, r1, r2, r3, r4, r5, r6, r7, r8, r9, send, recv, loc, *s):
    place = Place()
    enter(place)
    copies = Copies(send, recv, loc)
    half = own.shape[1] // 2
    arrive = ((r0, r1, r2, r3, r4), (r5, r6, r7, r8, r9))
    parts = []
    for w, orders in enumerate(((P_Y, P_Z), (Q_Y, Q_Z))):
        for i, order in enumerate(orders):
            rows = pl.ds(i * half, half)
            parts.append(ReducePart(place, copies, grad.at[w], total.at[w], arrive[w], own.at[w], order[::-1], rows))
    for part in parts:
        part.begin()
    moved = []

    def advance(*which):
        for i in which:
            parts[i].advance()

    def rows():
        moved.extend(start_rows(place, copies, out, out_rows))

    ticks = [
        (2, functools.partial(advance, 0, 1, 2, 3)),
        (3, rows),
        (9, functools.partial(advance, 0, 1, 2, 3)),
        (12, functools.partial(advance, 0, 2)),
        (13, functools.partial(advance, 1, 3)),
        (14, functools.partial(advance, 0, 2)),
        (15, functools.partial(advance, 1, 3)),
    ]
    bwd_core(qkv, ctx, dctx, lse, seg, xt, gh1, g, da, gx, qsum, s, ticks, place)
    advance(0, 1, 2, 3)
    wait_all(moved)


def bwd_comm(qkv, ctx, dctx, lse, seg, xt, gh1, g, grad, out):
    groups, length, width = qkv.shape
    n = grad.shape[6]
    arrive = arrivals(n, width, BF)
    return pl.pallas_call(
        bwd_comm_kernel,
        in_specs=[ANY] * 3 + [VMEM] * 2 + [ANY] * 5,
        out_specs=[ANY, ANY, VMEM, VMEM, ANY],
        out_shape=bwd_shapes(groups, width, gh1.shape, groups // 2)
        + [
            jax.ShapeDtypeStruct((2, n, width), F32),
            jax.ShapeDtypeStruct(out.shape, BF),
        ],
        scratch_shapes=[
            pltpu.VMEM((2, 2, 2, 2, 2, n, width), BF),
            *arrive,
            *arrive,
            *sems(40),
            pltpu.SemaphoreType.DMA((10,)),
        ]
        + bwd_scratch(groups, length, width, gh1.shape),
        compiler_params=params(1),
        name="attention_backward",
    )(qkv, ctx, dctx, lse, seg, xt, gh1, g, grad, out)


def bwd_plain_kernel(qkv, ctx, dctx, lse, seg, xt, gh1, g, da, gx, qsum, *s):
    bwd_core(qkv, ctx, dctx, lse, seg, xt, gh1, g, da, gx, qsum, s, [])


def bwd_plain(qkv, ctx, dctx, lse, seg, xt, gh1, g):
    groups, length, width = qkv.shape
    return pl.pallas_call(
        bwd_plain_kernel,
        in_specs=[ANY] * 3 + [VMEM] * 2 + [ANY] * 3,
        out_specs=[ANY, ANY, VMEM],
        out_shape=bwd_shapes(groups, width, gh1.shape, groups),
        scratch_shapes=bwd_scratch(groups, length, width, gh1.shape),
        compiler_params=params(),
        name="attention_backward",
    )(qkv, ctx, dctx, lse, seg, xt, gh1, g)


def end_vectors(sums, qsum_v, tab_v):
    groups = qsum_v.shape[0]
    tab_v[...] = jnp.zeros_like(tab_v)
    for t in range(groups):
        tab_v[t : t + 1, :] = qsum_v[t][:1]
    parts = tab_v[...].T
    for k in range(sums.shape[0]):
        tab_v[k : k + 1, :] = jnp.sum(sums[k], axis=0, keepdims=True)
    table = tab_v[...].T
    q, v = [], []
    for t in range(groups):
        col = parts[:, t : t + 1]
        q += [col[:LANES], col[3 * LANES : 3 * LANES + HD]]
        v += [col[2 * LANES : 3 * LANES], col[5 * LANES : 5 * LANES + HD]]
    lanes = lane_ids(table.shape)
    table = jnp.where(lanes == 6, jnp.concatenate(q, axis=0), table)
    table = jnp.where(lanes == 7, jnp.concatenate(v, axis=0), table)
    return table


def sum_comm_kernel(da, vt, gx, own, vec_own, gx_rows, total, vtot, r0, r1, r2, r3, r4, r5, r6, r7, r8, send, recv, loc):
    place = Place()
    enter(place)
    copies = Copies(send, recv, loc)
    third = own.shape[0] // 3
    parts = []
    for i, order in enumerate((Q_X, Q_Y, Q_Z)):
        rows = pl.ds(i * third, third)
        parts.append(ReducePart(place, copies, da, total, (r0, r0, r1, r2, r3), own, order[::-1], rows, paired=True))
    rows = pl.ds(0, vec_own.shape[0])
    parts.append(ReducePart(place, copies, vt, vtot, (r4, r5, r6, r7, r8), vec_own, P_Y[::-1], rows, FEATURES))
    for part in parts:
        part.begin()
    moved = start_rows(place, copies, gx, gx_rows)
    for stage in range(5):
        for part in parts:
            part.advance()
    wait_all(moved)


def sum_comm(da, vt, gx):
    n, width = da.shape[-2:]
    fine = vt.shape[-2]
    return pl.pallas_call(
        sum_comm_kernel,
        in_specs=[ANY] * 3,
        out_specs=[VMEM, VMEM, ANY],
        out_shape=[
            jax.ShapeDtypeStruct((n, width), F32),
            jax.ShapeDtypeStruct((fine, LANES), F32),
            jax.ShapeDtypeStruct(gx.shape, BF),
        ],
        scratch_shapes=[
            pltpu.VMEM((2,) * 4 + (n, width), BF),
            pltpu.VMEM((2,) * 4 + (fine, LANES), F32),
            *arrivals(n, width, BF)[1:],
            *arrivals(fine, LANES, F32),
            *sems(40),
            pltpu.SemaphoreType.DMA((10,)),
        ],
        compiler_params=params(2),
        name="weight_sums",
    )(da, vt, gx)


def vector_kernel(sums, qsum, vt, tab_v):
    vt[...] = end_vectors(sums, qsum, tab_v)


def vector_table(sums, qsum):
    width = sums.shape[2]
    return pl.pallas_call(
        vector_kernel,
        in_specs=[VMEM] * 2,
        out_specs=VMEM,
        out_shape=jax.ShapeDtypeStruct((width, LANES), F32),
        scratch_shapes=[pltpu.VMEM((LANES, width), F32)],
        name="vector_table",
    )(sums, qsum)


def pack(qkv_weight, out_weight, in_weight, down_weight):
    q, k, v = qkv_weight[0], qkv_weight[1], qkv_weight[2]
    o = out_weight.T
    a = [q[:, :LANES], k[:, :LANES], v[:, :LANES]]
    a += [q[:, LANES:], o[:, HD:LANES], k[:, LANES:], o[:, :HD], v[:, LANES:], o[:, LANES:]]
    return jnp.stack([jnp.concatenate(a, axis=1), in_weight, down_weight.T])


def unpack(a):
    def cut(i, half):
        start = i * LANES + half * HD
        return a[:, start : start + HD]

    heads = [jnp.concatenate([cut(i, 0), cut(i, 1), cut(3 + i, 0)], axis=1) for i in range(3)]
    out = jnp.concatenate([cut(4, 1), cut(3, 1), cut(5, 1)], axis=1)
    return jnp.stack(heads), out.T


def local(tokens, segments, qkv_weight, out_weight, in_weight, down_weight, vectors, cotangent):
    n_dp, n_t = lax.axis_size("dp"), lax.axis_size("tensor")
    groups, block, width = tokens.shape
    length = groups * block
    n = in_weight.shape[0]
    fine = vectors.shape[1]
    n_v = vectors.shape[0]
    seg = lax.dynamic_slice_in_dim(segments, lax.axis_index("tensor"), 1, 0).reshape(length, 1)
    shard = pack(qkv_weight, out_weight, in_weight, down_weight)
    vec = jnp.pad(vectors.T, ((0, 0), (0, LANES - n_v)))
    kernels = n_dp == 8 and n_t == 4
    bits = (2,) * 5
    if kernels:
        g, x, cot, qkv, ctx, xt, lse, rows = fwd_comm(shard, vec, tokens, cotangent, seg)
    else:
        full = lax.all_gather(shard, ALL, axis=0, tiled=False).reshape(n_dp, n_t, 3, n, width)
        g = full.transpose(2, 1, 0, 3, 4).reshape((3,) + bits + (width // 8, width))
        vt = lax.all_gather(vec, ALL, axis=0, tiled=True)
        x = lax.all_to_all(tokens, "tensor", split_axis=0, concat_axis=0, tiled=True)
        cot = lax.all_to_all(cotangent, "tensor", split_axis=0, concat_axis=0, tiled=True)
        qkv, ctx, xt, lse, rows = fwd_plain(g, x, vt, seg)
    g = g.reshape(3, groups, width, width)
    out, grad, gh1, dctx, sums = middle(g, x, cot, ctx, rows)
    if kernels:
        grad = grad.reshape((2,) + bits + (n, width))
        da, gx, qsum, own, out_rows = bwd_comm(qkv, ctx, dctx, lse, seg, xt, gh1, g, grad, out)
        vt = vector_table(sums, qsum).reshape(bits + (fine, LANES))
        own_a, own_v, gx_rows = sum_comm(da.reshape(bits[1:] + (n, width)), vt, gx)
    else:
        da, gx, qsum = bwd_plain(qkv, ctx, dctx, lse, seg, xt, gh1, g)
        vt = vector_table(sums, qsum)
        every_grad = jnp.concatenate([da.reshape(1, n_t, n_dp, n, width), grad.reshape(2, n_t, n_dp, n, width)])
        every_grad = every_grad.transpose(2, 1, 0, 3, 4).reshape(n_dp * n_t, 3, n, width)
        own = lax.psum_scatter(every_grad, ALL, scatter_dimension=0, tiled=True)[0].astype(F32)
        own_a, own = own[0], own[1:]
        own_v = lax.psum_scatter(vt[:, :n_v], ALL, scatter_dimension=0, tiled=True)
        out_rows = lax.all_to_all(out, "tensor", split_axis=0, concat_axis=0, tiled=True)
        gx_rows = lax.all_to_all(gx, "tensor", split_axis=0, concat_axis=0, tiled=True)
    d_qkv, d_out = unpack(own_a)
    return out_rows, gx_rows, d_qkv, d_out, own[0], own[1].T, own_v[:, :n_v].T


def solution(mesh):
    rows = P("dp", "tensor", None)
    weights = (P(None, "dp", "tensor"), P("tensor", "dp"), P("dp", "tensor"), P("tensor", "dp"), P(None, ("dp", "tensor")))
    in_specs = (rows, P("dp", None), *weights, rows)
    out_specs = (rows, rows, *weights)
    return jax.shard_map(local, mesh=mesh, in_specs=in_specs, out_specs=out_specs, check_vma=False)
```

```python
import functools

import jax
import jax.numpy as jnp
from jax import lax
from jax.experimental import pallas as pl
from jax.experimental.pallas import tpu as pltpu
from jax.sharding import PartitionSpec as P

HD = 64
LANES = 128
EPS = 1e-05
MASKED = -1e30
SEGS = 32
TOP = 35
LOG2E = 1.4426950408889634
QSCALE = LOG2E * HD**-0.5
BF = jnp.bfloat16
F32 = jnp.float32
ALL = ("dp", "tensor")
MESH = pl.DeviceIdType.MESH
ANY = pl.BlockSpec(memory_space=pl.ANY)
VMEM = pl.BlockSpec(memory_space=pltpu.VMEM)
NT = (((1,), (1,)), ((), ()))
NN = (((1,), (0,)), ((), ()))
TN = (((0,), (0,)), ((), ()))
SLOTS = ((0, (0, 1)), (1, (2,)))


def mm(a, b, dims=NN):
    return lax.dot_general(a, b, dims, preferred_element_type=F32)


def lane_ids(shape):
    return lax.broadcasted_iota(jnp.int32, shape, 1)


def low_half(shape):
    return lane_ids(shape) < HD


def swap_halves(value):
    return pltpu.roll(value, HD, 1)


def tile(ref, t, i, rows=slice(None)):
    return ref[t, rows, i * LANES : (i + 1) * LANES]


def flat(value):
    return value.reshape(-1, value.shape[-1])


def at_tick(step, ticks):
    for when, work in ticks:
        pl.when(step == when)(functools.partial(work))


def group_biases(vt):
    length = vt.shape[0]
    groups = length // (3 * HD)
    lanes = lane_ids((length, LANES))
    q, v = vt[:, 6:7], vt[:, 7:8]
    zero = jnp.zeros((LANES, 1), F32)
    out = jnp.zeros((length, LANES), F32)
    for t in range(groups):
        a, b, c = 3 * HD * t, 3 * HD * t + LANES, 3 * HD * (t + 1)
        column = jnp.concatenate([q[a:b], zero, v[a:b], q[b:c], zero[:HD], zero, v[b:c], zero[:HD]], axis=0)
        out = jnp.where(lanes == t, column, out)
    return out.T


def fwd_setup(vt_v, seg, vec_rows, bias_v, oh_v, km_v):
    vt = flat(vt_v[...])
    vec_rows[...] = vt.T[: vec_rows.shape[0]]
    biases = group_biases(vt)
    for t in range(bias_v.shape[0]):
        bias_v[t] = biases[t : t + 1]
    place = lane_ids(oh_v.shape) % HD
    same = seg[...] == place
    oh_v[...] = jnp.where(same, 1.0, 0.0).astype(BF)
    km_v[...] = key_marks(seg, km_v.shape)


def key_marks(seg, shape):
    place = lane_ids(shape) % HD
    marks = jnp.where(place < SEGS, jnp.where(seg[...] == place, 0.0, MASKED), 1.0)
    return jnp.where(place < TOP, marks, 0.0).astype(BF)


def fwd_group(t, x_v, a_v, bias_v, km_v, qkv_v, ka_v, va_v):
    x = flat(x_v[...])
    w = flat(a_v[...])
    low = low_half((x.shape[0], LANES))
    for i in range(6):
        cols = slice(i * LANES, (i + 1) * LANES)
        out = mm(x, w[:, cols]) + bias_v[t, :, cols]
        if i % 3 == 0:
            out = out * QSCALE
        out = out.astype(BF)
        qkv_v[t, :, cols] = out
        one = jnp.ones_like(out)
        if i == 1:
            ka_v[0] = jnp.where(low, out, km_v[...])
            ka_v[1] = jnp.where(low, km_v[...], out)
        if i == 2:
            va_v[0] = jnp.where(low, out, one)
            va_v[1] = jnp.where(low, one, out)
        if i == 4:
            ka_v[2] = jnp.where(low, out, km_v[...])
        if i == 5:
            va_v[2] = jnp.where(low, out, one)


def fwd_block(t, rows, block, qkv_v, ka_v, va_v, oh_v, ctx_v, lse_ref):
    shape = (block, LANES)
    low = low_half(shape)
    lanes = lane_ids(shape)
    marks = oh_v[rows, :]
    lse = lse_ref[rows, :]
    parts = []
    for h in range(3):
        q = tile(qkv_v, t, 0 if h < 2 else 3, rows)
        q = jnp.where(low, marks, q) if h == 1 else jnp.where(low, q, marks)
        s = mm(q, ka_v[h], NT)
        top = jnp.max(s, axis=1, keepdims=True)
        w = jnp.exp2(s - top).astype(BF)
        o = mm(w, va_v[h])
        total = o[:, HD : HD + 1] if h != 1 else o[:, 0:1]
        lse = jnp.where(lanes == 3 * t + h, top + jnp.log2(total), lse)
        parts.append(o)
    lse_ref[rows, :] = lse
    sums = swap_halves(jnp.where(low, parts[1], parts[0]))
    pair = jnp.where(low, parts[0], parts[1]) / sums
    last = parts[2] / swap_halves(parts[2])
    zero = jnp.zeros(shape, F32)
    tiles = (pair, swap_halves(pair), swap_halves(last))
    for i, value in enumerate(tiles):
        ctx_v[t, rows, i * LANES : (i + 1) * LANES] = jnp.where(low, zero, value).astype(BF)


def spread(base, value, lanes):
    hi = value.astype(BF).astype(F32)
    rest = value - hi
    mid = rest.astype(BF).astype(F32)
    low = rest - mid
    place = lanes % HD
    out = jnp.where(place == SEGS, hi, jnp.where(place == SEGS + 1, mid, jnp.where(place == SEGS + 2, low, 0.0)))
    return jnp.where(place < SEGS, base, out.astype(BF))


def bwd_group(t, qkv, ctx, dctx, lse, oh_v, km_v, qa_v, ka_v, va_v, da_v, kt_v, dqt_v):
    length = oh_v.shape[0]
    shape = (length, LANES)
    low = low_half(shape)
    lanes = lane_ids(shape)
    oh, km = oh_v[...], km_v[...]
    ones = jnp.where((lanes % HD >= SEGS) & (lanes % HD < TOP), 1.0, 0.0).astype(BF)

    def cols(ref, i):
        return ref[:, i * LANES : (i + 1) * LANES]

    q, k, v = cols(qkv, 0), cols(qkv, 1), cols(qkv, 2)
    q2, k2, v2 = cols(qkv, 3), cols(qkv, 4), cols(qkv, 5)
    c_pair = jnp.where(low, swap_halves(cols(ctx, 1)), cols(ctx, 0))
    d_pair = jnp.where(low, swap_halves(cols(dctx, 1)), cols(dctx, 0))
    c_last = swap_halves(cols(ctx, 2))
    d_last = swap_halves(cols(dctx, 2))
    prod = c_pair.astype(F32) * d_pair.astype(F32)
    prod2 = c_last.astype(F32) * d_last.astype(F32)
    lse_all = lse[...]
    zero = jnp.zeros_like(prod)
    for h in range(3):
        mine = low if h != 1 else jnp.logical_not(low)
        delta = jnp.sum(jnp.where(mine, prod2 if h == 2 else prod, zero), axis=1, keepdims=True)
        top = jnp.sum(jnp.where(lanes == 3 * t + h, lse_all, zero), axis=1, keepdims=True)
        qa_v[h] = jnp.where(mine, q2 if h == 2 else q, spread(oh, -top, lanes))
        da_v[h] = jnp.where(mine, d_last if h == 2 else d_pair, spread(jnp.zeros_like(oh), -delta, lanes))
        ka_v[h] = jnp.where(mine, k2 if h == 2 else k, km)
        va_v[h] = jnp.where(mine, v2 if h == 2 else v, ones)
    kt_v[0] = k.T
    kt_v[1] = k2.T
    dqt_v[...] = jnp.zeros_like(dqt_v)


def bwd_block(rows, block, qa_v, ka_v, va_v, da_v, kt_v, dqt_v, out):
    low = low_half((block, LANES))
    dk, dv = [], []
    for h in range(3):
        s = mm(ka_v[h, rows, :], qa_v[h], NT)
        p = jnp.exp2(s)
        dv.append(mm(p.astype(BF), da_v[h]))
        dp = mm(va_v[h, rows, :], da_v[h], NT)
        ds = (p * dp).astype(BF)
        dk.append(mm(ds, qa_v[h]) * (1.0 / LOG2E))
        slot, half = h // 2, slice((h % 2) * HD, (h % 2 + 1) * HD)
        dqt_v[slot, half, :] += mm(kt_v[slot, half, rows], ds)
    zero = jnp.zeros((block, LANES), F32)
    tiles = {
        1: jnp.where(low, dk[0], dk[1]),
        2: jnp.where(low, dv[0], dv[1]),
        4: jnp.where(low, dk[2], zero),
        5: jnp.where(low, dv[2], zero),
    }
    for i, value in tiles.items():
        out[rows, i * LANES : (i + 1) * LANES] = value.astype(BF)


def bwd_finish(dqt_v, out):
    scale = HD**-0.5
    low = low_half((out.shape[0], LANES))
    out[:, 0:LANES] = (dqt_v[0].T * scale).astype(BF)
    last = dqt_v[1].T * scale
    out[:, 3 * LANES : 4 * LANES] = jnp.where(low, last, jnp.zeros_like(last)).astype(BF)


def normalize(values, gain_row, shift_row):
    average = jnp.mean(values, axis=-1, keepdims=True)
    centered = values - average
    variance = jnp.mean(centered * centered, axis=-1, keepdims=True)
    inverse = lax.rsqrt(variance + EPS)
    unit = centered * inverse
    return unit * gain_row + shift_row, unit, inverse


def normalize_back(upstream, unit, inverse, gain_row):
    d_unit = upstream * gain_row
    first = jnp.mean(d_unit, axis=-1, keepdims=True)
    second = jnp.mean(d_unit * unit, axis=-1, keepdims=True)
    return inverse * (d_unit - first - unit * second)


def eighths(value):
    return jnp.sum(value.reshape(-1, 8, value.shape[-1]), axis=0)


def gelu_both(x):
    a = jnp.abs(x)
    tail = jnp.exp2(x * x * (-0.5 * LOG2E))
    t = 1.0 / (1.0 + (0.3275911 * 0.5**0.5) * a)
    poly = ((((1.061405429 * t - 1.453152027) * t + 1.421413741) * t - 0.284496736) * t + 0.254829592) * t
    rest = 0.5 * poly * tail
    cdf = jnp.where(x < 0, rest, 1.0 - rest)
    return x * cdf, cdf + x * tail * 0.3989422804014327


def mid_rows(i, block, refs, late):
    (x_v, cot_v, ctx_v, ao_v, in_v, dn_v, vec, act_v, dact_v, dpre_v, y1_v, g2_v, out_v, gh1_v, dctx_v, sums_v) = refs
    rows = pl.ds(pl.multiple_of(i * block, block), block)
    few = block // x_v.shape[1]
    these = pl.ds(i * few, few)
    apart = (few, *x_v.shape[1:])
    groups = in_v.shape[0]

    def row(k):
        return vec[k : k + 1, :]

    def note(k, value):
        sums_v[k] += eighths(value)

    attn = mm(ctx_v[0, rows, :], ao_v[0], NT)
    for t in range(1, groups):
        attn = attn + mm(ctx_v[t, rows, :], ao_v[t], NT)
    h1 = flat(x_v[these]).astype(F32) + attn + row(4)
    y1, u1, r1 = normalize(h1, row(0), row(1))
    y1_low = y1.astype(BF)
    y1_v[rows, :] = y1_low
    ffn = row(5) + y1
    pl.when(i == 0)(lambda: wait_all(late))
    for t in range(groups):
        pre = mm(y1_low, in_v[t]) + row(8 + t)
        act, slope = gelu_both(pre)
        act = act.astype(BF)
        act_v[t, rows, :] = act
        dact_v[t] = slope.astype(BF)
        ffn = ffn + mm(act, dn_v[t], NT)
    out, u2, r2 = normalize(ffn, row(2), row(3))
    out_v[these] = out.astype(BF).reshape(apart)
    up = flat(cot_v[these]).astype(F32)
    g_h2 = normalize_back(up, u2, r2, row(2))
    note(2, up * u2)
    note(3, up)
    note(5, g_h2)
    g2 = g_h2.astype(BF)
    g2_v[rows, :] = g2
    g_y1 = g_h2
    for t in range(groups):
        dpre = (mm(g2, dn_v[t]) * dact_v[t].astype(F32)).astype(BF)
        dpre_v[t, rows, :] = dpre
        note(8 + t, dpre.astype(F32))
        g_y1 = g_y1 + mm(dpre, in_v[t], NT)
    note(0, g_y1 * u1)
    note(1, g_y1)
    g_h1 = normalize_back(g_y1, u1, r1, row(0))
    note(4, g_h1)
    gh1_v[these] = g_h1.reshape(apart)
    g1 = g_h1.astype(BF)
    for t in range(groups):
        dctx_v[t, rows, :] = mm(g1, ao_v[t]).astype(BF)

STEP = {"z2": 4, "z1": 2, "y": 1, "x": 2, "c": 1}
BLOCKS = ("x", "c", "z2", "z1", "y")
FEATURES = ("z2", "z1", "y", "x", "c")
P_Y = ("z2", "z1", "x", "y")
P_Z = ("z2", "x", "y", "z1")
Q_Y = ("z2", "x", "z1", "y")
Q_Z = ("z2", "x", "y", "z1")
P_X = ("z2", "y", "z1", "x")


class Place:
    def __init__(self):
        self.d = lax.axis_index("dp")
        self.t = lax.axis_index("tensor")
        self.bit = {
            "x": self.t // 2,
            "c": self.t % 2,
            "z2": self.d // 4,
            "z1": (self.d // 2) % 2,
            "y": self.d % 2,
        }

    def flip(self, dim):
        return 1 - self.bit[dim]

    def peer(self, dim):
        move = STEP[dim] * (1 - 2 * self.bit[dim])
        if dim in ("x", "c"):
            return (self.d, self.t + move)
        return (self.d + move, self.t)

    def row_peer(self, k):
        t = self.t
        if k in (1, 3):
            t = t + (1 - 2 * self.bit["c"])
        if k in (2, 3):
            t = t + 2 * (1 - 2 * self.bit["x"])
        return t

    def index(self, dims, **chosen):
        return tuple(chosen.get(dim, self.bit[dim]) for dim in dims)


def enter(place):
    bar = pltpu.get_barrier_semaphore()
    peers = [place.peer(dim) for dim in BLOCKS] + [(place.d, place.row_peer(3))]
    for peer in peers:
        pl.semaphore_signal(bar, inc=1, device_id=peer, device_id_type=MESH)
    pl.semaphore_wait(bar, len(peers))


class Copies:
    def __init__(self, send, recv, local):
        self.send, self.recv, self.local = send, recv, local
        self.count = self.locals = 0

    def remote(self, ends):
        i = self.count
        self.count += 1

        def copy():
            src, dst, peer = ends()
            return pltpu.make_async_remote_copy(
                src_ref=src,
                dst_ref=dst,
                send_sem=self.send.at[i],
                recv_sem=self.recv.at[i],
                device_id=peer,
                device_id_type=MESH,
            )

        copy().start()
        return lambda: copy().wait()

    def here(self, ends):
        i = self.locals
        self.locals += 1

        def copy():
            src, dst = ends()
            return pltpu.make_async_copy(src, dst, self.local.at[i])

        copy().start()
        return lambda: copy().wait()


ALLBITS = slice(None)


class GatherPart:
    def __init__(self, place, copies, own, full, order, rows, dims=BLOCKS):
        self.place, self.copies, self.own, self.full, self.order = place, copies, own, full, order
        self.rows, self.dims = rows, dims
        self.stage = 0
        self.side = []

    def at(self, **chosen):
        return self.full.at[self.place.index(self.dims, **chosen) + (self.rows,)]

    def begin(self):
        p, c = self.place, self.copies
        self.current = c.remote(lambda: (self.own.at[self.rows], self.at(), p.peer(self.order[0])))
        self.side.append(c.remote(lambda: (self.own.at[self.rows], self.at(), p.peer("c"))))
        self.keep = c.here(lambda: (self.own.at[self.rows], self.at()))

    def held(self, s):
        return self.at(**{dim: ALLBITS for dim in self.order[:s]})

    def arrived(self, s):
        dim = self.order[s]
        return self.at(**{other: ALLBITS for other in self.order[:s]}, **{dim: self.place.flip(dim)})

    def advance(self):
        p, c, s = self.place, self.copies, self.stage
        self.current()
        if s == 0:
            self.keep()
        if s + 1 < len(self.order):
            self.current = c.remote(lambda: (self.held(s + 1), self.held(s + 1), p.peer(self.order[s + 1])))
        self.side.append(c.remote(lambda: (self.arrived(s), self.arrived(s), p.peer("c"))))
        self.stage = s + 1

    def finish(self):
        wait_all(self.side)


def every(count, work):
    if count == 0:
        work(())
        return

    def body(i, carry):
        work(tuple((i // 2**j) % 2 for j in reversed(range(count))))
        return carry

    lax.fori_loop(0, 2**count, body, 0)


def blockwise(ref):
    return ref.reshape(2 ** (len(ref.shape) - 2), *ref.shape[-2:])


def spot(bits):
    place = 0
    for bit in bits:
        place = 2 * place + bit
    return place


class ReducePart:
    def __init__(self, place, copies, src, total, arrive, out, order, rows, dims=BLOCKS, paired=False):
        self.paired = paired
        self.place, self.copies, self.src, self.total, self.arrive = place, copies, src, total, arrive
        self.out, self.order, self.rows, self.dims = out, order, rows, dims
        self.inner = tuple(dim for dim in dims if dim != "c")
        self.kept = self.inner
        if total is None:
            self.total, self.kept = src, dims
        self.stage = 0

    def source(self, **chosen):
        return self.src.at[self.place.index(self.dims, **chosen) + (self.rows,)]

    def sums(self, **chosen):
        return self.total.at[self.place.index(self.kept, **chosen) + (self.rows,)]

    def half(self, bit):
        p, first = self.place, self.order[0]

        def ends():
            free = {dim: ALLBITS for dim in self.inner}
            free[first] = bit()
            dst = self.arrive[0].at[p.index(self.inner, **free) + (self.rows,)]
            return self.source(c=p.flip("c"), **free), dst, p.peer("c")

        return self.copies.remote(ends)

    def begin(self):
        p, first = self.place, self.order[0]
        if self.paired:
            self.keep = self.copies.here(lambda: (self.src.at[(ALLBITS,) * 4 + (self.rows,)], self.total.at[(ALLBITS,) * 4 + (self.rows,)]))
            return
        self.side = [self.half(lambda: p.flip(first)), self.half(lambda: p.bit[first])]
        if self.kept is self.inner:
            free = {dim: ALLBITS for dim in self.inner}
            self.keep = self.copies.here(lambda: (self.source(**free), self.sums(**free)))

    def add(self, fixed, bit):
        s = self.stage
        left = [dim for dim in self.inner if dim not in self.order[:s]] if s else list(self.inner)
        loose = [dim for dim in left if dim != fixed]

        total, arrive = blockwise(self.total), blockwise(self.arrive[s])

        def work(bits):
            chosen = dict(zip(loose, bits))
            chosen[fixed] = bit
            mine = spot(self.place.index(self.kept, **chosen))
            there = spot(tuple(chosen[dim] for dim in left))
            both = total[mine, self.rows, :].astype(F32) + arrive[there, self.rows, :].astype(F32)
            total[mine, self.rows, :] = both.astype(total.dtype)

        every(len(loose), work)

    def send(self):
        p, s = self.place, self.stage
        dim = self.order[s]
        free = {other: ALLBITS for other in self.order[s + 1 :]}

        def ends():
            src = self.sums(**free, **{dim: p.flip(dim)})
            dst = self.arrive[s + 1].at[(ALLBITS,) * len(free) + (self.rows,)]
            return src, dst, p.peer(dim)

        return self.copies.remote(ends)

    def advance(self):
        p, s = self.place, self.stage
        if s == 0:
            if self.kept is self.inner:
                self.keep()
            if not self.paired:
                self.side[0]()
        else:
            self.current()
        if s < len(self.order):
            dim = self.order[s]
            if s == 0 and self.paired:
                self.current = self.send()
                self.stage = 1
                return
            self.add(dim, p.flip(dim))
            self.current = self.send()
            if s == 0:
                self.side[1]()
            self.add(dim, p.bit[dim])
        else:
            mine = spot(self.place.index(self.kept))
            self.out[self.rows, :] = blockwise(self.total)[mine, self.rows, :].astype(F32) + self.arrive[s][self.rows, :].astype(F32)
        self.stage = s + 1


def arrivals(rows, cols, dtype):
    return [pltpu.VMEM((2,) * n + (rows, cols), dtype) for n in (4, 3, 2, 1, 0)]


def start_row(place, copies, src, dst, k):
    def ends():
        to = place.row_peer(k)
        return src.at[to], dst.at[place.t], (place.d, to)

    return copies.remote(ends)


def keep_row(place, copies, src, dst):
    return copies.here(lambda: (src.at[place.t], dst.at[place.t]))


def start_rows(place, copies, src, dst):
    return [start_row(place, copies, src, dst, k) for k in (2, 3, 1)] + [keep_row(place, copies, src, dst)]


def wait_all(waits):
    for wait in waits:
        wait()


def params(collective=None):
    more = {} if collective is None else {"collective_id": collective, "has_side_effects": True}
    return pltpu.CompilerParams(vmem_limit_bytes=60 << 20, **more)


def sems(count):
    return [pltpu.SemaphoreType.DMA((count,))] * 2


def fwd_core(group_ref, x_v, vt_v, seg, qkv, ctx, xt, lse, vec_rows, s, ticks):
    (a_v, bias_v, oh_v, km_v, qkv_v, ka_v, va_v, ctx_v, xt_v, a_sem, out_sem) = s
    groups, length = qkv.shape[:2]
    block = 256
    blocks = length // block

    def load(t):
        return pltpu.make_async_copy(group_ref(t), a_v.at[t % 2], a_sem.at[t % 2])

    load(0).start()
    fwd_setup(vt_v, seg, vec_rows, bias_v, oh_v, km_v)
    lse[...] = jnp.zeros_like(lse)

    def step(i, carry):
        t, b = i // blocks, i % blocks
        at_tick(i, ticks)

        @pl.when(b == 0)
        def _():
            load(t).wait()

            @pl.when(t + 1 < groups)
            def _():
                load(t + 1).start()

            fwd_group(t, x_v, a_v.at[t % 2], bias_v, km_v, qkv_v, ka_v, va_v)
            pltpu.make_async_copy(qkv_v.at[t], qkv.at[t], out_sem.at[0, t]).start()

        rows = pl.ds(pl.multiple_of(b * block, block), block)
        fwd_block(t, rows, block, qkv_v, ka_v, va_v, oh_v, ctx_v, lse)

        @pl.when(b == blocks - 1)
        def _():
            pltpu.make_async_copy(ctx_v.at[t], ctx.at[t], out_sem.at[1, t]).start()

        return carry

    lax.fori_loop(0, groups * blocks, step, 0)
    xt_v[...] = flat(x_v[...]).T
    turned = pltpu.make_async_copy(xt_v, xt, a_sem.at[0])
    turned.start()
    turned.wait()
    for t in range(groups):
        pltpu.make_async_copy(qkv_v.at[t], qkv.at[t], out_sem.at[0, t]).wait()
        pltpu.make_async_copy(ctx_v.at[t], ctx.at[t], out_sem.at[1, t]).wait()


def fwd_scratch(groups, length, width):
    return [
        pltpu.VMEM((2, 2, 2, 2, width // 8, width), BF),
        pltpu.VMEM((groups, 1, width), F32),
        pltpu.VMEM((length, LANES), BF),
        pltpu.VMEM((length, LANES), BF),
        pltpu.VMEM((groups, length, width), BF),
        pltpu.VMEM((3, length, LANES), BF),
        pltpu.VMEM((3, length, LANES), BF),
        pltpu.VMEM((groups, length, 3 * LANES), BF),
        pltpu.VMEM((width, length), BF),
        pltpu.SemaphoreType.DMA((2,)),
        pltpu.SemaphoreType.DMA((2, groups)),
    ]


def fwd_shapes(groups, length, width):
    return [
        jax.ShapeDtypeStruct((groups, length, width), BF),
        jax.ShapeDtypeStruct((groups, length, 3 * LANES), BF),
        jax.ShapeDtypeStruct((width, length), BF),
        jax.ShapeDtypeStruct((length, LANES), F32),
        jax.ShapeDtypeStruct((16, width), F32),
    ]


def fwd_comm_kernel(shard, vec, tok, cot, seg, g, x, co, qkv, ctx, xt, lse, vec_rows, x_v, vt_v, send, recv, loc, *s):
    place = Place()
    enter(place)
    copies = Copies(send, recv, loc)
    mk = functools.partial(GatherPart, place, copies)
    n = shard.shape[1]
    third, half = n // 3, n // 2
    first = [mk(vec, vt_v, Q_Z, pl.ds(0, vec.shape[0]), FEATURES)]
    first += [mk(shard.at[0], g.at[0], order, pl.ds(i * third, third)) for i, order in enumerate((Q_Y, Q_Z, P_X))]
    later = [mk(shard.at[1], g.at[1], order, pl.ds(i * half, half)) for i, order in enumerate((Q_Y, Q_Z))]
    later += [mk(shard.at[2], g.at[2], order, pl.ds(i * third, third)) for i, order in enumerate((Q_Y, Q_Z, P_X))]
    moved = []

    def advance():
        for part in later:
            part.advance()

    def cot_rows():
        advance()
        moved.extend(start_rows(place, copies, cot, co))

    for part in first:
        part.begin()
    rows = [start_row(place, copies, tok, x_v, k) for k in (2, 1)] + [keep_row(place, copies, tok, x_v)]
    for stage in range(4):
        for part in first:
            part.advance()
        if stage == 0:
            rows.append(start_row(place, copies, tok, x_v, 3))
        if stage == 2:
            for part in later:
                part.begin()
    for part in first:
        part.finish()
    wait_all(rows)
    keep = copies.here(lambda: (x_v, x))
    ticks = [(1, cot_rows), (4, advance), (8, advance)]
    fwd_core(lambda t: g.at[0, t // 2, t % 2], x_v, vt_v, seg, qkv, ctx, xt, lse, vec_rows, s, ticks)
    advance()
    for part in later:
        part.finish()
    wait_all(moved)
    keep()


def fwd_comm(shard, vec, tok, cot, seg):
    groups, block, width = tok.shape
    length = groups * block
    bits = (2,) * 5
    return pl.pallas_call(
        fwd_comm_kernel,
        in_specs=[ANY] * 4 + [VMEM],
        out_specs=[ANY] * 6 + [VMEM] * 2,
        out_shape=[
            jax.ShapeDtypeStruct((3,) + bits + shard.shape[1:], BF),
            jax.ShapeDtypeStruct(tok.shape, BF),
            jax.ShapeDtypeStruct(cot.shape, BF),
        ]
        + fwd_shapes(groups, length, width),
        scratch_shapes=[
            pltpu.VMEM(tok.shape, BF),
            pltpu.VMEM(bits + vec.shape, F32),
            *sems(96),
            pltpu.SemaphoreType.DMA((20,)),
        ]
        + fwd_scratch(groups, length, width),
        compiler_params=params(0),
        name="attention_forward",
    )(shard, vec, tok, cot, seg)


def fwd_plain_kernel(g, x, vt, seg, qkv, ctx, xt, lse, vec_rows, sem, x_v, *s):
    copy = pltpu.make_async_copy(x, x_v, sem)
    copy.start()
    copy.wait()
    fwd_core(lambda t: g.at[0, t // 2, t % 2], x_v, vt, seg, qkv, ctx, xt, lse, vec_rows, s, [])


def fwd_plain(g, x, vt, seg):
    groups, block, width = x.shape
    length = groups * block
    return pl.pallas_call(
        fwd_plain_kernel,
        in_specs=[ANY, ANY, VMEM, VMEM],
        out_specs=[ANY] * 3 + [VMEM] * 2,
        out_shape=fwd_shapes(groups, length, width),
        scratch_shapes=[pltpu.SemaphoreType.DMA, pltpu.VMEM(x.shape, BF)] + fwd_scratch(groups, length, width),
        compiler_params=params(),
        name="attention_forward",
    )(g, x, vt, seg)


def mid_kernel(g, x, cot, ctx, vec, out, grad, gh1, dctx, sums, x_v, cot_v, ctx_v, ao_v, in_v, dn_v, act_v, dact_v, dpre_v, y1_v, g2_v, out_v, gh1_v, dctx_v, t_v, sem, out_sem):
    groups, length = ctx.shape[:2]
    width = x.shape[2]
    half = width // 2
    blocks, block = x.shape[:2]
    few = dact_v.shape[1] // block

    def copy(src, dst, i):
        return pltpu.make_async_copy(src, dst, sem.at[i])

    loads = [copy(x, x_v, 0), copy(ctx, ctx_v, 1), copy(g.at[0, :, :, half:], ao_v, 2)]
    loads += [copy(g.at[1], in_v, 3), copy(g.at[2], dn_v, 4), copy(cot, cot_v, 5)]
    for load in loads:
        load.start()
    sums[...] = jnp.zeros_like(sums)
    for load in loads[:3]:
        load.wait()
    refs = (x_v, cot_v, ctx_v, ao_v, in_v, dn_v, vec, act_v, dact_v, dpre_v, y1_v, g2_v, out_v, gh1_v, dctx_v, sums)

    def step(i, carry):
        mid_rows(i, few * block, refs, [load.wait for load in loads[3:]])
        for j in range(few):
            b = i * few + j
            pltpu.make_async_copy(out_v.at[b], out.at[b], out_sem.at[0, b]).start()
            pltpu.make_async_copy(gh1_v.at[b], gh1.at[b], out_sem.at[1, b]).start()
        return carry

    lax.fori_loop(0, blocks // few, step, 0)
    send = copy(dctx_v, dctx, 0)
    send.start()
    t_v[...] = y1_v[...].T

    def in_step(t, carry):
        in_v[t] = mm(t_v[...], dpre_v[t]).astype(BF)
        pltpu.make_async_copy(in_v.at[t], grad.at[0, t], out_sem.at[2, t]).start()
        return carry

    lax.fori_loop(0, groups, in_step, 0)
    t_v[...] = g2_v[...].T

    def dn_step(t, carry):
        dn_v[t] = mm(t_v[...], act_v[t]).astype(BF)
        pltpu.make_async_copy(dn_v.at[t], grad.at[1, t], out_sem.at[3, t]).start()
        return carry

    lax.fori_loop(0, groups, dn_step, 0)
    send.wait()
    for i in range(blocks):
        pltpu.make_async_copy(out_v.at[i], out.at[i], out_sem.at[0, i]).wait()
        pltpu.make_async_copy(gh1_v.at[i], gh1.at[i], out_sem.at[1, i]).wait()
    for t in range(groups):
        pltpu.make_async_copy(in_v.at[t], grad.at[0, t], out_sem.at[2, t]).wait()
        pltpu.make_async_copy(dn_v.at[t], grad.at[1, t], out_sem.at[3, t]).wait()


def middle(g, x, cot, ctx, vec):
    groups, length, _ = ctx.shape
    blocks, block, width = x.shape
    flats = (groups, width, width)
    return pl.pallas_call(
        mid_kernel,
        in_specs=[ANY] * 4 + [VMEM],
        out_specs=[ANY] * 4 + [VMEM],
        out_shape=[
            jax.ShapeDtypeStruct(x.shape, BF),
            jax.ShapeDtypeStruct((2,) + flats, BF),
            jax.ShapeDtypeStruct(x.shape, F32),
            jax.ShapeDtypeStruct(ctx.shape, BF),
            jax.ShapeDtypeStruct((8 + groups, 8, width), F32),
        ],
        scratch_shapes=[
            pltpu.VMEM(x.shape, BF),
            pltpu.VMEM(x.shape, BF),
            pltpu.VMEM(ctx.shape, BF),
            pltpu.VMEM((groups, width, width // 2), BF),
            pltpu.VMEM(flats, BF),
            pltpu.VMEM(flats, BF),
            pltpu.VMEM((groups, length, width), BF),
            pltpu.VMEM((groups, block, width), BF),
            pltpu.VMEM((groups, length, width), BF),
            pltpu.VMEM((length, width), BF),
            pltpu.VMEM((length, width), BF),
            pltpu.VMEM(x.shape, BF),
            pltpu.VMEM(x.shape, F32),
            pltpu.VMEM(ctx.shape, BF),
            pltpu.VMEM((width, length), BF),
            pltpu.SemaphoreType.DMA((6,)),
            pltpu.SemaphoreType.DMA((4, max(groups, blocks))),
        ],
        compiler_params=params(),
        name="feed_forward",
    )(g, x, cot, ctx, vec)


def bwd_core(qkv, ctx, dctx, lse, seg, xt, gh1, g, da, gx, qsum, s, ticks, place=None):
    (qkv_v, ctx_v, dctx_v, a_v, oh_v, km_v, qa_v, ka_v, va_v, da_v, kt_v, dqt_v, dqkv_v, x_v, gx_v, xt_v, gt_v, dw_v, pair_v, in_sem, out_sem, x_sem, pair_sem) = s
    groups, length = qkv.shape[:2]
    block = 256
    blocks = length // block
    half = 3 * LANES

    early = groups if place is None else groups // 2

    def group(i):
        if place is None:
            return i
        core = place.bit["c"]
        return 2 * (i % 2) + core + (1 - i // 2) * (1 - 2 * core)

    def loads(i):
        t, slot = group(i), i % 2
        return [
            pltpu.make_async_copy(qkv.at[t], qkv_v.at[slot], in_sem.at[0, slot]),
            pltpu.make_async_copy(ctx.at[t], ctx_v.at[slot], in_sem.at[1, slot]),
            pltpu.make_async_copy(dctx.at[t], dctx_v.at[slot], in_sem.at[2, slot]),
            pltpu.make_async_copy(g.at[0, t], a_v.at[slot], in_sem.at[3, slot]),
        ]

    def result(i):
        if place is None:
            return pltpu.make_async_copy(dw_v.at[i], da.at[i], out_sem.at[i])
        return pltpu.make_async_copy(dw_v.at[i], da.at[i - early], out_sem.at[i])

    def hand_over(i):
        return pltpu.make_async_remote_copy(
            src_ref=dw_v.at[i],
            dst_ref=pair_v.at[i],
            send_sem=pair_sem.at[0, i],
            recv_sem=pair_sem.at[1, i],
            device_id=place.peer("c"),
            device_id_type=MESH,
        )

    more = [pltpu.make_async_copy(xt, xt_v, x_sem.at[0]), pltpu.make_async_copy(gh1, gx_v, x_sem.at[1])]
    for load in loads(0) + more:
        load.start()
    oh_v[...] = jnp.where(seg[...] == lane_ids(oh_v.shape) % HD, 1.0, 0.0).astype(BF)
    km_v[...] = key_marks(seg, km_v.shape)

    def ready():
        for load in more:
            load.wait()
        gt_v[...] = flat(gx_v[...]).astype(BF).T

    def weights(i, slot, add):
        def chunk(r, inner):
            part = pl.ds(pl.multiple_of(r * block, block), block)
            lead = mm(xt_v[part, :], dqkv_v[:, :half])
            rest = mm(xt_v[part, :], dqkv_v[:, half:]) + mm(gt_v[part, :], ctx_v[slot])
            if add:
                lead = lead + pair_v[i - early, part, :half].astype(F32)
                rest = rest + pair_v[i - early, part, half:].astype(F32)
            dw_v[i, part, :half] = lead.astype(BF)
            dw_v[i, part, half:] = rest.astype(BF)
            return inner

        lax.fori_loop(0, dw_v.shape[1] // block, chunk, 0)

    def rows(b, slot):
        part = pl.ds(pl.multiple_of(b * block, block), block)
        gx_v[b] = gx_v[b] + mm(dqkv_v[part, :], a_v[slot], NT)

    def step(i, carry):
        at, b = i // blocks, i % blocks
        slot = at % 2
        at_tick(i, ticks)
        pl.when(i == 1)(ready)

        @pl.when(b == 0)
        def _():
            for load in loads(at):
                load.wait()

            @pl.when(at + 1 < groups)
            def _():
                for load in loads(at + 1):
                    load.start()

            bwd_group(group(at), qkv_v.at[slot], ctx_v.at[slot], dctx_v.at[slot], lse, oh_v, km_v, qa_v, ka_v, va_v, da_v, kt_v, dqt_v)

        part = pl.ds(pl.multiple_of(b * block, block), block)
        bwd_block(part, block, qa_v, ka_v, va_v, da_v, kt_v, dqt_v, dqkv_v)

        @pl.when(b == blocks - 1)
        def _():
            bwd_finish(dqt_v, dqkv_v)
            qsum[group(at)] = mm(jnp.ones((8, length), BF), dqkv_v[...])
            if place is None:
                weights(at, slot, False)
                result(at).start()
            else:

                @pl.when(at < early)
                def _():
                    weights(at, slot, False)
                    hand_over(at).start()

                @pl.when(at >= early)
                def _():
                    hand_over(at - early).wait()
                    weights(at, slot, True)
                    result(at).start()

            def row_step(r, inner):
                rows(r, slot)
                return inner

            lax.fori_loop(0, blocks, row_step, 0)

        return carry

    lax.fori_loop(0, groups * blocks, step, 0)

    def low_step(r, carry):
        x_v[r] = gx_v[r].astype(BF)
        return carry

    lax.fori_loop(0, blocks, low_step, 0)
    last = pltpu.make_async_copy(x_v, gx, x_sem.at[0])
    last.start()
    for i in range(0 if place is None else early, groups):
        result(i).wait()
    last.wait()


def bwd_scratch(groups, length, width, x):
    half = 3 * LANES
    return [
        pltpu.VMEM((2, length, width), BF),
        pltpu.VMEM((2, length, half), BF),
        pltpu.VMEM((2, length, half), BF),
        pltpu.VMEM((2, width, width), BF),
        pltpu.VMEM((length, LANES), BF),
        pltpu.VMEM((length, LANES), BF),
        pltpu.VMEM((3, length, LANES), BF),
        pltpu.VMEM((3, length, LANES), BF),
        pltpu.VMEM((3, length, LANES), BF),
        pltpu.VMEM((3, length, LANES), BF),
        pltpu.VMEM((2, LANES, length), BF),
        pltpu.VMEM((2, LANES, length), F32),
        pltpu.VMEM((length, width), BF),
        pltpu.VMEM(x, BF),
        pltpu.VMEM(x, F32),
        pltpu.VMEM((width, length), BF),
        pltpu.VMEM((width, length), BF),
        pltpu.VMEM((groups, width, width), BF),
        pltpu.VMEM((groups // 2, width, width), BF),
        pltpu.SemaphoreType.DMA((4, 2)),
        pltpu.SemaphoreType.DMA((groups,)),
        pltpu.SemaphoreType.DMA((2,)),
        pltpu.SemaphoreType.DMA((2, groups // 2)),
    ]


def bwd_shapes(groups, width, x, held):
    return [
        jax.ShapeDtypeStruct((held, width, width), BF),
        jax.ShapeDtypeStruct(x, BF),
        jax.ShapeDtypeStruct((groups, 8, width), F32),
    ]


def bwd_comm_kernel(qkv, ctx, dctx, lse, seg, xt, gh1, g, grad, out, da, gx, qsum, own, out_rows, total, r0, r1, r2, r3, r4, r5, r6, r7, r8, r9, send, recv, loc, *s):
    place = Place()
    enter(place)
    copies = Copies(send, recv, loc)
    half = own.shape[1] // 2
    arrive = ((r0, r1, r2, r3, r4), (r5, r6, r7, r8, r9))
    parts = []
    for w, orders in enumerate(((P_Y, P_Z), (Q_Y, Q_Z))):
        for i, order in enumerate(orders):
            rows = pl.ds(i * half, half)
            parts.append(ReducePart(place, copies, grad.at[w], total.at[w], arrive[w], own.at[w], order[::-1], rows))
    for part in parts:
        part.begin()
    moved = []

    def advance(*which):
        for i in which:
            parts[i].advance()

    def rows():
        moved.extend(start_rows(place, copies, out, out_rows))

    ticks = [
        (2, functools.partial(advance, 0, 1, 2, 3)),
        (3, rows),
        (8, functools.partial(advance, 0, 1, 2, 3)),
        (11, functools.partial(advance, 0, 2)),
        (12, functools.partial(advance, 1, 3)),
        (13, functools.partial(advance, 0, 2)),
        (14, functools.partial(advance, 1, 3)),
    ]
    bwd_core(qkv, ctx, dctx, lse, seg, xt, gh1, g, da, gx, qsum, s, ticks, place)
    advance(0, 1, 2, 3)
    wait_all(moved)


def bwd_comm(qkv, ctx, dctx, lse, seg, xt, gh1, g, grad, out):
    groups, length, width = qkv.shape
    n = grad.shape[6]
    arrive = arrivals(n, width, BF)
    return pl.pallas_call(
        bwd_comm_kernel,
        in_specs=[ANY] * 3 + [VMEM] * 2 + [ANY] * 5,
        out_specs=[ANY, ANY, VMEM, VMEM, ANY],
        out_shape=bwd_shapes(groups, width, gh1.shape, groups // 2)
        + [
            jax.ShapeDtypeStruct((2, n, width), F32),
            jax.ShapeDtypeStruct(out.shape, BF),
        ],
        scratch_shapes=[
            pltpu.VMEM((2, 2, 2, 2, 2, n, width), BF),
            *arrive,
            *arrive,
            *sems(40),
            pltpu.SemaphoreType.DMA((10,)),
        ]
        + bwd_scratch(groups, length, width, gh1.shape),
        compiler_params=params(1),
        name="attention_backward",
    )(qkv, ctx, dctx, lse, seg, xt, gh1, g, grad, out)


def bwd_plain_kernel(qkv, ctx, dctx, lse, seg, xt, gh1, g, da, gx, qsum, *s):
    bwd_core(qkv, ctx, dctx, lse, seg, xt, gh1, g, da, gx, qsum, s, [])


def bwd_plain(qkv, ctx, dctx, lse, seg, xt, gh1, g):
    groups, length, width = qkv.shape
    return pl.pallas_call(
        bwd_plain_kernel,
        in_specs=[ANY] * 3 + [VMEM] * 2 + [ANY] * 3,
        out_specs=[ANY, ANY, VMEM],
        out_shape=bwd_shapes(groups, width, gh1.shape, groups),
        scratch_shapes=bwd_scratch(groups, length, width, gh1.shape),
        compiler_params=params(),
        name="attention_backward",
    )(qkv, ctx, dctx, lse, seg, xt, gh1, g)


def end_vectors(sums, qsum_v, tab_v):
    groups = qsum_v.shape[0]
    tab_v[...] = jnp.zeros_like(tab_v)
    for t in range(groups):
        tab_v[t : t + 1, :] = qsum_v[t][:1]
    parts = tab_v[...].T
    for k in range(sums.shape[0]):
        tab_v[k : k + 1, :] = jnp.sum(sums[k], axis=0, keepdims=True)
    table = tab_v[...].T
    q, v = [], []
    for t in range(groups):
        col = parts[:, t : t + 1]
        q += [col[:LANES], col[3 * LANES : 3 * LANES + HD]]
        v += [col[2 * LANES : 3 * LANES], col[5 * LANES : 5 * LANES + HD]]
    lanes = lane_ids(table.shape)
    table = jnp.where(lanes == 6, jnp.concatenate(q, axis=0), table)
    table = jnp.where(lanes == 7, jnp.concatenate(v, axis=0), table)
    return table


def sum_comm_kernel(da, vt, gx, own, vec_own, gx_rows, total, vtot, r0, r1, r2, r3, r4, r5, r6, r7, r8, send, recv, loc):
    place = Place()
    enter(place)
    copies = Copies(send, recv, loc)
    third = own.shape[0] // 3
    parts = []
    for i, order in enumerate((P_X, Q_Y, Q_Z)):
        rows = pl.ds(i * third, third)
        parts.append(ReducePart(place, copies, da, total, (r0, r0, r1, r2, r3), own, order[::-1], rows, paired=True))
    rows = pl.ds(0, vec_own.shape[0])
    parts.append(ReducePart(place, copies, vt, vtot, (r4, r5, r6, r7, r8), vec_own, P_Y[::-1], rows, FEATURES))
    for part in parts:
        part.begin()
    moved = []
    for stage in range(5):
        for part in parts:
            part.advance()
        if stage == 0:
            moved += [start_row(place, copies, gx, gx_rows, k) for k in (2, 1)] + [keep_row(place, copies, gx, gx_rows)]
        if stage == 2:
            moved.append(start_row(place, copies, gx, gx_rows, 3))
    wait_all(moved)


def sum_comm(da, vt, gx):
    n, width = da.shape[-2:]
    fine = vt.shape[-2]
    return pl.pallas_call(
        sum_comm_kernel,
        in_specs=[ANY] * 3,
        out_specs=[VMEM, VMEM, ANY],
        out_shape=[
            jax.ShapeDtypeStruct((n, width), F32),
            jax.ShapeDtypeStruct((fine, LANES), F32),
            jax.ShapeDtypeStruct(gx.shape, BF),
        ],
        scratch_shapes=[
            pltpu.VMEM((2,) * 4 + (n, width), BF),
            pltpu.VMEM((2,) * 4 + (fine, LANES), F32),
            *arrivals(n, width, BF)[1:],
            *arrivals(fine, LANES, F32),
            *sems(40),
            pltpu.SemaphoreType.DMA((10,)),
        ],
        compiler_params=params(2),
        name="weight_sums",
    )(da, vt, gx)


def vector_kernel(sums, qsum, vt, tab_v):
    vt[...] = end_vectors(sums, qsum, tab_v)


def vector_table(sums, qsum):
    width = sums.shape[2]
    return pl.pallas_call(
        vector_kernel,
        in_specs=[VMEM] * 2,
        out_specs=VMEM,
        out_shape=jax.ShapeDtypeStruct((width, LANES), F32),
        scratch_shapes=[pltpu.VMEM((LANES, width), F32)],
        name="vector_table",
    )(sums, qsum)


def pack(qkv_weight, out_weight, in_weight, down_weight):
    q, k, v = qkv_weight[0], qkv_weight[1], qkv_weight[2]
    o = out_weight.T
    a = [q[:, :LANES], k[:, :LANES], v[:, :LANES]]
    a += [q[:, LANES:], o[:, HD:LANES], k[:, LANES:], o[:, :HD], v[:, LANES:], o[:, LANES:]]
    return jnp.stack([jnp.concatenate(a, axis=1), in_weight, down_weight.T])


def unpack(a):
    def cut(i, half):
        start = i * LANES + half * HD
        return a[:, start : start + HD]

    heads = [jnp.concatenate([cut(i, 0), cut(i, 1), cut(3 + i, 0)], axis=1) for i in range(3)]
    out = jnp.concatenate([cut(4, 1), cut(3, 1), cut(5, 1)], axis=1)
    return jnp.stack(heads), out.T


def local(tokens, segments, qkv_weight, out_weight, in_weight, down_weight, vectors, cotangent):
    n_dp, n_t = lax.axis_size("dp"), lax.axis_size("tensor")
    groups, block, width = tokens.shape
    length = groups * block
    n = in_weight.shape[0]
    fine = vectors.shape[1]
    n_v = vectors.shape[0]
    seg = lax.dynamic_slice_in_dim(segments, lax.axis_index("tensor"), 1, 0).reshape(length, 1)
    shard = pack(qkv_weight, out_weight, in_weight, down_weight)
    vec = jnp.pad(vectors.T, ((0, 0), (0, LANES - n_v)))
    kernels = n_dp == 8 and n_t == 4
    bits = (2,) * 5
    if kernels:
        g, x, cot, qkv, ctx, xt, lse, rows = fwd_comm(shard, vec, tokens, cotangent, seg)
    else:
        full = lax.all_gather(shard, ALL, axis=0, tiled=False).reshape(n_dp, n_t, 3, n, width)
        g = full.transpose(2, 1, 0, 3, 4).reshape((3,) + bits + (width // 8, width))
        vt = lax.all_gather(vec, ALL, axis=0, tiled=True)
        x = lax.all_to_all(tokens, "tensor", split_axis=0, concat_axis=0, tiled=True)
        cot = lax.all_to_all(cotangent, "tensor", split_axis=0, concat_axis=0, tiled=True)
        qkv, ctx, xt, lse, rows = fwd_plain(g, x, vt, seg)
    g = g.reshape(3, groups, width, width)
    out, grad, gh1, dctx, sums = middle(g, x, cot, ctx, rows)
    if kernels:
        grad = grad.reshape((2,) + bits + (n, width))
        da, gx, qsum, own, out_rows = bwd_comm(qkv, ctx, dctx, lse, seg, xt, gh1, g, grad, out)
        vt = vector_table(sums, qsum).reshape(bits + (fine, LANES))
        own_a, own_v, gx_rows = sum_comm(da.reshape(bits[1:] + (n, width)), vt, gx)
    else:
        da, gx, qsum = bwd_plain(qkv, ctx, dctx, lse, seg, xt, gh1, g)
        vt = vector_table(sums, qsum)
        every_grad = jnp.concatenate([da.reshape(1, n_t, n_dp, n, width), grad.reshape(2, n_t, n_dp, n, width)])
        every_grad = every_grad.transpose(2, 1, 0, 3, 4).reshape(n_dp * n_t, 3, n, width)
        own = lax.psum_scatter(every_grad, ALL, scatter_dimension=0, tiled=True)[0].astype(F32)
        own_a, own = own[0], own[1:]
        own_v = lax.psum_scatter(vt[:, :n_v], ALL, scatter_dimension=0, tiled=True)
        out_rows = lax.all_to_all(out, "tensor", split_axis=0, concat_axis=0, tiled=True)
        gx_rows = lax.all_to_all(gx, "tensor", split_axis=0, concat_axis=0, tiled=True)
    d_qkv, d_out = unpack(own_a)
    return out_rows, gx_rows, d_qkv, d_out, own[0], own[1].T, own_v[:, :n_v].T


def solution(mesh):
    rows = P("dp", "tensor", None)
    weights = (P(None, "dp", "tensor"), P("tensor", "dp"), P("dp", "tensor"), P("tensor", "dp"), P(None, ("dp", "tensor")))
    in_specs = (rows, P("dp", None), *weights, rows)
    out_specs = (rows, rows, *weights)
    return jax.shard_map(local, mesh=mesh, in_specs=in_specs, out_specs=out_specs, check_vma=False)
```

```python
import functools

import jax
import jax.numpy as jnp
from jax import lax
from jax.experimental import pallas as pl
from jax.experimental.pallas import tpu as pltpu
from jax.sharding import PartitionSpec as P

HD = 64
LANES = 128
EPS = 1e-05
MASKED = -1e30
SEGS = 32
TOP = 35
LOG2E = 1.4426950408889634
QSCALE = LOG2E * HD**-0.5
BF = jnp.bfloat16
F32 = jnp.float32
ALL = ("dp", "tensor")
MESH = pl.DeviceIdType.MESH
ANY = pl.BlockSpec(memory_space=pl.ANY)
VMEM = pl.BlockSpec(memory_space=pltpu.VMEM)
NT = (((1,), (1,)), ((), ()))
NN = (((1,), (0,)), ((), ()))
TN = (((0,), (0,)), ((), ()))
SLOTS = ((0, (0, 1)), (1, (2,)))


def mm(a, b, dims=NN):
    return lax.dot_general(a, b, dims, preferred_element_type=F32)


def lane_ids(shape):
    return lax.broadcasted_iota(jnp.int32, shape, 1)


def low_half(shape):
    return lane_ids(shape) < HD


def swap_halves(value):
    return pltpu.roll(value, HD, 1)


def tile(ref, t, i, rows=slice(None)):
    return ref[t, rows, i * LANES : (i + 1) * LANES]


def flat(value):
    return value.reshape(-1, value.shape[-1])


def at_tick(step, ticks):
    for when, work in ticks:
        pl.when(step == when)(functools.partial(work))


def group_biases(vt):
    length = vt.shape[0]
    groups = length // (3 * HD)
    lanes = lane_ids((length, LANES))
    q, v = vt[:, 6:7], vt[:, 7:8]
    zero = jnp.zeros((LANES, 1), F32)
    out = jnp.zeros((length, LANES), F32)
    for t in range(groups):
        a, b, c = 3 * HD * t, 3 * HD * t + LANES, 3 * HD * (t + 1)
        column = jnp.concatenate([q[a:b], zero, v[a:b], q[b:c], zero[:HD], zero, v[b:c], zero[:HD]], axis=0)
        out = jnp.where(lanes == t, column, out)
    return out.T


def fwd_setup(vt_v, seg, vec_rows, bias_v, oh_v, km_v):
    vt = flat(vt_v[...])
    vec_rows[...] = vt.T[: vec_rows.shape[0]]
    biases = group_biases(vt)
    for t in range(bias_v.shape[0]):
        bias_v[t] = biases[t : t + 1]
    place = lane_ids(oh_v.shape) % HD
    same = seg[...] == place
    oh_v[...] = jnp.where(same, 1.0, 0.0).astype(BF)
    km_v[...] = key_marks(seg, km_v.shape)


def key_marks(seg, shape):
    place = lane_ids(shape) % HD
    marks = jnp.where(place < SEGS, jnp.where(seg[...] == place, 0.0, MASKED), 1.0)
    return jnp.where(place < TOP, marks, 0.0).astype(BF)


def fwd_group(t, x_v, a_v, bias_v, km_v, qkv_v, ka_v, va_v):
    x = flat(x_v[...])
    w = flat(a_v[...])
    low = low_half((x.shape[0], LANES))
    for i in range(6):
        cols = slice(i * LANES, (i + 1) * LANES)
        out = mm(x, w[:, cols]) + bias_v[t, :, cols]
        if i % 3 == 0:
            out = out * QSCALE
        out = out.astype(BF)
        qkv_v[t, :, cols] = out
        one = jnp.ones_like(out)
        if i == 1:
            ka_v[0] = jnp.where(low, out, km_v[...])
            ka_v[1] = jnp.where(low, km_v[...], out)
        if i == 2:
            va_v[0] = jnp.where(low, out, one)
            va_v[1] = jnp.where(low, one, out)
        if i == 4:
            ka_v[2] = jnp.where(low, out, km_v[...])
        if i == 5:
            va_v[2] = jnp.where(low, out, one)


def fwd_block(t, rows, block, qkv_v, ka_v, va_v, oh_v, ctx_v, lse_ref):
    shape = (block, LANES)
    low = low_half(shape)
    lanes = lane_ids(shape)
    marks = oh_v[rows, :]
    lse = lse_ref[rows, :]
    parts = []
    for h in range(3):
        q = tile(qkv_v, t, 0 if h < 2 else 3, rows)
        q = jnp.where(low, marks, q) if h == 1 else jnp.where(low, q, marks)
        s = mm(q, ka_v[h], NT)
        top = jnp.max(s, axis=1, keepdims=True)
        w = jnp.exp2(s - top).astype(BF)
        o = mm(w, va_v[h])
        total = o[:, HD : HD + 1] if h != 1 else o[:, 0:1]
        lse = jnp.where(lanes == 3 * t + h, top + jnp.log2(total), lse)
        parts.append(o)
    lse_ref[rows, :] = lse
    sums = swap_halves(jnp.where(low, parts[1], parts[0]))
    pair = jnp.where(low, parts[0], parts[1]) / sums
    last = parts[2] / swap_halves(parts[2])
    zero = jnp.zeros(shape, F32)
    tiles = (pair, swap_halves(pair), swap_halves(last))
    for i, value in enumerate(tiles):
        ctx_v[t, rows, i * LANES : (i + 1) * LANES] = jnp.where(low, zero, value).astype(BF)


def spread(base, value, lanes):
    hi = value.astype(BF).astype(F32)
    rest = value - hi
    mid = rest.astype(BF).astype(F32)
    low = rest - mid
    place = lanes % HD
    out = jnp.where(place == SEGS, hi, jnp.where(place == SEGS + 1, mid, jnp.where(place == SEGS + 2, low, 0.0)))
    return jnp.where(place < SEGS, base, out.astype(BF))


def bwd_group(t, qkv, ctx, dctx, lse, oh_v, km_v, qa_v, ka_v, va_v, da_v, kt_v, dqt_v):
    length = oh_v.shape[0]
    shape = (length, LANES)
    low = low_half(shape)
    lanes = lane_ids(shape)
    oh, km = oh_v[...], km_v[...]
    ones = jnp.where((lanes % HD >= SEGS) & (lanes % HD < TOP), 1.0, 0.0).astype(BF)

    def cols(ref, i):
        return ref[:, i * LANES : (i + 1) * LANES]

    q, k, v = cols(qkv, 0), cols(qkv, 1), cols(qkv, 2)
    q2, k2, v2 = cols(qkv, 3), cols(qkv, 4), cols(qkv, 5)
    c_pair = jnp.where(low, swap_halves(cols(ctx, 1)), cols(ctx, 0))
    d_pair = jnp.where(low, swap_halves(cols(dctx, 1)), cols(dctx, 0))
    c_last = swap_halves(cols(ctx, 2))
    d_last = swap_halves(cols(dctx, 2))
    prod = c_pair.astype(F32) * d_pair.astype(F32)
    prod2 = c_last.astype(F32) * d_last.astype(F32)
    lse_all = lse[...]
    zero = jnp.zeros_like(prod)
    for h in range(3):
        mine = low if h != 1 else jnp.logical_not(low)
        delta = jnp.sum(jnp.where(mine, prod2 if h == 2 else prod, zero), axis=1, keepdims=True)
        top = jnp.sum(jnp.where(lanes == 3 * t + h, lse_all, zero), axis=1, keepdims=True)
        qa_v[h] = jnp.where(mine, q2 if h == 2 else q, spread(oh, -top, lanes))
        da_v[h] = jnp.where(mine, d_last if h == 2 else d_pair, spread(jnp.zeros_like(oh), -delta, lanes))
        ka_v[h] = jnp.where(mine, k2 if h == 2 else k, km)
        va_v[h] = jnp.where(mine, v2 if h == 2 else v, ones)
    kt_v[0] = k.T
    kt_v[1] = k2.T
    dqt_v[...] = jnp.zeros_like(dqt_v)


def bwd_block(rows, block, qa_v, ka_v, va_v, da_v, kt_v, dqt_v, out):
    low = low_half((block, LANES))
    dk, dv = [], []
    for h in range(3):
        s = mm(ka_v[h, rows, :], qa_v[h], NT)
        p = jnp.exp2(s)
        dv.append(mm(p.astype(BF), da_v[h]))
        dp = mm(va_v[h, rows, :], da_v[h], NT)
        ds = (p * dp).astype(BF)
        dk.append(mm(ds, qa_v[h]) * (1.0 / LOG2E))
        slot, half = h // 2, slice((h % 2) * HD, (h % 2 + 1) * HD)
        dqt_v[slot, half, :] += mm(kt_v[slot, half, rows], ds)
    zero = jnp.zeros((block, LANES), F32)
    tiles = {
        1: jnp.where(low, dk[0], dk[1]),
        2: jnp.where(low, dv[0], dv[1]),
        4: jnp.where(low, dk[2], zero),
        5: jnp.where(low, dv[2], zero),
    }
    for i, value in tiles.items():
        out[rows, i * LANES : (i + 1) * LANES] = value.astype(BF)


def bwd_finish(dqt_v, out):
    scale = HD**-0.5
    low = low_half((out.shape[0], LANES))
    out[:, 0:LANES] = (dqt_v[0].T * scale).astype(BF)
    last = dqt_v[1].T * scale
    out[:, 3 * LANES : 4 * LANES] = jnp.where(low, last, jnp.zeros_like(last)).astype(BF)


def normalize(values, gain_row, shift_row):
    average = jnp.mean(values, axis=-1, keepdims=True)
    centered = values - average
    variance = jnp.mean(centered * centered, axis=-1, keepdims=True)
    inverse = lax.rsqrt(variance + EPS)
    unit = centered * inverse
    return unit * gain_row + shift_row, unit, inverse


def normalize_back(upstream, unit, inverse, gain_row):
    d_unit = upstream * gain_row
    first = jnp.mean(d_unit, axis=-1, keepdims=True)
    second = jnp.mean(d_unit * unit, axis=-1, keepdims=True)
    return inverse * (d_unit - first - unit * second)


def eighths(value):
    return jnp.sum(value.reshape(-1, 8, value.shape[-1]), axis=0)


def gelu_both(x):
    a = jnp.abs(x)
    tail = jnp.exp2(x * x * (-0.5 * LOG2E))
    t = 1.0 / (1.0 + (0.3275911 * 0.5**0.5) * a)
    poly = ((((0.5307027145 * t - 0.7265760135) * t + 0.7107068705) * t - 0.142248368) * t + 0.127414796) * t
    rest = poly * tail
    cdf = jnp.where(x < 0, rest, 1.0 - rest)
    return x * cdf, cdf + x * tail * 0.3989422804014327


def mid_rows(i, block, refs, late):
    (x_v, cot_v, ctx_v, ao_v, in_v, dn_v, vec, act_v, dact_v, dpre_v, y1_v, g2_v, out_v, gh1_v, dctx_v, sums_v) = refs
    rows = pl.ds(pl.multiple_of(i * block, block), block)
    few = block // x_v.shape[1]
    these = pl.ds(i * few, few)
    apart = (few, *x_v.shape[1:])
    groups = in_v.shape[0]

    def row(k):
        return vec[k : k + 1, :]

    def note(k, value):
        sums_v[k] += eighths(value)

    attn = mm(ctx_v[0, rows, :], ao_v[0], NT)
    for t in range(1, groups):
        attn = attn + mm(ctx_v[t, rows, :], ao_v[t], NT)
    h1 = flat(x_v[these]).astype(F32) + attn + row(4)
    y1, u1, r1 = normalize(h1, row(0), row(1))
    y1_low = y1.astype(BF)
    y1_v[rows, :] = y1_low
    ffn = row(5) + y1
    pl.when(i == 0)(lambda: wait_all(late))
    for t in range(groups):
        pre = mm(y1_low, in_v[t]) + row(8 + t)
        act, slope = gelu_both(pre)
        act = act.astype(BF)
        act_v[t, rows, :] = act
        dact_v[t] = slope.astype(BF)
        ffn = ffn + mm(act, dn_v[t], NT)
    out, u2, r2 = normalize(ffn, row(2), row(3))
    out_v[these] = out.astype(BF).reshape(apart)
    up = flat(cot_v[these]).astype(F32)
    g_h2 = normalize_back(up, u2, r2, row(2))
    note(2, up * u2)
    note(3, up)
    note(5, g_h2)
    g2 = g_h2.astype(BF)
    g2_v[rows, :] = g2
    g_y1 = g_h2
    for t in range(groups):
        dpre = (mm(g2, dn_v[t]) * dact_v[t].astype(F32)).astype(BF)
        dpre_v[t, rows, :] = dpre
        note(8 + t, dpre.astype(F32))
        g_y1 = g_y1 + mm(dpre, in_v[t], NT)
    note(0, g_y1 * u1)
    note(1, g_y1)
    g_h1 = normalize_back(g_y1, u1, r1, row(0))
    note(4, g_h1)
    gh1_v[these] = g_h1.reshape(apart)
    g1 = g_h1.astype(BF)
    for t in range(groups):
        dctx_v[t, rows, :] = mm(g1, ao_v[t]).astype(BF)

STEP = {"z2": 4, "z1": 2, "y": 1, "x": 2, "c": 1}
BLOCKS = ("x", "c", "z2", "z1", "y")
FEATURES = ("z2", "z1", "y", "x", "c")
P_Y = ("z2", "z1", "x", "y")
P_Z = ("z2", "x", "y", "z1")
Q_Y = ("z2", "x", "z1", "y")
Q_Z = ("z2", "x", "y", "z1")
P_X = ("z2", "y", "z1", "x")


class Place:
    def __init__(self):
        self.d = lax.axis_index("dp")
        self.t = lax.axis_index("tensor")
        self.bit = {
            "x": self.t // 2,
            "c": self.t % 2,
            "z2": self.d // 4,
            "z1": (self.d // 2) % 2,
            "y": self.d % 2,
        }

    def flip(self, dim):
        return 1 - self.bit[dim]

    def peer(self, dim):
        move = STEP[dim] * (1 - 2 * self.bit[dim])
        if dim in ("x", "c"):
            return (self.d, self.t + move)
        return (self.d + move, self.t)

    def row_peer(self, k):
        t = self.t
        if k in (1, 3):
            t = t + (1 - 2 * self.bit["c"])
        if k in (2, 3):
            t = t + 2 * (1 - 2 * self.bit["x"])
        return t

    def index(self, dims, **chosen):
        return tuple(chosen.get(dim, self.bit[dim]) for dim in dims)


def enter(place):
    bar = pltpu.get_barrier_semaphore()
    peers = [place.peer(dim) for dim in BLOCKS] + [(place.d, place.row_peer(3))]
    for peer in peers:
        pl.semaphore_signal(bar, inc=1, device_id=peer, device_id_type=MESH)
    pl.semaphore_wait(bar, len(peers))


class Copies:
    def __init__(self, send, recv, local):
        self.send, self.recv, self.local = send, recv, local
        self.count = self.locals = 0

    def remote(self, ends):
        i = self.count
        self.count += 1

        def copy():
            src, dst, peer = ends()
            return pltpu.make_async_remote_copy(
                src_ref=src,
                dst_ref=dst,
                send_sem=self.send.at[i],
                recv_sem=self.recv.at[i],
                device_id=peer,
                device_id_type=MESH,
            )

        copy().start()
        return lambda: copy().wait()

    def here(self, ends):
        i = self.locals
        self.locals += 1

        def copy():
            src, dst = ends()
            return pltpu.make_async_copy(src, dst, self.local.at[i])

        copy().start()
        return lambda: copy().wait()


ALLBITS = slice(None)


class GatherPart:
    def __init__(self, place, copies, own, full, order, rows, dims=BLOCKS):
        self.place, self.copies, self.own, self.full, self.order = place, copies, own, full, order
        self.rows, self.dims = rows, dims
        self.stage = 0
        self.side = []

    def at(self, **chosen):
        return self.full.at[self.place.index(self.dims, **chosen) + (self.rows,)]

    def begin(self):
        p, c = self.place, self.copies
        self.current = c.remote(lambda: (self.own.at[self.rows], self.at(), p.peer(self.order[0])))
        self.side.append(c.remote(lambda: (self.own.at[self.rows], self.at(), p.peer("c"))))
        self.keep = c.here(lambda: (self.own.at[self.rows], self.at()))

    def held(self, s):
        return self.at(**{dim: ALLBITS for dim in self.order[:s]})

    def arrived(self, s):
        dim = self.order[s]
        return self.at(**{other: ALLBITS for other in self.order[:s]}, **{dim: self.place.flip(dim)})

    def advance(self):
        p, c, s = self.place, self.copies, self.stage
        self.current()
        if s == 0:
            self.keep()
        if s + 1 < len(self.order):
            self.current = c.remote(lambda: (self.held(s + 1), self.held(s + 1), p.peer(self.order[s + 1])))
        self.side.append(c.remote(lambda: (self.arrived(s), self.arrived(s), p.peer("c"))))
        self.stage = s + 1

    def finish(self):
        wait_all(self.side)


def every(count, work):
    if count == 0:
        work(())
        return

    def body(i, carry):
        work(tuple((i // 2**j) % 2 for j in reversed(range(count))))
        return carry

    lax.fori_loop(0, 2**count, body, 0)


def blockwise(ref):
    return ref.reshape(2 ** (len(ref.shape) - 2), *ref.shape[-2:])


def spot(bits):
    place = 0
    for bit in bits:
        place = 2 * place + bit
    return place


class ReducePart:
    def __init__(self, place, copies, src, total, arrive, out, order, rows, dims=BLOCKS, paired=False):
        self.paired = paired
        self.place, self.copies, self.src, self.total, self.arrive = place, copies, src, total, arrive
        self.out, self.order, self.rows, self.dims = out, order, rows, dims
        self.inner = tuple(dim for dim in dims if dim != "c")
        self.kept = self.inner
        if total is None:
            self.total, self.kept = src, dims
        self.stage = 0

    def source(self, **chosen):
        return self.src.at[self.place.index(self.dims, **chosen) + (self.rows,)]

    def sums(self, **chosen):
        return self.total.at[self.place.index(self.kept, **chosen) + (self.rows,)]

    def half(self, bit):
        p, first = self.place, self.order[0]

        def ends():
            free = {dim: ALLBITS for dim in self.inner}
            free[first] = bit()
            dst = self.arrive[0].at[p.index(self.inner, **free) + (self.rows,)]
            return self.source(c=p.flip("c"), **free), dst, p.peer("c")

        return self.copies.remote(ends)

    def begin(self):
        p, first = self.place, self.order[0]
        if self.paired:
            self.keep = self.copies.here(lambda: (self.src.at[(ALLBITS,) * 4 + (self.rows,)], self.total.at[(ALLBITS,) * 4 + (self.rows,)]))
            return
        self.side = [self.half(lambda: p.flip(first)), self.half(lambda: p.bit[first])]
        if self.kept is self.inner:
            free = {dim: ALLBITS for dim in self.inner}
            self.keep = self.copies.here(lambda: (self.source(**free), self.sums(**free)))

    def add(self, fixed, bit):
        s = self.stage
        left = [dim for dim in self.inner if dim not in self.order[:s]] if s else list(self.inner)
        loose = [dim for dim in left if dim != fixed]

        total, arrive = blockwise(self.total), blockwise(self.arrive[s])

        def work(bits):
            chosen = dict(zip(loose, bits))
            chosen[fixed] = bit
            mine = spot(self.place.index(self.kept, **chosen))
            there = spot(tuple(chosen[dim] for dim in left))
            both = total[mine, self.rows, :].astype(F32) + arrive[there, self.rows, :].astype(F32)
            total[mine, self.rows, :] = both.astype(total.dtype)

        every(len(loose), work)

    def send(self):
        p, s = self.place, self.stage
        dim = self.order[s]
        free = {other: ALLBITS for other in self.order[s + 1 :]}

        def ends():
            src = self.sums(**free, **{dim: p.flip(dim)})
            dst = self.arrive[s + 1].at[(ALLBITS,) * len(free) + (self.rows,)]
            return src, dst, p.peer(dim)

        return self.copies.remote(ends)

    def advance(self):
        p, s = self.place, self.stage
        if s == 0:
            if self.kept is self.inner:
                self.keep()
            if not self.paired:
                self.side[0]()
        else:
            self.current()
        if s < len(self.order):
            dim = self.order[s]
            if s == 0 and self.paired:
                self.current = self.send()
                self.stage = 1
                return
            self.add(dim, p.flip(dim))
            self.current = self.send()
            if s == 0:
                self.side[1]()
            self.add(dim, p.bit[dim])
        else:
            mine = spot(self.place.index(self.kept))
            self.out[self.rows, :] = blockwise(self.total)[mine, self.rows, :].astype(F32) + self.arrive[s][self.rows, :].astype(F32)
        self.stage = s + 1


def arrivals(rows, cols, dtype):
    return [pltpu.VMEM((2,) * n + (rows, cols), dtype) for n in (4, 3, 2, 1, 0)]


def start_row(place, copies, src, dst, k):
    def ends():
        to = place.row_peer(k)
        return src.at[to], dst.at[place.t], (place.d, to)

    return copies.remote(ends)


def keep_row(place, copies, src, dst):
    return copies.here(lambda: (src.at[place.t], dst.at[place.t]))


def start_rows(place, copies, src, dst):
    return [start_row(place, copies, src, dst, k) for k in (2, 3, 1)] + [keep_row(place, copies, src, dst)]


def wait_all(waits):
    for wait in waits:
        wait()


def params(collective=None):
    more = {} if collective is None else {"collective_id": collective, "has_side_effects": True}
    return pltpu.CompilerParams(vmem_limit_bytes=60 << 20, **more)


def sems(count):
    return [pltpu.SemaphoreType.DMA((count,))] * 2


def fwd_core(group_ref, x_v, vt_v, seg, qkv, ctx, xt, lse, vec_rows, s, ticks, closing=None):
    (a_v, bias_v, oh_v, km_v, qkv_v, ka_v, va_v, ctx_v, xt_v, a_sem, out_sem) = s
    groups, length = qkv.shape[:2]
    block = 256
    blocks = length // block

    def load(t):
        return pltpu.make_async_copy(group_ref(t), a_v.at[t % 2], a_sem.at[t % 2])

    load(0).start()
    fwd_setup(vt_v, seg, vec_rows, bias_v, oh_v, km_v)
    lse[...] = jnp.zeros_like(lse)

    def step(i, carry):
        t, b = i // blocks, i % blocks
        at_tick(i, ticks)

        @pl.when(b == 0)
        def _():
            load(t).wait()

            @pl.when(t + 1 < groups)
            def _():
                load(t + 1).start()

            fwd_group(t, x_v, a_v.at[t % 2], bias_v, km_v, qkv_v, ka_v, va_v)
            pltpu.make_async_copy(qkv_v.at[t], qkv.at[t], out_sem.at[0, t]).start()

        rows = pl.ds(pl.multiple_of(b * block, block), block)
        fwd_block(t, rows, block, qkv_v, ka_v, va_v, oh_v, ctx_v, lse)

        @pl.when(b == blocks - 1)
        def _():
            pltpu.make_async_copy(ctx_v.at[t], ctx.at[t], out_sem.at[1, t]).start()

        return carry

    lax.fori_loop(0, groups * blocks, step, 0)
    xt_v[...] = flat(x_v[...]).T
    turned = pltpu.make_async_copy(xt_v, xt, a_sem.at[0])
    turned.start()
    if closing is not None:
        closing()
    turned.wait()
    for t in range(groups):
        pltpu.make_async_copy(qkv_v.at[t], qkv.at[t], out_sem.at[0, t]).wait()
        pltpu.make_async_copy(ctx_v.at[t], ctx.at[t], out_sem.at[1, t]).wait()


def fwd_scratch(groups, length, width):
    return [
        pltpu.VMEM((2, 2, 2, 2, width // 8, width), BF),
        pltpu.VMEM((groups, 1, width), F32),
        pltpu.VMEM((length, LANES), BF),
        pltpu.VMEM((length, LANES), BF),
        pltpu.VMEM((groups, length, width), BF),
        pltpu.VMEM((3, length, LANES), BF),
        pltpu.VMEM((3, length, LANES), BF),
        pltpu.VMEM((groups, length, 3 * LANES), BF),
        pltpu.VMEM((width, length), BF),
        pltpu.SemaphoreType.DMA((2,)),
        pltpu.SemaphoreType.DMA((2, groups)),
    ]


def fwd_shapes(groups, length, width):
    return [
        jax.ShapeDtypeStruct((groups, length, width), BF),
        jax.ShapeDtypeStruct((groups, length, 3 * LANES), BF),
        jax.ShapeDtypeStruct((width, length), BF),
        jax.ShapeDtypeStruct((length, LANES), F32),
        jax.ShapeDtypeStruct((16, width), F32),
    ]


def fwd_comm_kernel(shard, vec, tok, cot, seg, g, x, co, qkv, ctx, xt, lse, vec_rows, x_v, vt_v, send, recv, loc, *s):
    place = Place()
    enter(place)
    copies = Copies(send, recv, loc)
    mk = functools.partial(GatherPart, place, copies)
    n = shard.shape[1]
    third, half = n // 3, n // 2
    first = [mk(vec, vt_v, Q_Z, pl.ds(0, vec.shape[0]), FEATURES)]
    first += [mk(shard.at[0], g.at[0], order, pl.ds(i * third, third)) for i, order in enumerate((Q_Y, Q_Z, P_X))]
    later = [mk(shard.at[1], g.at[1], order, pl.ds(i * half, half)) for i, order in enumerate((Q_Y, Q_Z))]
    later += [mk(shard.at[2], g.at[2], order, pl.ds(i * third, third)) for i, order in enumerate((Q_Y, Q_Z, P_X))]
    moved = []

    def advance():
        for part in later:
            part.advance()

    def cot_rows():
        advance()
        moved.extend(start_rows(place, copies, cot, co))

    for part in first:
        part.begin()
    rows = [start_row(place, copies, tok, x_v, k) for k in (2, 1)] + [keep_row(place, copies, tok, x_v)]
    for stage in range(4):
        for part in first:
            part.advance()
        if stage == 0:
            rows.append(start_row(place, copies, tok, x_v, 3))
        if stage == 2:
            for part in later:
                part.begin()
    for part in first:
        part.finish()
    wait_all(rows)
    keep = copies.here(lambda: (x_v, x))
    ticks = [(1, cot_rows), (4, advance), (8, advance)]
    fwd_core(lambda t: g.at[0, t // 2, t % 2], x_v, vt_v, seg, qkv, ctx, xt, lse, vec_rows, s, ticks, advance)
    for part in later:
        part.finish()
    wait_all(moved)
    keep()


def fwd_comm(shard, vec, tok, cot, seg):
    groups, block, width = tok.shape
    length = groups * block
    bits = (2,) * 5
    return pl.pallas_call(
        fwd_comm_kernel,
        in_specs=[ANY] * 4 + [VMEM],
        out_specs=[ANY] * 6 + [VMEM] * 2,
        out_shape=[
            jax.ShapeDtypeStruct((3,) + bits + shard.shape[1:], BF),
            jax.ShapeDtypeStruct(tok.shape, BF),
            jax.ShapeDtypeStruct(cot.shape, BF),
        ]
        + fwd_shapes(groups, length, width),
        scratch_shapes=[
            pltpu.VMEM(tok.shape, BF),
            pltpu.VMEM(bits + vec.shape, F32),
            *sems(96),
            pltpu.SemaphoreType.DMA((20,)),
        ]
        + fwd_scratch(groups, length, width),
        compiler_params=params(0),
        name="attention_forward",
    )(shard, vec, tok, cot, seg)


def fwd_plain_kernel(g, x, vt, seg, qkv, ctx, xt, lse, vec_rows, sem, x_v, *s):
    copy = pltpu.make_async_copy(x, x_v, sem)
    copy.start()
    copy.wait()
    fwd_core(lambda t: g.at[0, t // 2, t % 2], x_v, vt, seg, qkv, ctx, xt, lse, vec_rows, s, [])


def fwd_plain(g, x, vt, seg):
    groups, block, width = x.shape
    length = groups * block
    return pl.pallas_call(
        fwd_plain_kernel,
        in_specs=[ANY, ANY, VMEM, VMEM],
        out_specs=[ANY] * 3 + [VMEM] * 2,
        out_shape=fwd_shapes(groups, length, width),
        scratch_shapes=[pltpu.SemaphoreType.DMA, pltpu.VMEM(x.shape, BF)] + fwd_scratch(groups, length, width),
        compiler_params=params(),
        name="attention_forward",
    )(g, x, vt, seg)


def mid_kernel(g, x, cot, ctx, vec, out, grad, gh1, dctx, sums, x_v, cot_v, ctx_v, ao_v, in_v, dn_v, act_v, dact_v, dpre_v, y1_v, g2_v, out_v, gh1_v, dctx_v, t_v, sem, out_sem):
    groups, length = ctx.shape[:2]
    width = x.shape[2]
    half = width // 2
    blocks, block = x.shape[:2]
    few = dact_v.shape[1] // block

    def copy(src, dst, i):
        return pltpu.make_async_copy(src, dst, sem.at[i])

    loads = [copy(x, x_v, 0), copy(ctx, ctx_v, 1), copy(g.at[0, :, :, half:], ao_v, 2)]
    loads += [copy(g.at[1], in_v, 3), copy(g.at[2], dn_v, 4), copy(cot, cot_v, 5)]
    for load in loads:
        load.start()
    sums[...] = jnp.zeros_like(sums)
    for load in loads[:3]:
        load.wait()
    refs = (x_v, cot_v, ctx_v, ao_v, in_v, dn_v, vec, act_v, dact_v, dpre_v, y1_v, g2_v, out_v, gh1_v, dctx_v, sums)

    def step(i, carry):
        mid_rows(i, few * block, refs, [load.wait for load in loads[3:]])
        for j in range(few):
            b = i * few + j
            pltpu.make_async_copy(out_v.at[b], out.at[b], out_sem.at[0, b]).start()
            pltpu.make_async_copy(gh1_v.at[b], gh1.at[b], out_sem.at[1, b]).start()
        return carry

    lax.fori_loop(0, blocks // few, step, 0)
    send = copy(dctx_v, dctx, 0)
    send.start()
    t_v[...] = y1_v[...].T

    def in_step(t, carry):
        in_v[t] = mm(t_v[...], dpre_v[t]).astype(BF)
        pltpu.make_async_copy(in_v.at[t], grad.at[0, t], out_sem.at[2, t]).start()
        return carry

    lax.fori_loop(0, groups, in_step, 0)
    t_v[...] = g2_v[...].T

    def dn_step(t, carry):
        dn_v[t] = mm(t_v[...], act_v[t]).astype(BF)
        pltpu.make_async_copy(dn_v.at[t], grad.at[1, t], out_sem.at[3, t]).start()
        return carry

    lax.fori_loop(0, groups, dn_step, 0)
    send.wait()
    for i in range(blocks):
        pltpu.make_async_copy(out_v.at[i], out.at[i], out_sem.at[0, i]).wait()
        pltpu.make_async_copy(gh1_v.at[i], gh1.at[i], out_sem.at[1, i]).wait()
    for t in range(groups):
        pltpu.make_async_copy(in_v.at[t], grad.at[0, t], out_sem.at[2, t]).wait()
        pltpu.make_async_copy(dn_v.at[t], grad.at[1, t], out_sem.at[3, t]).wait()


def middle(g, x, cot, ctx, vec):
    groups, length, _ = ctx.shape
    blocks, block, width = x.shape
    flats = (groups, width, width)
    return pl.pallas_call(
        mid_kernel,
        in_specs=[ANY] * 4 + [VMEM],
        out_specs=[ANY] * 4 + [VMEM],
        out_shape=[
            jax.ShapeDtypeStruct(x.shape, BF),
            jax.ShapeDtypeStruct((2,) + flats, BF),
            jax.ShapeDtypeStruct(x.shape, F32),
            jax.ShapeDtypeStruct(ctx.shape, BF),
            jax.ShapeDtypeStruct((8 + groups, 8, width), F32),
        ],
        scratch_shapes=[
            pltpu.VMEM(x.shape, BF),
            pltpu.VMEM(x.shape, BF),
            pltpu.VMEM(ctx.shape, BF),
            pltpu.VMEM((groups, width, width // 2), BF),
            pltpu.VMEM(flats, BF),
            pltpu.VMEM(flats, BF),
            pltpu.VMEM((groups, length, width), BF),
            pltpu.VMEM((groups, block, width), BF),
            pltpu.VMEM((groups, length, width), BF),
            pltpu.VMEM((length, width), BF),
            pltpu.VMEM((length, width), BF),
            pltpu.VMEM(x.shape, BF),
            pltpu.VMEM(x.shape, F32),
            pltpu.VMEM(ctx.shape, BF),
            pltpu.VMEM((width, length), BF),
            pltpu.SemaphoreType.DMA((6,)),
            pltpu.SemaphoreType.DMA((4, max(groups, blocks))),
        ],
        compiler_params=params(),
        name="feed_forward",
    )(g, x, cot, ctx, vec)


def bwd_core(qkv, ctx, dctx, lse, seg, xt, gh1, g, da, gx, qsum, s, ticks, place=None, closing=None):
    (qkv_v, ctx_v, dctx_v, a_v, oh_v, km_v, qa_v, ka_v, va_v, da_v, kt_v, dqt_v, dqkv_v, x_v, gx_v, xt_v, gt_v, dw_v, pair_v, in_sem, out_sem, x_sem, pair_sem) = s
    groups, length = qkv.shape[:2]
    block = 256
    blocks = length // block
    half = 3 * LANES

    early = groups if place is None else groups // 2

    def group(i):
        if place is None:
            return i
        core = place.bit["c"]
        return 2 * (i % 2) + core + (1 - i // 2) * (1 - 2 * core)

    def loads(i):
        t, slot = group(i), i % 2
        return [
            pltpu.make_async_copy(qkv.at[t], qkv_v.at[slot], in_sem.at[0, slot]),
            pltpu.make_async_copy(ctx.at[t], ctx_v.at[slot], in_sem.at[1, slot]),
            pltpu.make_async_copy(dctx.at[t], dctx_v.at[slot], in_sem.at[2, slot]),
            pltpu.make_async_copy(g.at[0, t], a_v.at[slot], in_sem.at[3, slot]),
        ]

    def result(i):
        if place is None:
            return pltpu.make_async_copy(dw_v.at[i], da.at[i], out_sem.at[i])
        return pltpu.make_async_copy(dw_v.at[i], da.at[i - early], out_sem.at[i])

    def hand_over(i):
        return pltpu.make_async_remote_copy(
            src_ref=dw_v.at[i],
            dst_ref=pair_v.at[i],
            send_sem=pair_sem.at[0, i],
            recv_sem=pair_sem.at[1, i],
            device_id=place.peer("c"),
            device_id_type=MESH,
        )

    more = [pltpu.make_async_copy(xt, xt_v, x_sem.at[0]), pltpu.make_async_copy(gh1, gx_v, x_sem.at[1])]
    for load in loads(0) + more:
        load.start()
    oh_v[...] = jnp.where(seg[...] == lane_ids(oh_v.shape) % HD, 1.0, 0.0).astype(BF)
    km_v[...] = key_marks(seg, km_v.shape)

    def ready():
        for load in more:
            load.wait()
        gt_v[...] = flat(gx_v[...]).astype(BF).T

    def weights(i, slot, add):
        def chunk(r, inner):
            part = pl.ds(pl.multiple_of(r * block, block), block)
            lead = mm(xt_v[part, :], dqkv_v[:, :half])
            rest = mm(xt_v[part, :], dqkv_v[:, half:]) + mm(gt_v[part, :], ctx_v[slot])
            if add:
                lead = lead + pair_v[i - early, part, :half].astype(F32)
                rest = rest + pair_v[i - early, part, half:].astype(F32)
            dw_v[i, part, :half] = lead.astype(BF)
            dw_v[i, part, half:] = rest.astype(BF)
            return inner

        lax.fori_loop(0, dw_v.shape[1] // block, chunk, 0)

    def rows(b, slot):
        part = pl.ds(pl.multiple_of(b * block, block), block)
        gx_v[b] = gx_v[b] + mm(dqkv_v[part, :], a_v[slot], NT)

    def step(i, carry):
        at, b = i // blocks, i % blocks
        slot = at % 2
        at_tick(i, ticks)
        pl.when(i == 1)(ready)

        @pl.when(b == 0)
        def _():
            for load in loads(at):
                load.wait()

            @pl.when(at + 1 < groups)
            def _():
                for load in loads(at + 1):
                    load.start()

            bwd_group(group(at), qkv_v.at[slot], ctx_v.at[slot], dctx_v.at[slot], lse, oh_v, km_v, qa_v, ka_v, va_v, da_v, kt_v, dqt_v)

        part = pl.ds(pl.multiple_of(b * block, block), block)
        bwd_block(part, block, qa_v, ka_v, va_v, da_v, kt_v, dqt_v, dqkv_v)

        @pl.when(b == blocks - 1)
        def _():
            bwd_finish(dqt_v, dqkv_v)
            qsum[group(at)] = mm(jnp.ones((8, length), BF), dqkv_v[...])
            if place is None:
                weights(at, slot, False)
                result(at).start()
            else:

                @pl.when(at < early)
                def _():
                    weights(at, slot, False)
                    hand_over(at).start()

                @pl.when(at >= early)
                def _():
                    hand_over(at - early).wait()
                    weights(at, slot, True)
                    result(at).start()

            def row_step(r, inner):
                rows(r, slot)
                return inner

            lax.fori_loop(0, blocks, row_step, 0)

        return carry

    lax.fori_loop(0, groups * blocks, step, 0)

    def low_step(r, carry):
        x_v[r] = gx_v[r].astype(BF)
        return carry

    lax.fori_loop(0, blocks, low_step, 0)
    last = pltpu.make_async_copy(x_v, gx, x_sem.at[0])
    last.start()
    if closing is not None:
        closing()
    for i in range(0 if place is None else early, groups):
        result(i).wait()
    last.wait()


def bwd_scratch(groups, length, width, x):
    half = 3 * LANES
    return [
        pltpu.VMEM((2, length, width), BF),
        pltpu.VMEM((2, length, half), BF),
        pltpu.VMEM((2, length, half), BF),
        pltpu.VMEM((2, width, width), BF),
        pltpu.VMEM((length, LANES), BF),
        pltpu.VMEM((length, LANES), BF),
        pltpu.VMEM((3, length, LANES), BF),
        pltpu.VMEM((3, length, LANES), BF),
        pltpu.VMEM((3, length, LANES), BF),
        pltpu.VMEM((3, length, LANES), BF),
        pltpu.VMEM((2, LANES, length), BF),
        pltpu.VMEM((2, LANES, length), F32),
        pltpu.VMEM((length, width), BF),
        pltpu.VMEM(x, BF),
        pltpu.VMEM(x, F32),
        pltpu.VMEM((width, length), BF),
        pltpu.VMEM((width, length), BF),
        pltpu.VMEM((groups, width, width), BF),
        pltpu.VMEM((groups // 2, width, width), BF),
        pltpu.SemaphoreType.DMA((4, 2)),
        pltpu.SemaphoreType.DMA((groups,)),
        pltpu.SemaphoreType.DMA((2,)),
        pltpu.SemaphoreType.DMA((2, groups // 2)),
    ]


def bwd_shapes(groups, width, x, held):
    return [
        jax.ShapeDtypeStruct((held, width, width), BF),
        jax.ShapeDtypeStruct(x, BF),
        jax.ShapeDtypeStruct((groups, 8, width), F32),
    ]


def bwd_comm_kernel(qkv, ctx, dctx, lse, seg, xt, gh1, g, grad, out, da, gx, qsum, own, out_rows, total, r0, r1, r2, r3, r4, r5, r6, r7, r8, r9, send, recv, loc, *s):
    place = Place()
    enter(place)
    copies = Copies(send, recv, loc)
    half = own.shape[1] // 2
    arrive = ((r0, r1, r2, r3, r4), (r5, r6, r7, r8, r9))
    parts = []
    for w, orders in enumerate(((P_Y, P_Z), (Q_Y, Q_Z))):
        for i, order in enumerate(orders):
            rows = pl.ds(i * half, half)
            parts.append(ReducePart(place, copies, grad.at[w], total.at[w], arrive[w], own.at[w], order[::-1], rows))
    for part in parts:
        part.begin()
    moved = []

    def advance(*which):
        for i in which:
            parts[i].advance()

    def rows():
        moved.extend(start_rows(place, copies, out, out_rows))

    ticks = [
        (2, functools.partial(advance, 0, 1, 2, 3)),
        (3, rows),
        (8, functools.partial(advance, 0, 1, 2, 3)),
        (11, functools.partial(advance, 0, 2)),
        (12, functools.partial(advance, 1, 3)),
        (13, functools.partial(advance, 0, 2)),
        (14, functools.partial(advance, 1, 3)),
    ]
    bwd_core(qkv, ctx, dctx, lse, seg, xt, gh1, g, da, gx, qsum, s, ticks, place, functools.partial(advance, 0, 1, 2, 3))
    wait_all(moved)


def bwd_comm(qkv, ctx, dctx, lse, seg, xt, gh1, g, grad, out):
    groups, length, width = qkv.shape
    n = grad.shape[6]
    arrive = arrivals(n, width, BF)
    return pl.pallas_call(
        bwd_comm_kernel,
        in_specs=[ANY] * 3 + [VMEM] * 2 + [ANY] * 5,
        out_specs=[ANY, ANY, VMEM, VMEM, ANY],
        out_shape=bwd_shapes(groups, width, gh1.shape, groups // 2)
        + [
            jax.ShapeDtypeStruct((2, n, width), F32),
            jax.ShapeDtypeStruct(out.shape, BF),
        ],
        scratch_shapes=[
            pltpu.VMEM((2, 2, 2, 2, 2, n, width), BF),
            *arrive,
            *arrive,
            *sems(40),
            pltpu.SemaphoreType.DMA((10,)),
        ]
        + bwd_scratch(groups, length, width, gh1.shape),
        compiler_params=params(1),
        name="attention_backward",
    )(qkv, ctx, dctx, lse, seg, xt, gh1, g, grad, out)


def bwd_plain_kernel(qkv, ctx, dctx, lse, seg, xt, gh1, g, da, gx, qsum, *s):
    bwd_core(qkv, ctx, dctx, lse, seg, xt, gh1, g, da, gx, qsum, s, [])


def bwd_plain(qkv, ctx, dctx, lse, seg, xt, gh1, g):
    groups, length, width = qkv.shape
    return pl.pallas_call(
        bwd_plain_kernel,
        in_specs=[ANY] * 3 + [VMEM] * 2 + [ANY] * 3,
        out_specs=[ANY, ANY, VMEM],
        out_shape=bwd_shapes(groups, width, gh1.shape, groups),
        scratch_shapes=bwd_scratch(groups, length, width, gh1.shape),
        compiler_params=params(),
        name="attention_backward",
    )(qkv, ctx, dctx, lse, seg, xt, gh1, g)


def end_vectors(sums, qsum_v, tab_v):
    groups = qsum_v.shape[0]
    tab_v[...] = jnp.zeros_like(tab_v)
    for t in range(groups):
        tab_v[t : t + 1, :] = qsum_v[t][:1]
    parts = tab_v[...].T
    for k in range(sums.shape[0]):
        tab_v[k : k + 1, :] = jnp.sum(sums[k], axis=0, keepdims=True)
    table = tab_v[...].T
    q, v = [], []
    for t in range(groups):
        col = parts[:, t : t + 1]
        q += [col[:LANES], col[3 * LANES : 3 * LANES + HD]]
        v += [col[2 * LANES : 3 * LANES], col[5 * LANES : 5 * LANES + HD]]
    lanes = lane_ids(table.shape)
    table = jnp.where(lanes == 6, jnp.concatenate(q, axis=0), table)
    table = jnp.where(lanes == 7, jnp.concatenate(v, axis=0), table)
    return table


def sum_comm_kernel(da, vt, gx, own, vec_own, gx_rows, total, vtot, r0, r1, r2, r3, r4, r5, r6, r7, r8, send, recv, loc):
    place = Place()
    enter(place)
    copies = Copies(send, recv, loc)
    third = own.shape[0] // 3
    parts = []
    for i, order in enumerate((P_X, Q_Y, Q_Z)):
        rows = pl.ds(i * third, third)
        parts.append(ReducePart(place, copies, da, total, (r0, r0, r1, r2, r3), own, order[::-1], rows, paired=True))
    rows = pl.ds(0, vec_own.shape[0])
    parts.append(ReducePart(place, copies, vt, vtot, (r4, r5, r6, r7, r8), vec_own, P_Y[::-1], rows, FEATURES))
    for part in parts:
        part.begin()
    moved = []
    for stage in range(5):
        for part in parts:
            part.advance()
        if stage == 0:
            moved += [start_row(place, copies, gx, gx_rows, k) for k in (2, 1)] + [keep_row(place, copies, gx, gx_rows)]
        if stage == 2:
            moved.append(start_row(place, copies, gx, gx_rows, 3))
    wait_all(moved)


def sum_comm(da, vt, gx):
    n, width = da.shape[-2:]
    fine = vt.shape[-2]
    return pl.pallas_call(
        sum_comm_kernel,
        in_specs=[ANY] * 3,
        out_specs=[VMEM, VMEM, ANY],
        out_shape=[
            jax.ShapeDtypeStruct((n, width), F32),
            jax.ShapeDtypeStruct((fine, LANES), F32),
            jax.ShapeDtypeStruct(gx.shape, BF),
        ],
        scratch_shapes=[
            pltpu.VMEM((2,) * 4 + (n, width), BF),
            pltpu.VMEM((2,) * 4 + (fine, LANES), F32),
            *arrivals(n, width, BF)[1:],
            *arrivals(fine, LANES, F32),
            *sems(40),
            pltpu.SemaphoreType.DMA((10,)),
        ],
        compiler_params=params(2),
        name="weight_sums",
    )(da, vt, gx)


def vector_kernel(sums, qsum, vt, tab_v):
    vt[...] = end_vectors(sums, qsum, tab_v)


def vector_table(sums, qsum):
    width = sums.shape[2]
    return pl.pallas_call(
        vector_kernel,
        in_specs=[VMEM] * 2,
        out_specs=VMEM,
        out_shape=jax.ShapeDtypeStruct((width, LANES), F32),
        scratch_shapes=[pltpu.VMEM((LANES, width), F32)],
        name="vector_table",
    )(sums, qsum)


def pack(qkv_weight, out_weight, in_weight, down_weight):
    q, k, v = qkv_weight[0], qkv_weight[1], qkv_weight[2]
    o = out_weight.T
    a = [q[:, :LANES], k[:, :LANES], v[:, :LANES]]
    a += [q[:, LANES:], o[:, HD:LANES], k[:, LANES:], o[:, :HD], v[:, LANES:], o[:, LANES:]]
    return jnp.stack([jnp.concatenate(a, axis=1), in_weight, down_weight.T])


def unpack(a):
    def cut(i, half):
        start = i * LANES + half * HD
        return a[:, start : start + HD]

    heads = [jnp.concatenate([cut(i, 0), cut(i, 1), cut(3 + i, 0)], axis=1) for i in range(3)]
    out = jnp.concatenate([cut(4, 1), cut(3, 1), cut(5, 1)], axis=1)
    return jnp.stack(heads), out.T


def local(tokens, segments, qkv_weight, out_weight, in_weight, down_weight, vectors, cotangent):
    n_dp, n_t = lax.axis_size("dp"), lax.axis_size("tensor")
    groups, block, width = tokens.shape
    length = groups * block
    n = in_weight.shape[0]
    fine = vectors.shape[1]
    n_v = vectors.shape[0]
    seg = lax.dynamic_slice_in_dim(segments, lax.axis_index("tensor"), 1, 0).reshape(length, 1)
    shard = pack(qkv_weight, out_weight, in_weight, down_weight)
    vec = jnp.pad(vectors.T, ((0, 0), (0, LANES - n_v)))
    kernels = n_dp == 8 and n_t == 4
    bits = (2,) * 5
    if kernels:
        g, x, cot, qkv, ctx, xt, lse, rows = fwd_comm(shard, vec, tokens, cotangent, seg)
    else:
        full = lax.all_gather(shard, ALL, axis=0, tiled=False).reshape(n_dp, n_t, 3, n, width)
        g = full.transpose(2, 1, 0, 3, 4).reshape((3,) + bits + (width // 8, width))
        vt = lax.all_gather(vec, ALL, axis=0, tiled=True)
        x = lax.all_to_all(tokens, "tensor", split_axis=0, concat_axis=0, tiled=True)
        cot = lax.all_to_all(cotangent, "tensor", split_axis=0, concat_axis=0, tiled=True)
        qkv, ctx, xt, lse, rows = fwd_plain(g, x, vt, seg)
    g = g.reshape(3, groups, width, width)
    out, grad, gh1, dctx, sums = middle(g, x, cot, ctx, rows)
    if kernels:
        grad = grad.reshape((2,) + bits + (n, width))
        da, gx, qsum, own, out_rows = bwd_comm(qkv, ctx, dctx, lse, seg, xt, gh1, g, grad, out)
        vt = vector_table(sums, qsum).reshape(bits + (fine, LANES))
        own_a, own_v, gx_rows = sum_comm(da.reshape(bits[1:] + (n, width)), vt, gx)
    else:
        da, gx, qsum = bwd_plain(qkv, ctx, dctx, lse, seg, xt, gh1, g)
        vt = vector_table(sums, qsum)
        every_grad = jnp.concatenate([da.reshape(1, n_t, n_dp, n, width), grad.reshape(2, n_t, n_dp, n, width)])
        every_grad = every_grad.transpose(2, 1, 0, 3, 4).reshape(n_dp * n_t, 3, n, width)
        own = lax.psum_scatter(every_grad, ALL, scatter_dimension=0, tiled=True)[0].astype(F32)
        own_a, own = own[0], own[1:]
        own_v = lax.psum_scatter(vt[:, :n_v], ALL, scatter_dimension=0, tiled=True)
        out_rows = lax.all_to_all(out, "tensor", split_axis=0, concat_axis=0, tiled=True)
        gx_rows = lax.all_to_all(gx, "tensor", split_axis=0, concat_axis=0, tiled=True)
    d_qkv, d_out = unpack(own_a)
    return out_rows, gx_rows, d_qkv, d_out, own[0], own[1].T, own_v[:, :n_v].T


def solution(mesh):
    rows = P("dp", "tensor", None)
    weights = (P(None, "dp", "tensor"), P("tensor", "dp"), P("dp", "tensor"), P("tensor", "dp"), P(None, ("dp", "tensor")))
    in_specs = (rows, P("dp", None), *weights, rows)
    out_specs = (rows, rows, *weights)
    return jax.shard_map(local, mesh=mesh, in_specs=in_specs, out_specs=out_specs, check_vma=False)
```
